32 devices in a mesh: rows: 8 (over z, x), cols: 4 (over y, core).
Axes of the slice: x: 2, y: 2, z: 4, core: 2. Of those that a mesh axis runs over, the one named last changes fastest.
Arguments:
- query: bfloat16 [24, 256, 2048], P('rows', 'cols'), may hold values from -6 to 6
- key: bfloat16 [24, 256, 2048], P('rows', 'cols'), may hold values from -6 to 6
- value: bfloat16 [24, 256, 2048], P('rows', 'cols'), may hold values from -6 to 6
- cotangent: bfloat16 [24, 256, 2048], P('rows', 'cols'), may hold values from -6 to 6
- conv_weight: bfloat16 [9, 2048], replicated, may hold values from -1.1953125 to 1.1953125
- row_mask: int32 [24, 2, 2], P('rows'), may hold values from 0 to 1, as said below
- col_mask: int32 [256, 3, 3], P('cols'), may hold values from 0 to 1, as said below
Outputs:
- out: bfloat16 [24, 256, 2048], P('rows', 'cols')
- dquery: bfloat16 [24, 256, 2048], P('rows', 'cols')
- dkey: bfloat16 [24, 256, 2048], P('rows', 'cols')
- dvalue: bfloat16 [24, 256, 2048], P('rows', 'cols')
The draws below stay inside these ranges and needn't reach their ends.
Inputs may be any that keep to these rules, and one draw needn't show every extreme that they name: `row_mask`: every diagonal block is 1: a query block always sees its own block. `col_mask`: every diagonal block is 1: a query block always sees its own block.
All inputs are finite; a program needn't handle non-finite values.
Results may differ from the reference program's by a relative error of at most 0.011.
Values may be sent and summed in bfloat16 or wider, within the bound.
A program may use at most 128 MiB of HBM per device.

```python
import math
import jax
import jax.numpy as jnp
from jax import lax

D = 2048
HEAD_DIM = 128
SHEET_ROW_BLOCKS = 2
COL_BLOCKS = 3
SHEET_ROWS = 24
SHEET_COLS = 256


def draw_query(key, part):
    base = jax.random.normal(jax.random.fold_in(key, 1), (SHEET_ROWS, SHEET_COLS, D), jnp.float32)
    return jnp.clip(base, -6.0, 6.0).astype(jnp.bfloat16)


def draw_key(key, part):
    base = jax.random.normal(jax.random.fold_in(key, 4), (SHEET_ROWS, SHEET_COLS, D), jnp.float32)
    return jnp.clip(base, -6.0, 6.0).astype(jnp.bfloat16)


def block_mask_table(key, lines, blocks):
    flips = jax.random.randint(key, (lines, blocks, blocks), 0, 2)
    diagonal = lax.broadcasted_iota(jnp.int32, (1, blocks, blocks), 1) == lax.broadcasted_iota(jnp.int32, (1, blocks, blocks), 2)
    return jnp.where(diagonal, 1, flips).astype(jnp.int32)


def draw_row_mask(key, part):
    return block_mask_table(jax.random.fold_in(key, 21), SHEET_ROWS, SHEET_ROW_BLOCKS)


def draw_col_mask(key, part):
    return block_mask_table(jax.random.fold_in(key, 22), SHEET_COLS, COL_BLOCKS)


def block_levels(rng, dims, shards, low, largest):
    gain, own = 1.0, jax.random.fold_in(rng, 6)
    for position, shards_of in shards:
        heights = jnp.exp(jax.random.uniform(jax.random.fold_in(own, position), (shards_of,), jnp.float32, low / len(shards), largest / len(shards)))
        gain = gain * jnp.repeat(heights, dims[position] // shards_of).reshape([-1 if axis == position else 1 for axis in range(len(dims))])
    return gain


def bell_draw(own_key, extent, deviation, most, cuts=(), held_as=jnp.bfloat16):
    gain = block_levels(own_key, extent, cuts, -0.22, 0.18) if cuts else 1.0
    entries = jax.random.normal(own_key, extent, jnp.float32) * deviation * gain
    return jnp.minimum(jnp.maximum(entries, -most), most).astype(held_as)


def setup_inputs(seed: int = 0) -> dict:
    arg_keys = jax.random.split(jax.random.key(seed), 8)
    return {
        "query": draw_query(jax.random.fold_in(arg_keys[7], 71), 0),
        "key": draw_key(jax.random.fold_in(arg_keys[7], 71), 0),
        "value": bell_draw(arg_keys[2], (SHEET_ROWS, SHEET_COLS, D), 1.0, 6.0, ((0, 8), (1, 4))),
        "cotangent": bell_draw(arg_keys[3], (SHEET_ROWS, SHEET_COLS, D), 1.0, 6.0, ((0, 8), (1, 4))),
        "conv_weight": bell_draw(arg_keys[4], (9, D), 0.3, 1.1953125),
        "row_mask": draw_row_mask(jax.random.fold_in(arg_keys[7], 71), 0),
        "col_mask": draw_col_mask(jax.random.fold_in(arg_keys[7], 71), 0),
    }


def attend_line(query_line, key_line, value_line, grad_line, allowed):
    score_scale = 1.0 / math.sqrt(HEAD_DIM)
    query_full = query_line.astype(jnp.float32)
    key_full = key_line.astype(jnp.float32)
    value_full = value_line.astype(jnp.float32)
    grad_full = grad_line.astype(jnp.float32)
    scores = jnp.einsum('qhd,khd->hqk', query_full, key_full) * score_scale
    scores = jnp.where(allowed[None], scores, -jnp.inf)
    highest = lax.optimization_barrier(jnp.max(scores, axis=-1, keepdims=True))
    weights = jnp.exp(scores - highest)
    weights = weights / lax.optimization_barrier(jnp.sum(weights, axis=-1, keepdims=True))
    rounded = lax.optimization_barrier(weights.astype(jnp.bfloat16)).astype(jnp.float32)
    attended = jnp.einsum('hqk,khd->qhd', rounded, value_full)
    dweights = jnp.einsum('qhd,khd->hqk', grad_full, value_full)
    delta = jnp.transpose(lax.optimization_barrier(jnp.sum(grad_full * attended, axis=-1)), (1, 0))
    dscores = (weights * (dweights - delta[:, :, None]) * score_scale).astype(jnp.bfloat16)
    dscores = lax.optimization_barrier(dscores).astype(jnp.float32)
    dquery = jnp.einsum('hqk,khd->qhd', dscores, key_full)
    dkey = jnp.einsum('hqk,qhd->khd', dscores, query_full)
    dvalue = jnp.einsum('hqk,qhd->khd', rounded, grad_full)
    return (attended.astype(jnp.bfloat16), dquery.astype(jnp.bfloat16), dkey.astype(jnp.bfloat16), dvalue.astype(jnp.bfloat16))

def depthwise_sheet(field, taps, reverse_taps):
    padded = jnp.pad(field, ((1, 1), (1, 1), (0, 0)))

    def one_row(index):
        window = lax.dynamic_slice_in_dim(padded, index.astype(jnp.int32), 3, 0).astype(jnp.float32)
        summed = jnp.zeros((SHEET_COLS, D), jnp.float32)
        for row_offset_start in range(3):
            for offset_col in range(3):
                if reverse_taps:
                    start_row = 2 - row_offset_start
                    start_col = 2 - offset_col
                else:
                    start_row = row_offset_start
                    start_col = offset_col
                picked = window[start_row, start_col:start_col + SHEET_COLS]
                summed = summed + taps[row_offset_start * 3 + offset_col] * picked
        return summed
    return lax.map(one_row, jnp.arange(SHEET_ROWS, dtype=jnp.int32))

def run_line(items):
    return attend_line(items[0], items[1], items[2], items[3], items[4])

def reference(query, key, value, cotangent, conv_weight, row_mask, col_mask):
    half_width = D // 2
    head_count = half_width // HEAD_DIM
    shaped = [x.reshape(SHEET_ROWS, SHEET_COLS, 2, head_count, HEAD_DIM) for x in (query, key, value, cotangent)]
    row_parts = tuple((x[:, :, 0] for x in shaped))
    col_parts = tuple((jnp.transpose(x[:, :, 1], (1, 0, 2, 3)) for x in shaped))
    row_len = SHEET_COLS // SHEET_ROW_BLOCKS
    row_allowed = jnp.repeat(jnp.repeat(row_mask, row_len, axis=1), row_len, axis=2) == 1
    col_len = SHEET_ROWS // COL_BLOCKS
    col_allowed = jnp.repeat(jnp.repeat(col_mask, col_len, axis=1), col_len, axis=2) == 1
    row_results = lax.map(run_line, row_parts + (row_allowed,))
    col_results = lax.map(run_line, col_parts + (col_allowed,))

    def assemble(row_piece, col_piece):
        joined = jnp.stack([row_piece, jnp.transpose(col_piece, (1, 0, 2, 3))], axis=2)
        return lax.optimization_barrier(joined.reshape(SHEET_ROWS, SHEET_COLS, D))
    attended16 = assemble(row_results[0], col_results[0])
    dquery = assemble(row_results[1], col_results[1])
    dkey = assemble(row_results[2], col_results[2])
    dvalue_attn = assemble(row_results[3], col_results[3])
    taps = conv_weight.astype(jnp.float32)
    lepe = depthwise_sheet(value, taps, False)
    out = (attended16.astype(jnp.float32) + lepe).astype(jnp.bfloat16)
    dvalue = (dvalue_attn.astype(jnp.float32) + depthwise_sheet(cotangent, taps, True)).astype(jnp.bfloat16)
    return (out, dquery, dkey, dvalue)
```

```python
import functools
import math

import jax
import jax.numpy as jnp
from jax import lax
from jax.experimental import pallas as pl
from jax.experimental.pallas import tpu as pltpu
from jax.sharding import PartitionSpec as P

HEAD_DIM = 128
SHEET_ROW_BLOCKS = 2
COL_BLOCKS = 3


def padded(array, sides, width):
    for axis, dim in sides:
        devices, length = (lax.axis_size(axis), array.shape[dim])
        up = [(i, (i + 1) % devices) for i in range(devices - 1)]
        down = [(j, i) for i, j in up]
        last = lax.slice_in_dim(array, length - width, length, axis=dim)
        leading = lax.slice_in_dim(array, 0, width, axis=dim)
        before = lax.ppermute(last, axis, up)
        after = lax.ppermute(leading, axis, down)
        array = jnp.concatenate([before, array, after], axis=dim)
    return array


def block_allow(block_mask_table, query_pos, key_pos, block_len, block_count):
    labels = jnp.arange(block_count)
    query_onehot_rows = (query_pos[:, None] // block_len == labels[None, :]).astype(jnp.float32)
    key_onehot_rows = (key_pos[:, None] // block_len == labels[None, :]).astype(jnp.float32)
    merged_links = jnp.einsum(
        "xv,zvs,hs->zxh", query_onehot_rows, block_mask_table.astype(jnp.float32), key_onehot_rows
    )
    return merged_links > 0.5


def line_attention(query_part, key_part, value_part, grad_part, allowed, layout):
    if layout == "bq":
        query_form = "bqhd"
        key_layout_shape = "bkhd"
    else:
        query_form = "qbhd"
        key_layout_shape = "kbhd"
    score_scale = 1.0 / math.sqrt(query_part.shape[-1])
    pair_form = query_form + "," + key_layout_shape + "->bhqk"
    scores = (
        jnp.einsum(pair_form, query_part, key_part, preferred_element_type=jnp.float32)
        * score_scale
    )
    scores = jnp.where(allowed[:, None], scores, -jnp.inf)
    highest = jnp.max(scores, axis=-1, keepdims=True)
    weights = jnp.exp(scores - highest)
    weights = weights / jnp.sum(weights, axis=-1, keepdims=True)
    rounded = weights.astype(jnp.bfloat16)
    attended = jnp.einsum(
        "bhqk," + key_layout_shape + "->" + query_form,
        rounded,
        value_part,
        preferred_element_type=jnp.float32,
    )
    dweights = jnp.einsum(pair_form, grad_part, value_part, preferred_element_type=jnp.float32)
    delta = jnp.sum(grad_part.astype(jnp.float32) * attended, axis=-1)
    if layout == "bq":
        delta = jnp.transpose(delta, (0, 2, 1))
    else:
        delta = jnp.transpose(delta, (1, 2, 0))
    dscores = (weights * (dweights - delta[..., None]) * score_scale).astype(jnp.bfloat16)
    dquery = jnp.einsum(
        "bhqk," + key_layout_shape + "->" + query_form,
        dscores,
        key_part,
        preferred_element_type=jnp.float32,
    )
    dkey = jnp.einsum(
        "bhqk," + query_form + "->" + key_layout_shape,
        dscores,
        query_part,
        preferred_element_type=jnp.float32,
    )
    dvalue = jnp.einsum(
        "bhqk," + query_form + "->" + key_layout_shape,
        rounded,
        grad_part,
        preferred_element_type=jnp.float32,
    )
    return (attended, dquery, dkey, dvalue)


def depthwise(padded_field, taps, rows_count, cols_count, reverse_taps):
    summed = jnp.zeros((rows_count, cols_count, taps.shape[1]), jnp.float32)
    for row_offset_start in range(3):
        for offset_col in range(3):
            if reverse_taps:
                start_row = 2 - row_offset_start
                start_col = 2 - offset_col
            else:
                start_row = row_offset_start
                start_col = offset_col
            window = padded_field[
                start_row : start_row + rows_count, start_col : start_col + cols_count
            ]
            summed = summed + taps[row_offset_start * 3 + offset_col] * window.astype(jnp.float32)
    return summed


def body(query, key, value, cotangent, conv_weight, row_mask, col_mask):
    rows_here, cols_here, width = query.shape
    half_width = width // 2
    head_groups = half_width // HEAD_DIM
    row_devices = lax.axis_size("rows")
    col_devices = lax.axis_size("cols")
    sheet_rows = rows_here * row_devices
    sheet_cols = cols_here * col_devices
    taps = conv_weight.astype(jnp.float32)
    padded_value = padded(value, (("rows", 0), ("cols", 1)), 1)
    padded_grad = padded(cotangent, (("rows", 0), ("cols", 1)), 1)
    row_len = sheet_cols // SHEET_ROW_BLOCKS
    keys_row, values_row = (
        lax.all_gather(key[:, :, :half_width], "cols", axis=1, tiled=True),
        lax.all_gather(value[:, :, :half_width], "cols", axis=1, tiled=True),
    )
    col_start = lax.axis_index("cols") * cols_here
    allowed = block_allow(
        row_mask,
        col_start + jnp.arange(cols_here),
        jnp.arange(sheet_cols),
        row_len,
        SHEET_ROW_BLOCKS,
    )
    local_shape = (rows_here, cols_here, head_groups, HEAD_DIM)
    whole_shape = (rows_here, sheet_cols, head_groups, HEAD_DIM)
    results = line_attention(
        query[:, :, :half_width].reshape(local_shape),
        keys_row.reshape(whole_shape),
        values_row.reshape(whole_shape),
        cotangent[:, :, :half_width].reshape(local_shape),
        allowed,
        "bq",
    )
    key_terms = results[2].reshape(rows_here, sheet_cols, half_width)
    value_terms = results[3].reshape(rows_here, sheet_cols, half_width)
    key_grads, value_grads = (
        lax.psum_scatter(key_terms, "cols", scatter_dimension=1, tiled=True),
        lax.psum_scatter(value_terms, "cols", scatter_dimension=1, tiled=True),
    )
    out_row = results[0].reshape(rows_here, cols_here, half_width).astype(jnp.bfloat16)
    dq_row = results[1].reshape(rows_here, cols_here, half_width).astype(jnp.bfloat16)
    dk_row = key_grads.astype(jnp.bfloat16)
    dv_row = value_grads.astype(jnp.bfloat16)
    columns_each = cols_here // row_devices
    moved = (
        lax.all_to_all(query[:, :, half_width:], "rows", split_axis=1, concat_axis=0, tiled=True),
        lax.all_to_all(key[:, :, half_width:], "rows", split_axis=1, concat_axis=0, tiled=True),
        lax.all_to_all(value[:, :, half_width:], "rows", split_axis=1, concat_axis=0, tiled=True),
        lax.all_to_all(
            cotangent[:, :, half_width:], "rows", split_axis=1, concat_axis=0, tiled=True
        ),
    )
    column_shape = (sheet_rows, columns_each, head_groups, HEAD_DIM)
    my_tables = lax.dynamic_slice_in_dim(
        col_mask, lax.axis_index("rows") * columns_each, columns_each, 0
    )
    col_len = sheet_rows // COL_BLOCKS
    positions = jnp.arange(sheet_rows)
    col_allowed = block_allow(my_tables, positions, positions, col_len, COL_BLOCKS)
    col_results = line_attention(
        moved[0].reshape(column_shape),
        moved[1].reshape(column_shape),
        moved[2].reshape(column_shape),
        moved[3].reshape(column_shape),
        col_allowed,
        "qb",
    )
    column_flat = (sheet_rows, columns_each, half_width)
    col_pieces = [piece.reshape(column_flat).astype(jnp.bfloat16) for piece in col_results]
    out_col, dq_col, dk_col, dv_col = (
        lax.all_to_all(col_pieces[0], "rows", split_axis=0, concat_axis=1, tiled=True),
        lax.all_to_all(col_pieces[1], "rows", split_axis=0, concat_axis=1, tiled=True),
        lax.all_to_all(col_pieces[2], "rows", split_axis=0, concat_axis=1, tiled=True),
        lax.all_to_all(col_pieces[3], "rows", split_axis=0, concat_axis=1, tiled=True),
    )
    lepe = depthwise(padded_value, taps, rows_here, cols_here, False)
    back_conv = depthwise(padded_grad, taps, rows_here, cols_here, True)
    attended16 = jnp.concatenate([out_row, out_col], axis=2)
    out = (attended16.astype(jnp.float32) + lepe).astype(jnp.bfloat16)
    dquery = jnp.concatenate([dq_row, dq_col], axis=2)
    dkey = jnp.concatenate([dk_row, dk_col], axis=2)
    dvalue_attn = jnp.concatenate([dv_row, dv_col], axis=2)
    dvalue = (dvalue_attn.astype(jnp.float32) + back_conv).astype(jnp.bfloat16)
    return (out, dquery, dkey, dvalue)


SUB = 8
VMEM_LIMIT = 28 << 20
MESH = pl.DeviceIdType.MESH


def attend(q, k, v, g, allow):
    scale = 1.0 / math.sqrt(HEAD_DIM)
    nt = (((1,), (1,)), ((), ()))
    nn = (((1,), (0,)), ((), ()))
    tn = (((0,), (0,)), ((), ()))
    dot = functools.partial(lax.dot_general, preferred_element_type=jnp.float32)
    s = jnp.where(allow, dot(q, k, nt) * scale, -jnp.inf)
    e = jnp.exp(s - jnp.max(s, axis=-1, keepdims=True))
    w = e * (1.0 / jnp.sum(e, axis=-1, keepdims=True))
    w16 = w.astype(jnp.bfloat16)
    att = dot(w16, v, nn)
    dw = dot(g, v, nt)
    delta = jnp.sum(g.astype(jnp.float32) * att, axis=-1, keepdims=True)
    ds = (w * (dw - delta) * scale).astype(jnp.bfloat16)
    return att, dot(ds, k, nn), dot(ds, q, tn), dot(w16, g, tn)


def dots():
    dot = functools.partial(lax.dot_general, preferred_element_type=jnp.float32)
    return (
        functools.partial(dot, dimension_numbers=(((1,), (1,)), ((), ()))),
        functools.partial(dot, dimension_numbers=(((1,), (0,)), ((), ()))),
        functools.partial(dot, dimension_numbers=(((0,), (0,)), ((), ()))),
    )


def softmax(q, k, allow):
    nt, _, _ = dots()
    s = jnp.where(allow, nt(q, k) * (1.0 / math.sqrt(HEAD_DIM)), -jnp.inf)
    e = jnp.exp(s - jnp.max(s, axis=-1, keepdims=True))
    return e * (1.0 / jnp.sum(e, axis=-1, keepdims=True))


def layer_kernel(dims, q_hbm, k_hbm, v_hbm, g_hbm, taps, row_mask, col_mask, ret, *rest):
    R, C, rows, groups, width = dims
    colbuf, colout, rowbuf, rowout, ext, conv, hop, land, weights, attended = rest[:10]
    (ci_s, ci_r, co_s, co_r, ri_s, ri_r, ro_s, ro_r, ha_s, ha_r, bo_s, bo_r, local) = rest[10:]
    half = width // 2
    share = half // C
    heads = half // HEAD_DIM
    me = lax.axis_index("rows")
    mc = lax.axis_index("cols")
    inputs = (q_hbm, k_hbm, v_hbm, g_hbm)
    f32 = jnp.float32
    first, second = pl.ds(0, half), pl.ds(half, half)

    def lanes(start, size):
        return pl.ds(pl.multiple_of(start, 128), size)

    def send(src, dst, send_sem, recv_sem, target):
        return pltpu.make_async_remote_copy(
            src_ref=src, dst_ref=dst, send_sem=send_sem, recv_sem=recv_sem,
            device_id=target, device_id_type=MESH)

    def home(t):
        return land.at[t // 3] if t in (0, 3) else ret.at[t]

    def col_in(t, p, slot):
        return send(inputs[t].at[:, p, :, second], colbuf.at[t, slot],
                    ci_s.at[t, p], ci_r.at[t, slot], {"rows": p})

    def col_back(t, p, slot):
        return send(colout.at[t, p], home(t).at[:, slot, :, second],
                    co_s.at[t, p], co_r.at[t, slot], {"rows": p})

    def row_in(t, p, slot):
        return send(inputs[t].at[:, :, :, lanes(p * share, share)], rowbuf.at[t, :, slot],
                    ri_s.at[t, p], ri_r.at[t, slot], {"cols": p})

    def row_back(t, p, slot):
        return send(rowout.at[t, :, p], home(t).at[:, :, :, lanes(slot * share, share)],
                    ro_s.at[t, p], ro_r.at[t, slot], {"cols": p})

    odd = lax.rem(me, 2)
    sign = 2 * odd - 1
    crosses = jnp.logical_and(me + sign >= 0, me + sign < R)
    relays = jnp.logical_and(me - 2 * sign >= 0, me - 2 * sign < R)
    inner = pl.ds(1, groups)
    even_slot, odd_slot = (1 - odd) * (rows + 1), odd * (rows + 1)
    mid = R // 2
    side = me // mid
    gate = mid - 1 + side
    at_gate = me == gate
    beside_gate = me - sign == gate
    direct = 3 * half // 4
    extra = half - direct
    owned, others = pl.ds(side * mid, mid), pl.ds((1 - side) * mid, mid)

    def halo(kind, t, src, dst, target):
        return send(src, dst, ha_s.at[kind, t], ha_r.at[kind, t], target)

    def part(n):
        if n == 0:
            return pl.ds(0, groups), pl.ds(direct, extra), pl.ds(0, extra)
        return (owned, others)[n - 1], second, pl.ds(extra, half)

    def cross(t, slot):
        return halo(0, t, inputs[2 + t].at[odd * (rows - 1), :, :, pl.ds(0, direct)],
                    ext.at[t, slot, inner, :, pl.ds(0, direct)], {"rows": me + sign})

    def detour(t, n):
        span, features, place = part(n)
        return halo(1 + n, t, inputs[2 + t].at[odd * (rows - 1), span, :, features],
                    hop.at[t, span, :, place], {"rows": me - sign})

    def forward(t, slot, n):
        span, features, place = part(n)
        return halo(4 + n, t, hop.at[t, span, :, place],
                    ext.at[t, slot, inner].at[span, :, features], {"rows": me - 2 * sign})

    def near(t, slot):
        return halo(7, t, inputs[2 + t].at[(1 - odd) * (rows - 1)], ext.at[t, slot, inner], {"rows": me - sign})

    def rightward(t):
        return halo(8, t, inputs[2 + t].at[:, groups - 1], ext.at[t, pl.ds(1, rows), 0], {"cols": mc + 1})

    def leftward(t):
        return halo(9, t, inputs[2 + t].at[:, 0], ext.at[t, pl.ds(1, rows), groups + 1], {"cols": mc - 1})

    def corner_right(t, e):
        r = e * (rows + 1)
        return halo(10 + e, t, ext.at[t, r, groups], ext.at[t, r, 0], {"cols": mc + 1})

    def corner_left(t, e):
        r = e * (rows + 1)
        return halo(12 + e, t, ext.at[t, r, 1], ext.at[t, r, groups + 1], {"cols": mc - 1})

    def border_copy(t, p):
        here = colbuf.at[2 + t, mid - side, side * (rows - 1)]
        there = ext.at[t, (1 - side) * (rows + 1), 1 + p, :, second]
        return here, there

    def border(t, p):
        here, there = border_copy(t, p)
        return send(here, there, bo_s.at[t], bo_r.at[t, p], {"rows": gate})

    def border_own(t):
        here, there = border_copy(t, me)
        return pltpu.make_async_copy(here, there, local.at[2, t])

    order = sorted(range(1, R), key=lambda d: abs(d - R / 2))
    col_order = sorted(range(1, C), key=lambda d: abs(d - C / 2))
    away = jnp.logical_not(at_gate)
    has_right, has_left = mc < C - 1, mc > 0

    def each_piece(gone, act):
        for t in range(2):
            for n in range(3):
                if n < 2:
                    act(t, n)
                else:
                    pl.when(jnp.logical_not(gone))(functools.partial(act, t, n))

    barrier = pltpu.get_barrier_semaphore()
    for d in range(1, R):
        pl.semaphore_signal(barrier, inc=1, device_id={"rows": lax.rem(me + d, R)}, device_id_type=MESH)
    for d in range(1, C):
        pl.semaphore_signal(barrier, inc=1, device_id={"cols": lax.rem(mc + d, C)}, device_id_type=MESH)
    pl.semaphore_wait(barrier, R - 1 + C - 1)

    def send_halo():
        @pl.when(crosses)
        def _():
            each_piece(at_gate, lambda t, n: detour(t, n).start())
            for t in range(2):
                cross(t, even_slot).start()

        for t in range(2):
            near(t, odd_slot).start()

    def send_sides():
        @pl.when(has_right)
        def _():
            for t in range(2):
                rightward(t).start()

        @pl.when(has_left)
        def _():
            for t in range(2):
                leftward(t).start()

    def pass_halo():
        @pl.when(relays)
        def _():
            def act(t, n):
                detour(t, n).wait_recv()
                forward(t, odd_slot, n).start()

            each_piece(beside_gate, act)

    def send_cols(t):
        for d in order:
            col_in(t, lax.rem(me + d, R), me).start()

    def send_rows(t):
        for d in col_order:
            row_in(t, lax.rem(mc + d, C), mc).start()

    for t in range(4):
        send_cols(t)
    for t in range(4):
        send_rows(t)
    send_halo()
    send_sides()

    near_copies = []
    for t in range(4):
        near_copies.append(pltpu.make_async_copy(inputs[t].at[:, :, :, lanes(mc * share, share)], rowbuf.at[t, :, mc], local.at[0, t]))
        near_copies.append(pltpu.make_async_copy(inputs[t].at[:, me, :, second], colbuf.at[t, me], local.at[1, t]))
    for t in range(2):
        near_copies.append(pltpu.make_async_copy(inputs[2 + t], ext.at[t, pl.ds(1, rows), inner], local.at[2, t]))
    for c in near_copies:
        c.start()
    for edge, area in (
        (me == 0, (slice(None), 0, inner)),
        (me == R - 1, (slice(None), rows + 1, inner)),
        (mc == 0, (slice(None), slice(None), 0)),
        (mc == C - 1, (slice(None), slice(None), groups + 1)),
    ):
        @pl.when(edge)
        def _(area=area):
            for t in range(2):
                view = ext.at[(t,) + area[1:]]
                view[...] = jnp.zeros(view.shape, view.dtype)
    for c in near_copies:
        c.wait()

    length = R * rows * SUB
    col_size = length // COL_BLOCKS
    key_pos = lax.broadcasted_iota(jnp.int32, (SUB, length), 1)
    lane_col = lax.broadcasted_iota(jnp.int32, (SUB, length), 0)
    block = jnp.where(lax.rem(key_pos, SUB) == lane_col, key_pos // col_size, -1)
    col_tables = []
    for b in range(COL_BLOCKS):
        table = jnp.zeros((SUB, length), jnp.int32)
        for c in range(SUB):
            for j in range(COL_BLOCKS):
                here = jnp.logical_and(lane_col == c, block == j)
                table = jnp.where(here, col_mask[b, j, me * SUB + c], table)
        col_tables.append(table)

    pass_halo()

    for t in range(4):
        for d in col_order:
            p = lax.rem(mc + d, C)
            row_in(t, p, p).wait_recv()
    tokens = C * groups * SUB

    def row_step(n, carry):
        i, h = n // (share // HEAD_DIM), lax.rem(n, share // HEAD_DIM)
        cols = lanes(h * HEAD_DIM, HEAD_DIM)
        x = [rowbuf[t, i, :, :, :, cols].astype(f32).reshape(tokens, HEAD_DIM).astype(jnp.bfloat16) for t in range(4)]
        size = tokens // SHEET_ROW_BLOCKS
        place = lax.broadcasted_iota(jnp.int32, (SUB, tokens), 1) // size
        bands = []
        for b in range(SHEET_ROW_BLOCKS):
            table = jnp.zeros((SUB, tokens), jnp.int32)
            for j in range(SHEET_ROW_BLOCKS):
                table = jnp.where(place == j, row_mask[b, j, i], table)
            bands.append(jnp.broadcast_to(table[None], (size // SUB, SUB, tokens)).reshape(size, tokens))
        allow = jnp.concatenate(bands, axis=0) > 0
        for t, y in enumerate(attend(*x, allow)):
            rowout[t, i, :, :, :, cols] = y.reshape(C, groups, SUB, HEAD_DIM).astype(jnp.bfloat16)
        return carry

    lax.fori_loop(0, rows * (share // HEAD_DIM), row_step, 0)
    kept = []
    for t in (0, 3, 1, 2):
        for d in col_order:
            row_back(t, lax.rem(mc + d, C), mc).start()
    for t in range(4):
        kept.append([pltpu.make_async_copy(rowout.at[t, :, mc], home(t).at[:, :, :, lanes(mc * share, share)], local.at[0, t])])
        kept[t][0].start()

    nt, nn, tn = dots()

    def arrived(t):
        for d in order:
            p = lax.rem(me + d, R)
            col_in(t, p, p).wait_recv()

    def give_back(t):
        for d in order:
            col_back(t, lax.rem(me + d, R), me).start()
        kept[t].append(pltpu.make_async_copy(colout.at[t, me], home(t).at[:, me, :, second], local.at[1, t]))
        kept[t][1].start()

    def column(t, h):
        return colbuf[t, :, :, :, lanes(h * HEAD_DIM, HEAD_DIM)].astype(f32).reshape(length, HEAD_DIM).astype(jnp.bfloat16)

    def give(t, h, y):
        colout[t, :, :, :, lanes(h * HEAD_DIM, HEAD_DIM)] = y.reshape(R, rows, SUB, HEAD_DIM).astype(jnp.bfloat16)

    def weigh(h, carry):
        allow = jnp.concatenate(
            [jnp.broadcast_to(t[None], (col_size // SUB, SUB, length)).reshape(col_size, length) for t in col_tables], axis=0) > 0
        weights[h] = softmax(column(0, h), column(1, h), allow)
        return carry

    def forward_step(h, carry):
        att = nn(weights[h].astype(jnp.bfloat16), column(2, h))
        attended[h] = att
        give(0, h, att)
        return carry

    def value_step(h, carry):
        give(3, h, tn(weights[h].astype(jnp.bfloat16), column(3, h)))
        return carry

    def score_step(h, carry):
        g = column(3, h)
        delta = jnp.sum(g.astype(f32) * attended[h], axis=-1, keepdims=True)
        ds = (weights[h] * (nt(g, column(2, h)) - delta) * (1.0 / math.sqrt(HEAD_DIM))).astype(jnp.bfloat16)
        give(1, h, nn(ds, column(1, h)))
        give(2, h, tn(ds, column(0, h)))
        return carry

    def send_border(t):
        @pl.when(away)
        def _():
            border(t, me).start()

        @pl.when(at_gate)
        def _():
            border_own(t).start()

    arrived(0)
    arrived(1)
    lax.fori_loop(0, heads, weigh, 0)
    arrived(2)
    send_border(0)
    lax.fori_loop(0, heads, forward_step, 0)
    give_back(0)
    arrived(3)
    send_border(1)
    lax.fori_loop(0, heads, value_step, 0)
    give_back(3)

    for t in range(2):
        near(t, even_slot).wait_recv()

    @pl.when(crosses)
    def _():
        for t in range(2):
            cross(t, odd_slot).wait_recv()
        each_piece(at_gate, lambda t, n: forward(t, odd_slot, n).wait_recv())

    @pl.when(at_gate)
    def _():
        for t in range(2):
            border_own(t).wait()
            for j in range(mid):
                p = side * mid + j

                @pl.when(p != me)
                def _(t=t, p=p):
                    border(t, p).wait_recv()

    for t in range(2):
        for e in range(2):
            @pl.when(has_right)
            def _(t=t, e=e):
                corner_right(t, e).start()

            @pl.when(has_left)
            def _(t=t, e=e):
                corner_left(t, e).start()

    lax.fori_loop(0, heads, score_step, 0)
    give_back(1)
    give_back(2)

    @pl.when(has_left)
    def _():
        for t in range(2):
            rightward(t).wait_recv()
            for e in range(2):
                corner_right(t, e).wait_recv()

    @pl.when(has_right)
    def _():
        for t in range(2):
            leftward(t).wait_recv()
            for e in range(2):
                corner_left(t, e).wait_recv()

    long = groups * SUB

    def conv_step(n, carry):
        cols = lanes(n * 128, 128)
        taps_here = taps[:, cols].astype(f32)
        for t in range(2):
            sums = [None] * rows
            for r in range(rows + 2):
                line = ext[t, r, :, :, cols].astype(f32).reshape(long + 2 * SUB, 128)
                for b in range(3):
                    seen = line[SUB + b - 1 : SUB + b - 1 + long]
                    for a in range(3):
                        o = r - a
                        if 0 <= o < rows:
                            tap = 3 * a + b if t == 0 else 8 - 3 * a - b
                            term = taps_here[tap : tap + 1] * seen
                            sums[o] = term if sums[o] is None else sums[o] + term
            for o in range(rows):
                conv[t, o, :, :, cols] = sums[o].reshape(groups, SUB, 128)
        return carry

    lax.fori_loop(0, width // 128, conv_step, 0)

    def returned(t):
        for c in kept[t]:
            c.wait()
        for d in col_order:
            p = lax.rem(mc + d, C)
            row_back(t, p, p).wait_recv()
        for d in order:
            p = lax.rem(me + d, R)
            col_back(t, p, p).wait_recv()

    stored = []
    for t in range(2):
        returned(3 * t)

        def add_step(n, carry):
            cols = lanes(n * 128, 128)
            land[t, :, :, :, cols] = (land[t, :, :, :, cols].astype(f32) + conv[t, :, :, :, cols]).astype(jnp.bfloat16)
            return carry

        lax.fori_loop(0, width // 128, add_step, 0)
        stored.append(pltpu.make_async_copy(land.at[t], ret.at[3 * t], local.at[2, 2 + t]))
        stored[t].start()
    returned(1)
    returned(2)
    for t in range(4):
        for d in col_order:
            p = lax.rem(mc + d, C)
            row_in(t, p, p).wait_send()
            row_back(t, p, p).wait_send()
        for d in order:
            p = lax.rem(me + d, R)
            col_in(t, p, p).wait_send()
            col_back(t, p, p).wait_send()
    for t in range(2):
        near(t, odd_slot).wait_send()

    @pl.when(crosses)
    def _():
        for t in range(2):
            cross(t, even_slot).wait_send()
        each_piece(at_gate, lambda t, n: detour(t, n).wait_send())

    @pl.when(relays)
    def _():
        each_piece(beside_gate, lambda t, n: forward(t, odd_slot, n).wait_send())

    @pl.when(away)
    def _():
        for t in range(2):
            border(t, me).wait_send()

    @pl.when(has_right)
    def _():
        for t in range(2):
            rightward(t).wait_send()
            for e in range(2):
                corner_right(t, e).wait_send()

    @pl.when(has_left)
    def _():
        for t in range(2):
            leftward(t).wait_send()
            for e in range(2):
                corner_left(t, e).wait_send()
    for c in stored:
        c.wait()


def finish_kernel(ret, *rest):
    copies = [pltpu.make_async_copy(ret.at[t], rest[t], rest[4].at[t]) for t in range(4)]
    for c in copies:
        c.start()
    for c in copies:
        c.wait()


def fused_body(query, key, value, cotangent, conv_weight, row_mask, col_mask):
    rows, cols_here, width = query.shape
    R, C = lax.axis_size("rows"), lax.axis_size("cols")
    groups = cols_here // SUB
    half = width // 2
    share = half // C
    views = [x.reshape(rows, groups, SUB, width) for x in (query, key, value, cotangent)]
    bf16 = jnp.bfloat16
    any_spec = pl.BlockSpec(memory_space=pl.ANY)
    vmem = pl.BlockSpec(memory_space=pltpu.VMEM)
    dma = pltpu.SemaphoreType.DMA
    smem = pl.BlockSpec(memory_space=pltpu.SMEM)
    heads = half // HEAD_DIM
    length = R * rows * SUB
    ret = pl.pallas_call(
        functools.partial(layer_kernel, (R, C, rows, groups, width)),
        out_shape=jax.ShapeDtypeStruct((4, rows, groups, SUB, width), bf16),
        in_specs=[any_spec] * 4 + [vmem, smem, smem],
        out_specs=any_spec,
        scratch_shapes=[
            pltpu.VMEM((4, R, rows, SUB, half), bf16),
            pltpu.VMEM((4, R, rows, SUB, half), bf16),
            pltpu.VMEM((4, rows, C, groups, SUB, share), bf16),
            pltpu.VMEM((4, rows, C, groups, SUB, share), bf16),
            pltpu.VMEM((2, rows + 2, groups + 2, SUB, width), bf16),
            pltpu.VMEM((2, rows, groups, SUB, width), jnp.float32),
            pltpu.VMEM((2, groups, SUB, half + half // 4), bf16),
            pltpu.VMEM((2, rows, groups, SUB, width), bf16),
            pltpu.VMEM((heads, length, length), jnp.float32),
            pltpu.VMEM((heads, length, HEAD_DIM), jnp.float32),
            dma((4, R)), dma((4, R)), dma((4, R)), dma((4, R)),
            dma((4, C)), dma((4, C)), dma((4, C)), dma((4, C)),
            dma((14, 2)), dma((14, 2)), dma((2,)), dma((2, R)), dma((3, 4)),
        ],
        compiler_params=pltpu.CompilerParams(collective_id=0, has_side_effects=True, vmem_limit_bytes=VMEM_LIMIT),
    )(*[pltpu.with_memory_space_constraint(x, pltpu.HBM) for x in (*views, conv_weight, jnp.transpose(row_mask, (1, 2, 0)), jnp.transpose(col_mask, (1, 2, 0)))])
    outs = pl.pallas_call(
        finish_kernel,
        out_shape=[jax.ShapeDtypeStruct((rows, groups, SUB, width), bf16)] * 4,
        in_specs=[any_spec],
        out_specs=[any_spec] * 4,
        scratch_shapes=[dma((4,))],
        compiler_params=pltpu.CompilerParams(vmem_limit_bytes=1 << 20),
    )(ret)
    return tuple(x.reshape(query.shape) for x in outs)


def any_body(query, key, value, cotangent, conv_weight, row_mask, col_mask):
    rows, cols_here, width = query.shape
    R, C = lax.axis_size("rows"), lax.axis_size("cols")
    fits = R % 4 == 0 and cols_here == R * SUB and (width // 2) % (C * HEAD_DIM) == 0 and (width // 2) % (4 * HEAD_DIM) == 0
    chosen = fused_body if fits else body
    return chosen(query, key, value, cotangent, conv_weight, row_mask, col_mask)


def solution(mesh):
    return jax.shard_map(
        any_body,
        mesh=mesh,
        in_specs=(
            P("rows", "cols", None),
            P("rows", "cols", None),
            P("rows", "cols", None),
            P("rows", "cols", None),
            P(),
            P("rows", None, None),
            P("cols", None, None),
        ),
        out_specs=(
            P("rows", "cols", None),
            P("rows", "cols", None),
            P("rows", "cols", None),
            P("rows", "cols", None),
        ),
        check_vma=False,
    )
```

```python
import functools
import math

import jax
import jax.numpy as jnp
from jax import lax
from jax.experimental import pallas as pl
from jax.experimental.pallas import tpu as pltpu
from jax.sharding import PartitionSpec as P

HEAD_DIM = 128
SHEET_ROW_BLOCKS = 2
COL_BLOCKS = 3


def padded(array, sides, width):
    for axis, dim in sides:
        devices, length = (lax.axis_size(axis), array.shape[dim])
        up = [(i, (i + 1) % devices) for i in range(devices - 1)]
        down = [(j, i) for i, j in up]
        last = lax.slice_in_dim(array, length - width, length, axis=dim)
        leading = lax.slice_in_dim(array, 0, width, axis=dim)
        before = lax.ppermute(last, axis, up)
        after = lax.ppermute(leading, axis, down)
        array = jnp.concatenate([before, array, after], axis=dim)
    return array


def block_allow(block_mask_table, query_pos, key_pos, block_len, block_count):
    labels = jnp.arange(block_count)
    query_onehot_rows = (query_pos[:, None] // block_len == labels[None, :]).astype(jnp.float32)
    key_onehot_rows = (key_pos[:, None] // block_len == labels[None, :]).astype(jnp.float32)
    merged_links = jnp.einsum(
        "xv,zvs,hs->zxh", query_onehot_rows, block_mask_table.astype(jnp.float32), key_onehot_rows
    )
    return merged_links > 0.5


def line_attention(query_part, key_part, value_part, grad_part, allowed, layout):
    if layout == "bq":
        query_form = "bqhd"
        key_layout_shape = "bkhd"
    else:
        query_form = "qbhd"
        key_layout_shape = "kbhd"
    score_scale = 1.0 / math.sqrt(query_part.shape[-1])
    pair_form = query_form + "," + key_layout_shape + "->bhqk"
    scores = (
        jnp.einsum(pair_form, query_part, key_part, preferred_element_type=jnp.float32)
        * score_scale
    )
    scores = jnp.where(allowed[:, None], scores, -jnp.inf)
    highest = jnp.max(scores, axis=-1, keepdims=True)
    weights = jnp.exp(scores - highest)
    weights = weights / jnp.sum(weights, axis=-1, keepdims=True)
    rounded = weights.astype(jnp.bfloat16)
    attended = jnp.einsum(
        "bhqk," + key_layout_shape + "->" + query_form,
        rounded,
        value_part,
        preferred_element_type=jnp.float32,
    )
    dweights = jnp.einsum(pair_form, grad_part, value_part, preferred_element_type=jnp.float32)
    delta = jnp.sum(grad_part.astype(jnp.float32) * attended, axis=-1)
    if layout == "bq":
        delta = jnp.transpose(delta, (0, 2, 1))
    else:
        delta = jnp.transpose(delta, (1, 2, 0))
    dscores = (weights * (dweights - delta[..., None]) * score_scale).astype(jnp.bfloat16)
    dquery = jnp.einsum(
        "bhqk," + key_layout_shape + "->" + query_form,
        dscores,
        key_part,
        preferred_element_type=jnp.float32,
    )
    dkey = jnp.einsum(
        "bhqk," + query_form + "->" + key_layout_shape,
        dscores,
        query_part,
        preferred_element_type=jnp.float32,
    )
    dvalue = jnp.einsum(
        "bhqk," + query_form + "->" + key_layout_shape,
        rounded,
        grad_part,
        preferred_element_type=jnp.float32,
    )
    return (attended, dquery, dkey, dvalue)


def depthwise(padded_field, taps, rows_count, cols_count, reverse_taps):
    summed = jnp.zeros((rows_count, cols_count, taps.shape[1]), jnp.float32)
    for row_offset_start in range(3):
        for offset_col in range(3):
            if reverse_taps:
                start_row = 2 - row_offset_start
                start_col = 2 - offset_col
            else:
                start_row = row_offset_start
                start_col = offset_col
            window = padded_field[
                start_row : start_row + rows_count, start_col : start_col + cols_count
            ]
            summed = summed + taps[row_offset_start * 3 + offset_col] * window.astype(jnp.float32)
    return summed


def body(query, key, value, cotangent, conv_weight, row_mask, col_mask):
    rows_here, cols_here, width = query.shape
    half_width = width // 2
    head_groups = half_width // HEAD_DIM
    row_devices = lax.axis_size("rows")
    col_devices = lax.axis_size("cols")
    sheet_rows = rows_here * row_devices
    sheet_cols = cols_here * col_devices
    taps = conv_weight.astype(jnp.float32)
    padded_value = padded(value, (("rows", 0), ("cols", 1)), 1)
    padded_grad = padded(cotangent, (("rows", 0), ("cols", 1)), 1)
    row_len = sheet_cols // SHEET_ROW_BLOCKS
    keys_row, values_row = (
        lax.all_gather(key[:, :, :half_width], "cols", axis=1, tiled=True),
        lax.all_gather(value[:, :, :half_width], "cols", axis=1, tiled=True),
    )
    col_start = lax.axis_index("cols") * cols_here
    allowed = block_allow(
        row_mask,
        col_start + jnp.arange(cols_here),
        jnp.arange(sheet_cols),
        row_len,
        SHEET_ROW_BLOCKS,
    )
    local_shape = (rows_here, cols_here, head_groups, HEAD_DIM)
    whole_shape = (rows_here, sheet_cols, head_groups, HEAD_DIM)
    results = line_attention(
        query[:, :, :half_width].reshape(local_shape),
        keys_row.reshape(whole_shape),
        values_row.reshape(whole_shape),
        cotangent[:, :, :half_width].reshape(local_shape),
        allowed,
        "bq",
    )
    key_terms = results[2].reshape(rows_here, sheet_cols, half_width)
    value_terms = results[3].reshape(rows_here, sheet_cols, half_width)
    key_grads, value_grads = (
        lax.psum_scatter(key_terms, "cols", scatter_dimension=1, tiled=True),
        lax.psum_scatter(value_terms, "cols", scatter_dimension=1, tiled=True),
    )
    out_row = results[0].reshape(rows_here, cols_here, half_width).astype(jnp.bfloat16)
    dq_row = results[1].reshape(rows_here, cols_here, half_width).astype(jnp.bfloat16)
    dk_row = key_grads.astype(jnp.bfloat16)
    dv_row = value_grads.astype(jnp.bfloat16)
    columns_each = cols_here // row_devices
    moved = (
        lax.all_to_all(query[:, :, half_width:], "rows", split_axis=1, concat_axis=0, tiled=True),
        lax.all_to_all(key[:, :, half_width:], "rows", split_axis=1, concat_axis=0, tiled=True),
        lax.all_to_all(value[:, :, half_width:], "rows", split_axis=1, concat_axis=0, tiled=True),
        lax.all_to_all(
            cotangent[:, :, half_width:], "rows", split_axis=1, concat_axis=0, tiled=True
        ),
    )
    column_shape = (sheet_rows, columns_each, head_groups, HEAD_DIM)
    my_tables = lax.dynamic_slice_in_dim(
        col_mask, lax.axis_index("rows") * columns_each, columns_each, 0
    )
    col_len = sheet_rows // COL_BLOCKS
    positions = jnp.arange(sheet_rows)
    col_allowed = block_allow(my_tables, positions, positions, col_len, COL_BLOCKS)
    col_results = line_attention(
        moved[0].reshape(column_shape),
        moved[1].reshape(column_shape),
        moved[2].reshape(column_shape),
        moved[3].reshape(column_shape),
        col_allowed,
        "qb",
    )
    column_flat = (sheet_rows, columns_each, half_width)
    col_pieces = [piece.reshape(column_flat).astype(jnp.bfloat16) for piece in col_results]
    out_col, dq_col, dk_col, dv_col = (
        lax.all_to_all(col_pieces[0], "rows", split_axis=0, concat_axis=1, tiled=True),
        lax.all_to_all(col_pieces[1], "rows", split_axis=0, concat_axis=1, tiled=True),
        lax.all_to_all(col_pieces[2], "rows", split_axis=0, concat_axis=1, tiled=True),
        lax.all_to_all(col_pieces[3], "rows", split_axis=0, concat_axis=1, tiled=True),
    )
    lepe = depthwise(padded_value, taps, rows_here, cols_here, False)
    back_conv = depthwise(padded_grad, taps, rows_here, cols_here, True)
    attended16 = jnp.concatenate([out_row, out_col], axis=2)
    out = (attended16.astype(jnp.float32) + lepe).astype(jnp.bfloat16)
    dquery = jnp.concatenate([dq_row, dq_col], axis=2)
    dkey = jnp.concatenate([dk_row, dk_col], axis=2)
    dvalue_attn = jnp.concatenate([dv_row, dv_col], axis=2)
    dvalue = (dvalue_attn.astype(jnp.float32) + back_conv).astype(jnp.bfloat16)
    return (out, dquery, dkey, dvalue)


SUB = 8
VMEM_LIMIT = 28 << 20
MESH = pl.DeviceIdType.MESH


def attend(q, k, v, g, allow):
    scale = 1.0 / math.sqrt(HEAD_DIM)
    nt = (((1,), (1,)), ((), ()))
    nn = (((1,), (0,)), ((), ()))
    tn = (((0,), (0,)), ((), ()))
    dot = functools.partial(lax.dot_general, preferred_element_type=jnp.float32)
    s = jnp.where(allow, dot(q, k, nt) * scale, -jnp.inf)
    e = jnp.exp(s - jnp.max(s, axis=-1, keepdims=True))
    w = e * (1.0 / jnp.sum(e, axis=-1, keepdims=True))
    w16 = w.astype(jnp.bfloat16)
    att = dot(w16, v, nn)
    dw = dot(g, v, nt)
    delta = jnp.sum(g.astype(jnp.float32) * att, axis=-1, keepdims=True)
    ds = (w * (dw - delta) * scale).astype(jnp.bfloat16)
    return att, dot(ds, k, nn), dot(ds, q, tn), dot(w16, g, tn)


def dots():
    dot = functools.partial(lax.dot_general, preferred_element_type=jnp.float32)
    return (
        functools.partial(dot, dimension_numbers=(((1,), (1,)), ((), ()))),
        functools.partial(dot, dimension_numbers=(((1,), (0,)), ((), ()))),
        functools.partial(dot, dimension_numbers=(((0,), (0,)), ((), ()))),
    )


def softmax(q, k, allow):
    nt, _, _ = dots()
    s = jnp.where(allow, nt(q, k) * (1.0 / math.sqrt(HEAD_DIM)), -jnp.inf)
    e = jnp.exp(s - jnp.max(s, axis=-1, keepdims=True))
    return e * (1.0 / jnp.sum(e, axis=-1, keepdims=True))


def layer_kernel(dims, q_hbm, k_hbm, v_hbm, g_hbm, taps, row_mask, col_mask, ret, *rest):
    R, C, rows, groups, width = dims
    colbuf, colout, rowbuf, rowout, ext, conv, hop, land, weights, attended = rest[:10]
    (ci_s, ci_r, co_s, co_r, ri_s, ri_r, ro_s, ro_r, ha_s, ha_r, bo_s, bo_r, local, ends_in) = rest[10:]
    half = width // 2
    share = half // C
    heads = half // HEAD_DIM
    me = lax.axis_index("rows")
    mc = lax.axis_index("cols")
    inputs = (q_hbm, k_hbm, v_hbm, g_hbm)
    f32 = jnp.float32
    first, second = pl.ds(0, half), pl.ds(half, half)

    def lanes(start, size):
        return pl.ds(pl.multiple_of(start, 128), size)

    def send(src, dst, send_sem, recv_sem, target):
        return pltpu.make_async_remote_copy(
            src_ref=src, dst_ref=dst, send_sem=send_sem, recv_sem=recv_sem,
            device_id=target, device_id_type=MESH)

    def home(t):
        return land.at[t // 3] if t in (0, 3) else ret.at[t]

    def col_in(t, p, slot):
        return send(inputs[t].at[:, p, :, second], colbuf.at[t, slot],
                    ci_s.at[t, p], ci_r.at[t, slot], {"rows": p})

    def col_back(t, p, slot):
        if t == 1:
            pair = pl.ds(1, 2)
            src, dst = colout.at[pair, p], ret.at[pair, :, slot, :, second]
        else:
            src, dst = colout.at[t, p], land.at[t // 3, :, slot, :, second]
        return send(src, dst, co_s.at[t, p], co_r.at[t, slot], {"rows": p})

    def row_in(t, p, slot):
        return send(inputs[t].at[:, :, :, lanes(p * share, share)], rowbuf.at[t, :, slot],
                    ri_s.at[t, p], ri_r.at[t, slot], {"cols": p})

    def row_back(t, p, slot):
        return send(rowout.at[t, :, p], home(t).at[:, :, :, lanes(slot * share, share)],
                    ro_s.at[t, p], ro_r.at[t, slot], {"cols": p})

    odd = lax.rem(me, 2)
    sign = 2 * odd - 1
    crosses = jnp.logical_and(me + sign >= 0, me + sign < R)
    relays = jnp.logical_and(me - 2 * sign >= 0, me - 2 * sign < R)
    inner = pl.ds(1, groups)
    even_slot, odd_slot = (1 - odd) * (rows + 1), odd * (rows + 1)
    mid = R // 2
    side = me // mid
    gate = mid - 1 + side
    at_gate = me == gate
    beside_gate = me - sign == gate
    direct = 3 * half // 4
    extra = half - direct
    owned, others = pl.ds(side * mid, mid), pl.ds((1 - side) * mid, mid)

    def halo(kind, t, src, dst, target):
        return send(src, dst, ha_s.at[kind, t], ha_r.at[kind, t], target)

    def part(n):
        if n == 0:
            return pl.ds(0, groups), pl.ds(direct, extra), pl.ds(0, extra)
        return (owned, others)[n - 1], second, pl.ds(extra, half)

    def cross(t, slot):
        return halo(0, t, inputs[2 + t].at[odd * (rows - 1), :, :, pl.ds(0, direct)],
                    ext.at[t, slot, inner, :, pl.ds(0, direct)], {"rows": me + sign})

    def detour(t, n):
        span, features, place = part(n)
        return halo(1 + n, t, inputs[2 + t].at[odd * (rows - 1), span, :, features],
                    hop.at[t, span, :, place], {"rows": me - sign})

    def forward(t, slot, n):
        span, features, place = part(n)
        return halo(4 + n, t, hop.at[t, span, :, place],
                    ext.at[t, slot, inner].at[span, :, features], {"rows": me - 2 * sign})

    def near(t, slot):
        return halo(7, t, inputs[2 + t].at[(1 - odd) * (rows - 1)], ext.at[t, slot, inner], {"rows": me - sign})

    def rightward(t):
        return halo(8, t, inputs[2 + t].at[:, groups - 1], ext.at[t, pl.ds(1, rows), 0], {"cols": mc + 1})

    def leftward(t):
        return halo(9, t, inputs[2 + t].at[:, 0], ext.at[t, pl.ds(1, rows), groups + 1], {"cols": mc - 1})

    def corner_right(t, e):
        r = e * (rows + 1)
        return halo(10 + e, t, ext.at[t, r, groups], ext.at[t, r, 0], {"cols": mc + 1})

    def corner_left(t, e):
        r = e * (rows + 1)
        return halo(12 + e, t, ext.at[t, r, 1], ext.at[t, r, groups + 1], {"cols": mc - 1})

    def border_copy(t, p):
        here = colbuf.at[2 + t, mid - side, side * (rows - 1)]
        there = ext.at[t, (1 - side) * (rows + 1), 1 + p, :, second]
        return here, there

    def border(t, p):
        here, there = border_copy(t, p)
        return send(here, there, bo_s.at[t], bo_r.at[t, p], {"rows": gate})

    def border_own(t):
        here, there = border_copy(t, me)
        return pltpu.make_async_copy(here, there, local.at[2, t])

    order = sorted(range(1, R), key=lambda d: abs(d - R / 2))
    col_order = sorted(range(1, C), key=lambda d: abs(d - C / 2))
    away = jnp.logical_not(at_gate)
    has_right, has_left = mc < C - 1, mc > 0

    def each_piece(gone, act):
        for t in range(2):
            for n in range(3):
                if n < 2:
                    act(t, n)
                else:
                    pl.when(jnp.logical_not(gone))(functools.partial(act, t, n))

    quarter = R // 4
    in_mid = jnp.logical_and(me >= quarter, me < R - quarter)
    far_mid = mid - side * quarter
    near_mid = quarter + side * quarter
    far_end, near_end = (1 - side) * (R - quarter), side * (R - quarter)
    barrier = pltpu.get_barrier_semaphore()

    def tell(semaphore, target):
        pl.semaphore_signal(semaphore, inc=1, device_id=target, device_id_type=MESH)

    for d in range(1, C):
        tell(barrier, {"cols": lax.rem(mc + d, C)})

    @pl.when(in_mid)
    def _():
        for d in range(1, R):
            tell(barrier, {"rows": lax.rem(me + d, R)})
        pl.semaphore_wait(barrier, mid - 1 + C - 1)

    @pl.when(jnp.logical_not(in_mid))
    def _():
        for base in (far_end, near_end):
            for j in range(quarter):
                @pl.when(base + j != me)
                def _(p=base + j):
                    tell(barrier, {"rows": p})
        pl.semaphore_wait(barrier, R - 1 + C - 1)
        for j in range(mid):
            tell(ends_in, {"rows": quarter + j})

    def send_cols(kinds, bases):
        for t in kinds:
            for base in bases:
                for j in range(quarter):
                    @pl.when(base + j != me)
                    def _(t=t, p=base + j):
                        col_in(t, p, me).start()

    send_cols((0, 1), (far_mid, near_mid))

    @pl.when(in_mid)
    def _():
        pl.semaphore_wait(ends_in, 2 * quarter)

    send_cols((0, 1), (far_end, near_end))
    send_cols((2, 3), (far_mid, far_end, near_mid, near_end))

    def send_halo():
        @pl.when(crosses)
        def _():
            each_piece(at_gate, lambda t, n: detour(t, n).start())
            for t in range(2):
                cross(t, even_slot).start()

        for t in range(2):
            near(t, odd_slot).start()

    def send_sides():
        @pl.when(has_right)
        def _():
            for t in range(2):
                rightward(t).start()

        @pl.when(has_left)
        def _():
            for t in range(2):
                leftward(t).start()

    def pass_halo():
        @pl.when(relays)
        def _():
            def act(t, n):
                detour(t, n).wait_recv()
                forward(t, odd_slot, n).start()

            each_piece(beside_gate, act)

    def send_rows(t):
        for d in col_order:
            row_in(t, lax.rem(mc + d, C), mc).start()

    for t in range(4):
        send_rows(t)
    send_halo()
    send_sides()

    near_copies = []
    for t in range(4):
        near_copies.append(pltpu.make_async_copy(inputs[t].at[:, :, :, lanes(mc * share, share)], rowbuf.at[t, :, mc], local.at[0, t]))
        near_copies.append(pltpu.make_async_copy(inputs[t].at[:, me, :, second], colbuf.at[t, me], local.at[1, t]))
    for t in range(2):
        near_copies.append(pltpu.make_async_copy(inputs[2 + t], ext.at[t, pl.ds(1, rows), inner], local.at[2, t]))
    for c in near_copies:
        c.start()
    for edge, area in (
        (me == 0, (slice(None), 0, inner)),
        (me == R - 1, (slice(None), rows + 1, inner)),
        (mc == 0, (slice(None), slice(None), 0)),
        (mc == C - 1, (slice(None), slice(None), groups + 1)),
    ):
        @pl.when(edge)
        def _(area=area):
            for t in range(2):
                view = ext.at[(t,) + area[1:]]
                view[...] = jnp.zeros(view.shape, view.dtype)
    for c in near_copies:
        c.wait()

    length = R * rows * SUB
    col_size = length // COL_BLOCKS
    key_pos = lax.broadcasted_iota(jnp.int32, (SUB, length), 1)
    lane_col = lax.broadcasted_iota(jnp.int32, (SUB, length), 0)
    block = jnp.where(lax.rem(key_pos, SUB) == lane_col, key_pos // col_size, -1)
    col_tables = []
    for b in range(COL_BLOCKS):
        table = jnp.zeros((SUB, length), jnp.int32)
        for c in range(SUB):
            for j in range(COL_BLOCKS):
                here = jnp.logical_and(lane_col == c, block == j)
                table = jnp.where(here, col_mask[b, j, me * SUB + c], table)
        col_tables.append(table)

    pass_halo()

    for t in range(4):
        for d in col_order:
            p = lax.rem(mc + d, C)
            row_in(t, p, p).wait_recv()
    tokens = C * groups * SUB

    def row_step(n, carry):
        i, h = n // (share // HEAD_DIM), lax.rem(n, share // HEAD_DIM)
        cols = lanes(h * HEAD_DIM, HEAD_DIM)
        x = [rowbuf[t, i, :, :, :, cols].astype(f32).reshape(tokens, HEAD_DIM).astype(jnp.bfloat16) for t in range(4)]
        size = tokens // SHEET_ROW_BLOCKS
        place = lax.broadcasted_iota(jnp.int32, (SUB, tokens), 1) // size
        bands = []
        for b in range(SHEET_ROW_BLOCKS):
            table = jnp.zeros((SUB, tokens), jnp.int32)
            for j in range(SHEET_ROW_BLOCKS):
                table = jnp.where(place == j, row_mask[b, j, i], table)
            bands.append(jnp.broadcast_to(table[None], (size // SUB, SUB, tokens)).reshape(size, tokens))
        allow = jnp.concatenate(bands, axis=0) > 0
        for t, y in enumerate(attend(*x, allow)):
            rowout[t, i, :, :, :, cols] = y.reshape(C, groups, SUB, HEAD_DIM).astype(jnp.bfloat16)
        return carry

    lax.fori_loop(0, rows * (share // HEAD_DIM), row_step, 0)
    kept = []
    for t in (0, 3, 1, 2):
        for d in col_order:
            row_back(t, lax.rem(mc + d, C), mc).start()
    for t in range(4):
        kept.append([pltpu.make_async_copy(rowout.at[t, :, mc], home(t).at[:, :, :, lanes(mc * share, share)], local.at[0, t])])
        kept[t][0].start()

    nt, nn, tn = dots()

    def arrived(t):
        for d in order:
            p = lax.rem(me + d, R)
            col_in(t, p, p).wait_recv()

    def give_back(t):
        for d in order:
            col_back(t, lax.rem(me + d, R), me).start()
        for u in (1, 2) if t == 1 else (t,):
            kept[u].append(pltpu.make_async_copy(colout.at[u, me], home(u).at[:, me, :, second], local.at[1, u]))
            kept[u][1].start()

    def column(t, h):
        return colbuf[t, :, :, :, lanes(h * HEAD_DIM, HEAD_DIM)].astype(f32).reshape(length, HEAD_DIM).astype(jnp.bfloat16)

    def give(t, h, y):
        colout[t, :, :, :, lanes(h * HEAD_DIM, HEAD_DIM)] = y.reshape(R, rows, SUB, HEAD_DIM).astype(jnp.bfloat16)

    def weigh(h, carry):
        allow = jnp.concatenate(
            [jnp.broadcast_to(t[None], (col_size // SUB, SUB, length)).reshape(col_size, length) for t in col_tables], axis=0) > 0
        weights[h] = softmax(column(0, h), column(1, h), allow)
        return carry

    def forward_step(h, carry):
        att = nn(weights[h].astype(jnp.bfloat16), column(2, h))
        attended[h] = att
        give(0, h, att)
        return carry

    def value_step(h, carry):
        give(3, h, tn(weights[h].astype(jnp.bfloat16), column(3, h)))
        return carry

    def score_step(h, carry):
        g = column(3, h)
        delta = jnp.sum(g.astype(f32) * attended[h], axis=-1, keepdims=True)
        ds = (weights[h] * (nt(g, column(2, h)) - delta) * (1.0 / math.sqrt(HEAD_DIM))).astype(jnp.bfloat16)
        give(1, h, nn(ds, column(1, h)))
        give(2, h, tn(ds, column(0, h)))
        return carry

    def send_border(t):
        @pl.when(away)
        def _():
            border(t, me).start()

        @pl.when(at_gate)
        def _():
            border_own(t).start()

    arrived(0)
    arrived(1)
    lax.fori_loop(0, heads, weigh, 0)
    arrived(2)
    send_border(0)
    lax.fori_loop(0, heads, forward_step, 0)
    give_back(0)
    arrived(3)
    send_border(1)
    lax.fori_loop(0, heads, value_step, 0)
    give_back(3)

    for t in range(2):
        near(t, even_slot).wait_recv()

    @pl.when(crosses)
    def _():
        for t in range(2):
            cross(t, odd_slot).wait_recv()
        each_piece(at_gate, lambda t, n: forward(t, odd_slot, n).wait_recv())

    @pl.when(at_gate)
    def _():
        for t in range(2):
            border_own(t).wait()
            for j in range(mid):
                p = side * mid + j

                @pl.when(p != me)
                def _(t=t, p=p):
                    border(t, p).wait_recv()

    for t in range(2):
        for e in range(2):
            @pl.when(has_right)
            def _(t=t, e=e):
                corner_right(t, e).start()

            @pl.when(has_left)
            def _(t=t, e=e):
                corner_left(t, e).start()

    lax.fori_loop(0, heads, score_step, 0)
    give_back(1)

    @pl.when(has_left)
    def _():
        for t in range(2):
            rightward(t).wait_recv()
            for e in range(2):
                corner_right(t, e).wait_recv()

    @pl.when(has_right)
    def _():
        for t in range(2):
            leftward(t).wait_recv()
            for e in range(2):
                corner_left(t, e).wait_recv()

    long = groups * SUB

    def conv_step(n, carry):
        cols = lanes(n * 128, 128)
        taps_here = taps[:, cols].astype(f32)
        for t in range(2):
            sums = [None] * rows
            for r in range(rows + 2):
                line = ext[t, r, :, :, cols].astype(f32).reshape(long + 2 * SUB, 128)
                for b in range(3):
                    seen = line[SUB + b - 1 : SUB + b - 1 + long]
                    for a in range(3):
                        o = r - a
                        if 0 <= o < rows:
                            tap = 3 * a + b if t == 0 else 8 - 3 * a - b
                            term = taps_here[tap : tap + 1] * seen
                            sums[o] = term if sums[o] is None else sums[o] + term
            for o in range(rows):
                conv[t, o, :, :, cols] = sums[o].reshape(groups, SUB, 128)
        return carry

    lax.fori_loop(0, width // 128, conv_step, 0)

    for t in range(4):
        for d in col_order:
            p = lax.rem(mc + d, C)
            row_in(t, p, p).wait_send()
            row_back(t, p, p).wait_send()
        for d in order:
            p = lax.rem(me + d, R)
            col_in(t, p, p).wait_send()
    for t in range(2):
        near(t, odd_slot).wait_send()

    @pl.when(crosses)
    def _():
        for t in range(2):
            cross(t, even_slot).wait_send()
        each_piece(at_gate, lambda t, n: detour(t, n).wait_send())

    @pl.when(relays)
    def _():
        each_piece(beside_gate, lambda t, n: forward(t, odd_slot, n).wait_send())

    @pl.when(away)
    def _():
        for t in range(2):
            border(t, me).wait_send()

    @pl.when(has_right)
    def _():
        for t in range(2):
            rightward(t).wait_send()
            for e in range(2):
                corner_right(t, e).wait_send()

    @pl.when(has_left)
    def _():
        for t in range(2):
            leftward(t).wait_send()
            for e in range(2):
                corner_left(t, e).wait_send()

    def returned(t):
        for c in kept[t]:
            c.wait()
        for d in col_order:
            p = lax.rem(mc + d, C)
            row_back(t, p, p).wait_recv()
        for d in order if t != 2 else ():
            p = lax.rem(me + d, R)
            col_back(t, p, p).wait_send()
        for d in order if t != 2 else ():
            p = lax.rem(me + d, R)
            col_back(t, p, p).wait_recv()

    stored = []
    for t in range(2):
        returned(3 * t)

        def add_step(n, carry):
            cols = lanes(n * 128, 128)
            land[t, :, :, :, cols] = (land[t, :, :, :, cols].astype(f32) + conv[t, :, :, :, cols]).astype(jnp.bfloat16)
            return carry

        lax.fori_loop(0, width // 128, add_step, 0)
        stored.append(pltpu.make_async_copy(land.at[t], ret.at[3 * t], local.at[2, 2 + t]))
        stored[t].start()
    returned(2)
    returned(1)
    for c in stored:
        c.wait()


def finish_kernel(ret, *rest):
    copies = [pltpu.make_async_copy(ret.at[t], rest[t], rest[4].at[t]) for t in range(4)]
    for c in copies:
        c.start()
    for c in copies:
        c.wait()


def fused_body(query, key, value, cotangent, conv_weight, row_mask, col_mask):
    rows, cols_here, width = query.shape
    R, C = lax.axis_size("rows"), lax.axis_size("cols")
    groups = cols_here // SUB
    half = width // 2
    share = half // C
    views = [x.reshape(rows, groups, SUB, width) for x in (query, key, value, cotangent)]
    bf16 = jnp.bfloat16
    any_spec = pl.BlockSpec(memory_space=pl.ANY)
    vmem = pl.BlockSpec(memory_space=pltpu.VMEM)
    dma = pltpu.SemaphoreType.DMA
    smem = pl.BlockSpec(memory_space=pltpu.SMEM)
    heads = half // HEAD_DIM
    length = R * rows * SUB
    ret = pl.pallas_call(
        functools.partial(layer_kernel, (R, C, rows, groups, width)),
        out_shape=jax.ShapeDtypeStruct((4, rows, groups, SUB, width), bf16),
        in_specs=[any_spec] * 4 + [vmem, smem, smem],
        out_specs=any_spec,
        scratch_shapes=[
            pltpu.VMEM((4, R, rows, SUB, half), bf16),
            pltpu.VMEM((4, R, rows, SUB, half), bf16),
            pltpu.VMEM((4, rows, C, groups, SUB, share), bf16),
            pltpu.VMEM((4, rows, C, groups, SUB, share), bf16),
            pltpu.VMEM((2, rows + 2, groups + 2, SUB, width), bf16),
            pltpu.VMEM((2, rows, groups, SUB, width), jnp.float32),
            pltpu.VMEM((2, groups, SUB, half + half // 4), bf16),
            pltpu.VMEM((2, rows, groups, SUB, width), bf16),
            pltpu.VMEM((heads, length, length), jnp.float32),
            pltpu.VMEM((heads, length, HEAD_DIM), jnp.float32),
            dma((4, R)), dma((4, R)), dma((4, R)), dma((4, R)),
            dma((4, C)), dma((4, C)), dma((4, C)), dma((4, C)),
            dma((14, 2)), dma((14, 2)), dma((2,)), dma((2, R)), dma((3, 4)), pltpu.SemaphoreType.REGULAR,
        ],
        compiler_params=pltpu.CompilerParams(collective_id=0, has_side_effects=True, vmem_limit_bytes=VMEM_LIMIT),
    )(*[pltpu.with_memory_space_constraint(x, pltpu.HBM) for x in (*views, conv_weight, jnp.transpose(row_mask, (1, 2, 0)), jnp.transpose(col_mask, (1, 2, 0)))])
    outs = pl.pallas_call(
        finish_kernel,
        out_shape=[jax.ShapeDtypeStruct((rows, groups, SUB, width), bf16)] * 4,
        in_specs=[any_spec],
        out_specs=[any_spec] * 4,
        scratch_shapes=[dma((4,))],
        compiler_params=pltpu.CompilerParams(vmem_limit_bytes=1 << 20),
    )(ret)
    return tuple(x.reshape(query.shape) for x in outs)


def any_body(query, key, value, cotangent, conv_weight, row_mask, col_mask):
    rows, cols_here, width = query.shape
    R, C = lax.axis_size("rows"), lax.axis_size("cols")
    fits = R % 4 == 0 and cols_here == R * SUB and (width // 2) % (C * HEAD_DIM) == 0 and (width // 2) % (4 * HEAD_DIM) == 0
    chosen = fused_body if fits else body
    return chosen(query, key, value, cotangent, conv_weight, row_mask, col_mask)


def solution(mesh):
    return jax.shard_map(
        any_body,
        mesh=mesh,
        in_specs=(
            P("rows", "cols", None),
            P("rows", "cols", None),
            P("rows", "cols", None),
            P("rows", "cols", None),
            P(),
            P("rows", None, None),
            P("cols", None, None),
        ),
        out_specs=(
            P("rows", "cols", None),
            P("rows", "cols", None),
            P("rows", "cols", None),
            P("rows", "cols", None),
        ),
        check_vma=False,
    )
```

```python
import functools
import math

import jax
import jax.numpy as jnp
from jax import lax
from jax.experimental import pallas as pl
from jax.experimental.pallas import tpu as pltpu
from jax.sharding import PartitionSpec as P

HEAD_DIM = 128
SHEET_ROW_BLOCKS = 2
COL_BLOCKS = 3


def padded(array, sides, width):
    for axis, dim in sides:
        devices, length = (lax.axis_size(axis), array.shape[dim])
        up = [(i, (i + 1) % devices) for i in range(devices - 1)]
        down = [(j, i) for i, j in up]
        last = lax.slice_in_dim(array, length - width, length, axis=dim)
        leading = lax.slice_in_dim(array, 0, width, axis=dim)
        before = lax.ppermute(last, axis, up)
        after = lax.ppermute(leading, axis, down)
        array = jnp.concatenate([before, array, after], axis=dim)
    return array


def block_allow(block_mask_table, query_pos, key_pos, block_len, block_count):
    labels = jnp.arange(block_count)
    query_onehot_rows = (query_pos[:, None] // block_len == labels[None, :]).astype(jnp.float32)
    key_onehot_rows = (key_pos[:, None] // block_len == labels[None, :]).astype(jnp.float32)
    merged_links = jnp.einsum(
        "xv,zvs,hs->zxh", query_onehot_rows, block_mask_table.astype(jnp.float32), key_onehot_rows
    )
    return merged_links > 0.5


def line_attention(query_part, key_part, value_part, grad_part, allowed, layout):
    if layout == "bq":
        query_form = "bqhd"
        key_layout_shape = "bkhd"
    else:
        query_form = "qbhd"
        key_layout_shape = "kbhd"
    score_scale = 1.0 / math.sqrt(query_part.shape[-1])
    pair_form = query_form + "," + key_layout_shape + "->bhqk"
    scores = (
        jnp.einsum(pair_form, query_part, key_part, preferred_element_type=jnp.float32)
        * score_scale
    )
    scores = jnp.where(allowed[:, None], scores, -jnp.inf)
    highest = jnp.max(scores, axis=-1, keepdims=True)
    weights = jnp.exp(scores - highest)
    weights = weights / jnp.sum(weights, axis=-1, keepdims=True)
    rounded = weights.astype(jnp.bfloat16)
    attended = jnp.einsum(
        "bhqk," + key_layout_shape + "->" + query_form,
        rounded,
        value_part,
        preferred_element_type=jnp.float32,
    )
    dweights = jnp.einsum(pair_form, grad_part, value_part, preferred_element_type=jnp.float32)
    delta = jnp.sum(grad_part.astype(jnp.float32) * attended, axis=-1)
    if layout == "bq":
        delta = jnp.transpose(delta, (0, 2, 1))
    else:
        delta = jnp.transpose(delta, (1, 2, 0))
    dscores = (weights * (dweights - delta[..., None]) * score_scale).astype(jnp.bfloat16)
    dquery = jnp.einsum(
        "bhqk," + key_layout_shape + "->" + query_form,
        dscores,
        key_part,
        preferred_element_type=jnp.float32,
    )
    dkey = jnp.einsum(
        "bhqk," + query_form + "->" + key_layout_shape,
        dscores,
        query_part,
        preferred_element_type=jnp.float32,
    )
    dvalue = jnp.einsum(
        "bhqk," + query_form + "->" + key_layout_shape,
        rounded,
        grad_part,
        preferred_element_type=jnp.float32,
    )
    return (attended, dquery, dkey, dvalue)


def depthwise(padded_field, taps, rows_count, cols_count, reverse_taps):
    summed = jnp.zeros((rows_count, cols_count, taps.shape[1]), jnp.float32)
    for row_offset_start in range(3):
        for offset_col in range(3):
            if reverse_taps:
                start_row = 2 - row_offset_start
                start_col = 2 - offset_col
            else:
                start_row = row_offset_start
                start_col = offset_col
            window = padded_field[
                start_row : start_row + rows_count, start_col : start_col + cols_count
            ]
            summed = summed + taps[row_offset_start * 3 + offset_col] * window.astype(jnp.float32)
    return summed


def body(query, key, value, cotangent, conv_weight, row_mask, col_mask):
    rows_here, cols_here, width = query.shape
    half_width = width // 2
    head_groups = half_width // HEAD_DIM
    row_devices = lax.axis_size("rows")
    col_devices = lax.axis_size("cols")
    sheet_rows = rows_here * row_devices
    sheet_cols = cols_here * col_devices
    taps = conv_weight.astype(jnp.float32)
    padded_value = padded(value, (("rows", 0), ("cols", 1)), 1)
    padded_grad = padded(cotangent, (("rows", 0), ("cols", 1)), 1)
    row_len = sheet_cols // SHEET_ROW_BLOCKS
    keys_row, values_row = (
        lax.all_gather(key[:, :, :half_width], "cols", axis=1, tiled=True),
        lax.all_gather(value[:, :, :half_width], "cols", axis=1, tiled=True),
    )
    col_start = lax.axis_index("cols") * cols_here
    allowed = block_allow(
        row_mask,
        col_start + jnp.arange(cols_here),
        jnp.arange(sheet_cols),
        row_len,
        SHEET_ROW_BLOCKS,
    )
    local_shape = (rows_here, cols_here, head_groups, HEAD_DIM)
    whole_shape = (rows_here, sheet_cols, head_groups, HEAD_DIM)
    results = line_attention(
        query[:, :, :half_width].reshape(local_shape),
        keys_row.reshape(whole_shape),
        values_row.reshape(whole_shape),
        cotangent[:, :, :half_width].reshape(local_shape),
        allowed,
        "bq",
    )
    key_terms = results[2].reshape(rows_here, sheet_cols, half_width)
    value_terms = results[3].reshape(rows_here, sheet_cols, half_width)
    key_grads, value_grads = (
        lax.psum_scatter(key_terms, "cols", scatter_dimension=1, tiled=True),
        lax.psum_scatter(value_terms, "cols", scatter_dimension=1, tiled=True),
    )
    out_row = results[0].reshape(rows_here, cols_here, half_width).astype(jnp.bfloat16)
    dq_row = results[1].reshape(rows_here, cols_here, half_width).astype(jnp.bfloat16)
    dk_row = key_grads.astype(jnp.bfloat16)
    dv_row = value_grads.astype(jnp.bfloat16)
    columns_each = cols_here // row_devices
    moved = (
        lax.all_to_all(query[:, :, half_width:], "rows", split_axis=1, concat_axis=0, tiled=True),
        lax.all_to_all(key[:, :, half_width:], "rows", split_axis=1, concat_axis=0, tiled=True),
        lax.all_to_all(value[:, :, half_width:], "rows", split_axis=1, concat_axis=0, tiled=True),
        lax.all_to_all(
            cotangent[:, :, half_width:], "rows", split_axis=1, concat_axis=0, tiled=True
        ),
    )
    column_shape = (sheet_rows, columns_each, head_groups, HEAD_DIM)
    my_tables = lax.dynamic_slice_in_dim(
        col_mask, lax.axis_index("rows") * columns_each, columns_each, 0
    )
    col_len = sheet_rows // COL_BLOCKS
    positions = jnp.arange(sheet_rows)
    col_allowed = block_allow(my_tables, positions, positions, col_len, COL_BLOCKS)
    col_results = line_attention(
        moved[0].reshape(column_shape),
        moved[1].reshape(column_shape),
        moved[2].reshape(column_shape),
        moved[3].reshape(column_shape),
        col_allowed,
        "qb",
    )
    column_flat = (sheet_rows, columns_each, half_width)
    col_pieces = [piece.reshape(column_flat).astype(jnp.bfloat16) for piece in col_results]
    out_col, dq_col, dk_col, dv_col = (
        lax.all_to_all(col_pieces[0], "rows", split_axis=0, concat_axis=1, tiled=True),
        lax.all_to_all(col_pieces[1], "rows", split_axis=0, concat_axis=1, tiled=True),
        lax.all_to_all(col_pieces[2], "rows", split_axis=0, concat_axis=1, tiled=True),
        lax.all_to_all(col_pieces[3], "rows", split_axis=0, concat_axis=1, tiled=True),
    )
    lepe = depthwise(padded_value, taps, rows_here, cols_here, False)
    back_conv = depthwise(padded_grad, taps, rows_here, cols_here, True)
    attended16 = jnp.concatenate([out_row, out_col], axis=2)
    out = (attended16.astype(jnp.float32) + lepe).astype(jnp.bfloat16)
    dquery = jnp.concatenate([dq_row, dq_col], axis=2)
    dkey = jnp.concatenate([dk_row, dk_col], axis=2)
    dvalue_attn = jnp.concatenate([dv_row, dv_col], axis=2)
    dvalue = (dvalue_attn.astype(jnp.float32) + back_conv).astype(jnp.bfloat16)
    return (out, dquery, dkey, dvalue)


SUB = 8
VMEM_LIMIT = 28 << 20
MESH = pl.DeviceIdType.MESH


def attend(q, k, v, g, allow):
    scale = 1.0 / math.sqrt(HEAD_DIM)
    nt = (((1,), (1,)), ((), ()))
    nn = (((1,), (0,)), ((), ()))
    tn = (((0,), (0,)), ((), ()))
    dot = functools.partial(lax.dot_general, preferred_element_type=jnp.float32)
    s = jnp.where(allow, dot(q, k, nt) * scale, -jnp.inf)
    e = jnp.exp(s - jnp.max(s, axis=-1, keepdims=True))
    w = e * (1.0 / jnp.sum(e, axis=-1, keepdims=True))
    w16 = w.astype(jnp.bfloat16)
    att = dot(w16, v, nn)
    dw = dot(g, v, nt)
    delta = jnp.sum(g.astype(jnp.float32) * att, axis=-1, keepdims=True)
    ds = (w * (dw - delta) * scale).astype(jnp.bfloat16)
    return att, dot(ds, k, nn), dot(ds, q, tn), dot(w16, g, tn)


def dots():
    dot = functools.partial(lax.dot_general, preferred_element_type=jnp.float32)
    return (
        functools.partial(dot, dimension_numbers=(((1,), (1,)), ((), ()))),
        functools.partial(dot, dimension_numbers=(((1,), (0,)), ((), ()))),
        functools.partial(dot, dimension_numbers=(((0,), (0,)), ((), ()))),
    )


def softmax(q, k, allow):
    nt, _, _ = dots()
    s = jnp.where(allow, nt(q, k) * (1.0 / math.sqrt(HEAD_DIM)), -jnp.inf)
    e = jnp.exp(s - jnp.max(s, axis=-1, keepdims=True))
    return e * (1.0 / jnp.sum(e, axis=-1, keepdims=True))


def layer_kernel(dims, q_hbm, k_hbm, v_hbm, g_hbm, taps_hbm, row_hbm, col_hbm, ret, *rest):
    R, C, rows, groups, width = dims
    colbuf, colout, rowbuf, rowout, ext, conv, hop, land, weights, attended = rest[:10]
    sent, came, here_in, ends_in, taps, row_mask, col_mask = rest[10:]
    half = width // 2
    share = half // C
    heads = half // HEAD_DIM
    me = lax.axis_index("rows")
    mc = lax.axis_index("cols")
    inputs = (q_hbm, k_hbm, v_hbm, g_hbm)
    f32 = jnp.float32
    first, second = pl.ds(0, half), pl.ds(half, half)

    def lanes(start, size):
        return pl.ds(pl.multiple_of(start, 128), size)

    def send(src, dst, send_sem, recv_sem, target):
        return pltpu.make_async_remote_copy(
            src_ref=src, dst_ref=dst, send_sem=send_sem, recv_sem=recv_sem,
            device_id=target, device_id_type=MESH)

    col_sent, back_sent, row_sent, row_back_sent, near_sent, cross_sent, far_sent, pass_sent, pass_far_sent, border_sent, right_sent, left_sent = (
        sent.at[i] for i in range(12))
    col_came = [came.at[t] for t in range(4)]
    back_came = [came.at[4], came.at[5], came.at[5], came.at[6]]
    row_came, hop_came, hop_far_came, near_came, cross_came, right_came, left_came = (came.at[7 + i] for i in range(7))

    def drain(semaphore, ref):
        pltpu.make_async_copy(ref, ref, semaphore).wait()

    def home(t):
        return land.at[t // 3] if t in (0, 3) else ret.at[t]

    def col_in(t, p, slot):
        return send(inputs[t].at[:, p, :, second], colbuf.at[t, slot],
                    col_sent, col_came[t], {"rows": p})

    def col_back(t, p, slot):
        if t == 1:
            pair = pl.ds(1, 2)
            src, dst = colout.at[pair, p], ret.at[pair, :, slot, :, second]
        else:
            src, dst = colout.at[t, p], land.at[t // 3, :, slot, :, second]
        return send(src, dst, back_sent, back_came[t], {"rows": p})

    def row_in(t, p, slot):
        return send(inputs[t].at[:, :, :, lanes(p * share, share)], rowbuf.at[t, :, slot],
                    row_sent, row_came, {"cols": p})

    def row_back(t, p, slot):
        return send(rowout.at[t, :, p], home(t).at[:, :, :, lanes(slot * share, share)],
                    row_back_sent, back_came[t], {"cols": p})

    odd = lax.rem(me, 2)
    sign = 2 * odd - 1
    crosses = jnp.logical_and(me + sign >= 0, me + sign < R)
    relays = jnp.logical_and(me - 2 * sign >= 0, me - 2 * sign < R)
    inner = pl.ds(1, groups)
    even_slot, odd_slot = (1 - odd) * (rows + 1), odd * (rows + 1)
    mid = R // 2
    side = me // mid
    gate = mid - 1 + side
    at_gate = me == gate
    beside_gate = me - sign == gate
    direct = 3 * half // 4
    extra = half - direct
    owned = pl.ds(side * mid, mid)
    away = jnp.logical_not(at_gate)
    has_right, has_left = mc < C - 1, mc > 0

    def cross(t):
        return send(inputs[2 + t].at[odd * (rows - 1), :, :, pl.ds(0, direct)],
                    ext.at[t, even_slot, inner, :, pl.ds(0, direct)], cross_sent, cross_came, {"rows": me + sign})

    def detour(t):
        return send(inputs[2 + t].at[odd * (rows - 1), :, :, pl.ds(direct, extra)],
                    hop.at[t, :, :, pl.ds(0, extra)], cross_sent, hop_came, {"rows": me - sign})

    def detour_far(t, span):
        return send(inputs[2 + t].at[odd * (rows - 1), span, :, second],
                    hop.at[t, span, :, pl.ds(extra, half)], far_sent, hop_far_came, {"rows": me - sign})

    def forward():
        return send(hop.at[:, :, :, pl.ds(0, extra)], ext.at[:, odd_slot, inner, :, pl.ds(direct, extra)],
                    pass_sent, cross_came, {"rows": me - 2 * sign})

    def forward_far(span):
        return send(hop.at[:, span, :, pl.ds(extra, half)], ext.at[:, odd_slot, inner].at[:, span, :, second],
                    pass_far_sent, cross_came, {"rows": me - 2 * sign})

    def near(t):
        return send(inputs[2 + t].at[(1 - odd) * (rows - 1)], ext.at[t, odd_slot, inner],
                    near_sent, near_came, {"rows": me - sign})

    def rightward(t):
        return send(inputs[2 + t].at[:, groups - 1], ext.at[t, pl.ds(1, rows), 0],
                    right_sent, right_came, {"cols": mc + 1})

    def leftward(t):
        return send(inputs[2 + t].at[:, 0], ext.at[t, pl.ds(1, rows), groups + 1],
                    left_sent, left_came, {"cols": mc - 1})

    def corner_right(r):
        return send(ext.at[:, r, groups], ext.at[:, r, 0], right_sent, right_came, {"cols": mc + 1})

    def corner_left(r):
        return send(ext.at[:, r, 1], ext.at[:, r, groups + 1], left_sent, left_came, {"cols": mc - 1})

    border_from = colbuf.at[pl.ds(2, 2), mid - side, side * (rows - 1)]
    border_to = ext.at[:, (1 - side) * (rows + 1), 1 + me, :, second]

    def border():
        return send(border_from, border_to, border_sent, cross_came, {"rows": gate})

    def by_gate(gone, act):
        pl.when(gone)(functools.partial(act, owned))
        pl.when(jnp.logical_not(gone))(functools.partial(act, pl.ds(0, groups)))

    def others_on(here, count, act, spread=False):
        def step(n, carry):
            d = n + 1
            if spread:
                d = count // 2 + jnp.where(lax.rem(n, 2) == 0, d // 2, -(d // 2))
            act(lax.rem(here + d, count))
            return carry

        lax.fori_loop(0, count - 1, step, 0)

    each_row = functools.partial(others_on, me, R)
    each_col = functools.partial(others_on, mc, C)

    quarter = R // 4
    in_mid = jnp.logical_and(me >= quarter, me < R - quarter)
    far_mid = mid - side * quarter
    near_mid = quarter + side * quarter
    far_end, near_end = (1 - side) * (R - quarter), side * (R - quarter)
    barrier = pltpu.get_barrier_semaphore()

    def group(bases, act):
        def step(n, carry):
            base = bases[-1]
            for i in range(len(bases) - 1, 0, -1):
                base = jnp.where(n < i * quarter, bases[i - 1], base)
            p = base + lax.rem(n, quarter)
            pl.when(p != me)(lambda: act(p))
            return carry

        lax.fori_loop(0, len(bases) * quarter, step, 0)

    def tell(semaphore, target):
        pl.semaphore_signal(semaphore, inc=1, device_id=target, device_id_type=MESH)

    each_col(lambda p: tell(barrier, {"cols": p}))

    @pl.when(in_mid)
    def _():
        each_row(lambda p: tell(barrier, {"rows": p}))
        pl.semaphore_wait(barrier, mid - 1 + C - 1)

    @pl.when(jnp.logical_not(in_mid))
    def _():
        group((far_end, near_end), lambda p: tell(barrier, {"rows": p}))
        pl.semaphore_wait(barrier, R - 1 + C - 1)
        group((far_mid, near_mid), lambda p: tell(ends_in, {"rows": p}))

    def send_cols(kinds, bases):
        for t in kinds:
            group(bases, lambda p: col_in(t, p, me).start())

    send_cols((0, 1), (far_mid, near_mid))

    @pl.when(in_mid)
    def _():
        pl.semaphore_wait(ends_in, 2 * quarter)

    send_cols((0, 1), (far_end, near_end))
    send_cols((2, 3), (far_mid, far_end, near_mid, near_end))

    def send_halo():
        @pl.when(crosses)
        def _():
            for t in range(2):
                detour(t).start()
                by_gate(at_gate, lambda span: detour_far(t, span).start())
                cross(t).start()

        for t in range(2):
            near(t).start()

    def send_sides():
        @pl.when(has_right)
        def _():
            for t in range(2):
                rightward(t).start()

        @pl.when(has_left)
        def _():
            for t in range(2):
                leftward(t).start()

    def pass_halo():
        @pl.when(relays)
        def _():
            drain(hop_came, hop.at[:, :, :, pl.ds(0, extra)])
            forward().start()

            def act(span):
                drain(hop_far_came, hop.at[:, span, :, pl.ds(extra, half)])
                forward_far(span).start()

            by_gate(beside_gate, act)

    def send_rows(t):
        each_col(lambda p: row_in(t, p, mc).start(), spread=True)

    for t in range(4):
        send_rows(t)
    send_halo()
    send_sides()

    tables = [
        pltpu.make_async_copy(src, dst, here_in.at[i])
        for i, (src, dst) in enumerate(((taps_hbm, taps), (row_hbm, row_mask), (col_hbm, col_mask)))
    ]
    for c in tables:
        c.start()
    for t in range(4):
        pltpu.make_async_copy(inputs[t].at[:, :, :, lanes(mc * share, share)], rowbuf.at[t, :, mc], row_came).start()
        pltpu.make_async_copy(inputs[t].at[:, me, :, second], colbuf.at[t, me], col_came[t]).start()
    for t in range(2):
        pltpu.make_async_copy(inputs[2 + t], ext.at[t, pl.ds(1, rows), inner], here_in.at[3]).start()
    for edge, area in (
        (me == 0, (slice(None), 0, inner)),
        (me == R - 1, (slice(None), rows + 1, inner)),
        (mc == 0, (slice(None), slice(None), 0)),
        (mc == C - 1, (slice(None), slice(None), groups + 1)),
    ):
        @pl.when(edge)
        def _(area=area):
            for t in range(2):
                view = ext.at[(t,) + area[1:]]
                view[...] = jnp.zeros(view.shape, view.dtype)
    for c in tables:
        c.wait()

    length = R * rows * SUB
    col_size = length // COL_BLOCKS
    key_pos = lax.broadcasted_iota(jnp.int32, (SUB, length), 1)
    lane_col = lax.broadcasted_iota(jnp.int32, (SUB, length), 0)
    block = jnp.where(lax.rem(key_pos, SUB) == lane_col, key_pos // col_size, -1)
    col_tables = []
    for b in range(COL_BLOCKS):
        table = jnp.zeros((SUB, length), jnp.int32)
        for c in range(SUB):
            for j in range(COL_BLOCKS):
                here = jnp.logical_and(lane_col == c, block == j)
                table = jnp.where(here, col_mask[b, j, me * SUB + c], table)
        col_tables.append(table)

    pass_halo()

    drain(row_came, rowbuf)
    tokens = C * groups * SUB

    def row_step(n, carry):
        i, h = n // (share // HEAD_DIM), lax.rem(n, share // HEAD_DIM)
        cols = lanes(h * HEAD_DIM, HEAD_DIM)
        x = [rowbuf[t, i, :, :, :, cols].astype(f32).reshape(tokens, HEAD_DIM).astype(jnp.bfloat16) for t in range(4)]
        size = tokens // SHEET_ROW_BLOCKS
        place = lax.broadcasted_iota(jnp.int32, (SUB, tokens), 1) // size
        bands = []
        for b in range(SHEET_ROW_BLOCKS):
            table = jnp.zeros((SUB, tokens), jnp.int32)
            for j in range(SHEET_ROW_BLOCKS):
                table = jnp.where(place == j, row_mask[b, j, i], table)
            bands.append(jnp.broadcast_to(table[None], (size // SUB, SUB, tokens)).reshape(size, tokens))
        allow = jnp.concatenate(bands, axis=0) > 0
        for t, y in enumerate(attend(*x, allow)):
            rowout[t, i, :, :, :, cols] = y.reshape(C, groups, SUB, HEAD_DIM).astype(jnp.bfloat16)
        return carry

    lax.fori_loop(0, rows * (share // HEAD_DIM), row_step, 0)
    for t in (0, 3, 1, 2):
        each_col(lambda p: row_back(t, p, mc).start(), spread=True)
        pltpu.make_async_copy(rowout.at[t, :, mc], home(t).at[:, :, :, lanes(mc * share, share)], back_came[t]).start()

    nt, nn, tn = dots()

    def arrived(t):
        drain(col_came[t], colbuf.at[t])

    def give_back(t):
        each_row(lambda p: col_back(t, p, me).start(), spread=True)
        for u in (1, 2) if t == 1 else (t,):
            pltpu.make_async_copy(colout.at[u, me], home(u).at[:, me, :, second], back_came[u]).start()

    def column(t, h):
        return colbuf[t, :, :, :, lanes(h * HEAD_DIM, HEAD_DIM)].astype(f32).reshape(length, HEAD_DIM).astype(jnp.bfloat16)

    def give(t, h, y):
        colout[t, :, :, :, lanes(h * HEAD_DIM, HEAD_DIM)] = y.reshape(R, rows, SUB, HEAD_DIM).astype(jnp.bfloat16)

    def weigh(h, carry):
        allow = jnp.concatenate(
            [jnp.broadcast_to(t[None], (col_size // SUB, SUB, length)).reshape(col_size, length) for t in col_tables], axis=0) > 0
        weights[h] = softmax(column(0, h), column(1, h), allow)
        return carry

    def forward_step(h, carry):
        att = nn(weights[h].astype(jnp.bfloat16), column(2, h))
        attended[h] = att
        give(0, h, att)
        return carry

    def value_step(h, carry):
        give(3, h, tn(weights[h].astype(jnp.bfloat16), column(3, h)))
        return carry

    def score_step(h, carry):
        g = column(3, h)
        delta = jnp.sum(g.astype(f32) * attended[h], axis=-1, keepdims=True)
        ds = (weights[h] * (nt(g, column(2, h)) - delta) * (1.0 / math.sqrt(HEAD_DIM))).astype(jnp.bfloat16)
        give(1, h, nn(ds, column(1, h)))
        give(2, h, tn(ds, column(0, h)))
        return carry

    arrived(0)
    arrived(1)
    lax.fori_loop(0, heads, weigh, 0)
    arrived(2)
    lax.fori_loop(0, heads, forward_step, 0)
    give_back(0)
    arrived(3)

    @pl.when(away)
    def _():
        border().start()

    @pl.when(at_gate)
    def _():
        pltpu.make_async_copy(border_from, border_to, cross_came).start()

    lax.fori_loop(0, heads, value_step, 0)
    give_back(3)

    drain(near_came, ext.at[:, even_slot, inner])

    @pl.when(crosses)
    def _():
        drain(cross_came, ext.at[:, odd_slot, inner])

    for r in (0, rows + 1):
        @pl.when(has_right)
        def _(r=r):
            corner_right(r).start()

        @pl.when(has_left)
        def _(r=r):
            corner_left(r).start()

    lax.fori_loop(0, heads, score_step, 0)
    give_back(1)

    @pl.when(has_left)
    def _():
        drain(right_came, ext.at[:, :, 0])

    @pl.when(has_right)
    def _():
        drain(left_came, ext.at[:, :, groups + 1])

    drain(here_in.at[3], ext.at[:, pl.ds(1, rows), inner])
    long = groups * SUB

    def conv_step(n, carry):
        cols = lanes(n * 128, 128)
        taps_here = taps[:, cols].astype(f32)
        for t in range(2):
            sums = [None] * rows
            for r in range(rows + 2):
                line = ext[t, r, :, :, cols].astype(f32).reshape(long + 2 * SUB, 128)
                for b in range(3):
                    seen = line[SUB + b - 1 : SUB + b - 1 + long]
                    for a in range(3):
                        o = r - a
                        if 0 <= o < rows:
                            tap = 3 * a + b if t == 0 else 8 - 3 * a - b
                            term = taps_here[tap : tap + 1] * seen
                            sums[o] = term if sums[o] is None else sums[o] + term
            for o in range(rows):
                conv[t, o, :, :, cols] = sums[o].reshape(groups, SUB, 128)
        return carry

    lax.fori_loop(0, width // 128, conv_step, 0)

    drain(col_sent, colbuf.at[:, pl.ds(0, R - 1)])
    for semaphore in (row_sent, row_back_sent):
        drain(semaphore, rowbuf.at[:, :, pl.ds(0, C - 1)])
    drain(near_sent, ext.at[:, 0, inner])

    @pl.when(crosses)
    def _():
        drain(cross_sent, ext.at[:, 0, inner, :, first])
        by_gate(at_gate, lambda span: drain(far_sent, ext.at[:, 0, inner].at[:, span, :, second]))

    @pl.when(relays)
    def _():
        drain(pass_sent, hop.at[:, :, :, pl.ds(0, extra)])
        by_gate(beside_gate, lambda span: drain(pass_far_sent, hop.at[:, span, :, pl.ds(extra, half)]))

    @pl.when(away)
    def _():
        drain(border_sent, border_from)

    @pl.when(has_right)
    def _():
        drain(right_sent, ext.at[:, :, 0])

    @pl.when(has_left)
    def _():
        drain(left_sent, ext.at[:, :, 0])

    stored = []
    for t in range(2):
        drain(back_came[3 * t], land.at[t])

        def add_step(n, carry):
            cols = lanes(n * 128, 128)
            land[t, :, :, :, cols] = (land[t, :, :, :, cols].astype(f32) + conv[t, :, :, :, cols]).astype(jnp.bfloat16)
            return carry

        lax.fori_loop(0, width // 128, add_step, 0)
        stored.append(pltpu.make_async_copy(land.at[t], ret.at[3 * t], here_in.at[4 + t]))
        stored[t].start()
    drain(back_sent, colbuf.at[:, pl.ds(0, R - 1)])
    drain(back_came[1], ret.at[pl.ds(1, 2)])
    for c in stored:
        c.wait()


def finish_kernel(ret, *rest):
    copies = [pltpu.make_async_copy(ret.at[t], rest[t], rest[4].at[t]) for t in range(4)]
    for c in copies:
        c.start()
    for c in copies:
        c.wait()


def fused_body(query, key, value, cotangent, conv_weight, row_mask, col_mask):
    rows, cols_here, width = query.shape
    R, C = lax.axis_size("rows"), lax.axis_size("cols")
    groups = cols_here // SUB
    half = width // 2
    share = half // C
    views = [x.reshape(rows, groups, SUB, width) for x in (query, key, value, cotangent)]
    bf16 = jnp.bfloat16
    any_spec = pl.BlockSpec(memory_space=pl.ANY)
    dma = pltpu.SemaphoreType.DMA
    heads = half // HEAD_DIM
    length = R * rows * SUB
    row_table, col_table = jnp.transpose(row_mask, (1, 2, 0)), jnp.transpose(col_mask, (1, 2, 0))
    ret = pl.pallas_call(
        functools.partial(layer_kernel, (R, C, rows, groups, width)),
        out_shape=jax.ShapeDtypeStruct((4, rows, groups, SUB, width), bf16),
        in_specs=[any_spec] * 7,
        out_specs=any_spec,
        scratch_shapes=[
            pltpu.VMEM((4, R, rows, SUB, half), bf16),
            pltpu.VMEM((4, R, rows, SUB, half), bf16),
            pltpu.VMEM((4, rows, C, groups, SUB, share), bf16),
            pltpu.VMEM((4, rows, C, groups, SUB, share), bf16),
            pltpu.VMEM((2, rows + 2, groups + 2, SUB, width), bf16),
            pltpu.VMEM((2, rows, groups, SUB, width), jnp.float32),
            pltpu.VMEM((2, groups, SUB, half + half // 4), bf16),
            pltpu.VMEM((2, rows, groups, SUB, width), bf16),
            pltpu.VMEM((heads, length, length), jnp.float32),
            pltpu.VMEM((heads, length, HEAD_DIM), jnp.float32),
            dma((12,)), dma((14,)), dma((6,)), pltpu.SemaphoreType.REGULAR,
            pltpu.VMEM(conv_weight.shape, bf16), pltpu.SMEM(row_table.shape, jnp.int32), pltpu.SMEM(col_table.shape, jnp.int32),
        ],
        compiler_params=pltpu.CompilerParams(collective_id=0, has_side_effects=True, vmem_limit_bytes=VMEM_LIMIT),
    )(*[pltpu.with_memory_space_constraint(x, pltpu.HBM) for x in (*views, conv_weight, row_table, col_table)])
    outs = pl.pallas_call(
        finish_kernel,
        out_shape=[jax.ShapeDtypeStruct((rows, groups, SUB, width), bf16)] * 4,
        in_specs=[any_spec],
        out_specs=[any_spec] * 4,
        scratch_shapes=[dma((4,))],
        compiler_params=pltpu.CompilerParams(vmem_limit_bytes=1 << 20),
    )(ret)
    return tuple(x.reshape(query.shape) for x in outs)


def any_body(query, key, value, cotangent, conv_weight, row_mask, col_mask):
    rows, cols_here, width = query.shape
    R, C = lax.axis_size("rows"), lax.axis_size("cols")
    fits = R % 4 == 0 and cols_here == R * SUB and (width // 2) % (C * HEAD_DIM) == 0 and (width // 2) % (4 * HEAD_DIM) == 0
    chosen = fused_body if fits else body
    return chosen(query, key, value, cotangent, conv_weight, row_mask, col_mask)


def solution(mesh):
    return jax.shard_map(
        any_body,
        mesh=mesh,
        in_specs=(
            P("rows", "cols", None),
            P("rows", "cols", None),
            P("rows", "cols", None),
            P("rows", "cols", None),
            P(),
            P("rows", None, None),
            P("cols", None, None),
        ),
        out_specs=(
            P("rows", "cols", None),
            P("rows", "cols", None),
            P("rows", "cols", None),
            P("rows", "cols", None),
        ),
        check_vma=False,
    )
```

```python
import functools
import math

import jax
import jax.numpy as jnp
from jax import lax
from jax.experimental import pallas as pl
from jax.experimental.pallas import tpu as pltpu
from jax.sharding import PartitionSpec as P

HEAD_DIM = 128
SHEET_ROW_BLOCKS = 2
COL_BLOCKS = 3


def padded(array, sides, width):
    for axis, dim in sides:
        devices, length = (lax.axis_size(axis), array.shape[dim])
        up = [(i, (i + 1) % devices) for i in range(devices - 1)]
        down = [(j, i) for i, j in up]
        last = lax.slice_in_dim(array, length - width, length, axis=dim)
        leading = lax.slice_in_dim(array, 0, width, axis=dim)
        before = lax.ppermute(last, axis, up)
        after = lax.ppermute(leading, axis, down)
        array = jnp.concatenate([before, array, after], axis=dim)
    return array


def block_allow(block_mask_table, query_pos, key_pos, block_len, block_count):
    labels = jnp.arange(block_count)
    query_onehot_rows = (query_pos[:, None] // block_len == labels[None, :]).astype(jnp.float32)
    key_onehot_rows = (key_pos[:, None] // block_len == labels[None, :]).astype(jnp.float32)
    merged_links = jnp.einsum(
        "xv,zvs,hs->zxh", query_onehot_rows, block_mask_table.astype(jnp.float32), key_onehot_rows
    )
    return merged_links > 0.5


def line_attention(query_part, key_part, value_part, grad_part, allowed, layout):
    if layout == "bq":
        query_form = "bqhd"
        key_layout_shape = "bkhd"
    else:
        query_form = "qbhd"
        key_layout_shape = "kbhd"
    score_scale = 1.0 / math.sqrt(query_part.shape[-1])
    pair_form = query_form + "," + key_layout_shape + "->bhqk"
    scores = (
        jnp.einsum(pair_form, query_part, key_part, preferred_element_type=jnp.float32)
        * score_scale
    )
    scores = jnp.where(allowed[:, None], scores, -jnp.inf)
    highest = jnp.max(scores, axis=-1, keepdims=True)
    weights = jnp.exp(scores - highest)
    weights = weights / jnp.sum(weights, axis=-1, keepdims=True)
    rounded = weights.astype(jnp.bfloat16)
    attended = jnp.einsum(
        "bhqk," + key_layout_shape + "->" + query_form,
        rounded,
        value_part,
        preferred_element_type=jnp.float32,
    )
    dweights = jnp.einsum(pair_form, grad_part, value_part, preferred_element_type=jnp.float32)
    delta = jnp.sum(grad_part.astype(jnp.float32) * attended, axis=-1)
    if layout == "bq":
        delta = jnp.transpose(delta, (0, 2, 1))
    else:
        delta = jnp.transpose(delta, (1, 2, 0))
    dscores = (weights * (dweights - delta[..., None]) * score_scale).astype(jnp.bfloat16)
    dquery = jnp.einsum(
        "bhqk," + key_layout_shape + "->" + query_form,
        dscores,
        key_part,
        preferred_element_type=jnp.float32,
    )
    dkey = jnp.einsum(
        "bhqk," + query_form + "->" + key_layout_shape,
        dscores,
        query_part,
        preferred_element_type=jnp.float32,
    )
    dvalue = jnp.einsum(
        "bhqk," + query_form + "->" + key_layout_shape,
        rounded,
        grad_part,
        preferred_element_type=jnp.float32,
    )
    return (attended, dquery, dkey, dvalue)


def depthwise(padded_field, taps, rows_count, cols_count, reverse_taps):
    summed = jnp.zeros((rows_count, cols_count, taps.shape[1]), jnp.float32)
    for row_offset_start in range(3):
        for offset_col in range(3):
            if reverse_taps:
                start_row = 2 - row_offset_start
                start_col = 2 - offset_col
            else:
                start_row = row_offset_start
                start_col = offset_col
            window = padded_field[
                start_row : start_row + rows_count, start_col : start_col + cols_count
            ]
            summed = summed + taps[row_offset_start * 3 + offset_col] * window.astype(jnp.float32)
    return summed


def body(query, key, value, cotangent, conv_weight, row_mask, col_mask):
    rows_here, cols_here, width = query.shape
    half_width = width // 2
    head_groups = half_width // HEAD_DIM
    row_devices = lax.axis_size("rows")
    col_devices = lax.axis_size("cols")
    sheet_rows = rows_here * row_devices
    sheet_cols = cols_here * col_devices
    taps = conv_weight.astype(jnp.float32)
    padded_value = padded(value, (("rows", 0), ("cols", 1)), 1)
    padded_grad = padded(cotangent, (("rows", 0), ("cols", 1)), 1)
    row_len = sheet_cols // SHEET_ROW_BLOCKS
    keys_row, values_row = (
        lax.all_gather(key[:, :, :half_width], "cols", axis=1, tiled=True),
        lax.all_gather(value[:, :, :half_width], "cols", axis=1, tiled=True),
    )
    col_start = lax.axis_index("cols") * cols_here
    allowed = block_allow(
        row_mask,
        col_start + jnp.arange(cols_here),
        jnp.arange(sheet_cols),
        row_len,
        SHEET_ROW_BLOCKS,
    )
    local_shape = (rows_here, cols_here, head_groups, HEAD_DIM)
    whole_shape = (rows_here, sheet_cols, head_groups, HEAD_DIM)
    results = line_attention(
        query[:, :, :half_width].reshape(local_shape),
        keys_row.reshape(whole_shape),
        values_row.reshape(whole_shape),
        cotangent[:, :, :half_width].reshape(local_shape),
        allowed,
        "bq",
    )
    key_terms = results[2].reshape(rows_here, sheet_cols, half_width)
    value_terms = results[3].reshape(rows_here, sheet_cols, half_width)
    key_grads, value_grads = (
        lax.psum_scatter(key_terms, "cols", scatter_dimension=1, tiled=True),
        lax.psum_scatter(value_terms, "cols", scatter_dimension=1, tiled=True),
    )
    out_row = results[0].reshape(rows_here, cols_here, half_width).astype(jnp.bfloat16)
    dq_row = results[1].reshape(rows_here, cols_here, half_width).astype(jnp.bfloat16)
    dk_row = key_grads.astype(jnp.bfloat16)
    dv_row = value_grads.astype(jnp.bfloat16)
    columns_each = cols_here // row_devices
    moved = (
        lax.all_to_all(query[:, :, half_width:], "rows", split_axis=1, concat_axis=0, tiled=True),
        lax.all_to_all(key[:, :, half_width:], "rows", split_axis=1, concat_axis=0, tiled=True),
        lax.all_to_all(value[:, :, half_width:], "rows", split_axis=1, concat_axis=0, tiled=True),
        lax.all_to_all(
            cotangent[:, :, half_width:], "rows", split_axis=1, concat_axis=0, tiled=True
        ),
    )
    column_shape = (sheet_rows, columns_each, head_groups, HEAD_DIM)
    my_tables = lax.dynamic_slice_in_dim(
        col_mask, lax.axis_index("rows") * columns_each, columns_each, 0
    )
    col_len = sheet_rows // COL_BLOCKS
    positions = jnp.arange(sheet_rows)
    col_allowed = block_allow(my_tables, positions, positions, col_len, COL_BLOCKS)
    col_results = line_attention(
        moved[0].reshape(column_shape),
        moved[1].reshape(column_shape),
        moved[2].reshape(column_shape),
        moved[3].reshape(column_shape),
        col_allowed,
        "qb",
    )
    column_flat = (sheet_rows, columns_each, half_width)
    col_pieces = [piece.reshape(column_flat).astype(jnp.bfloat16) for piece in col_results]
    out_col, dq_col, dk_col, dv_col = (
        lax.all_to_all(col_pieces[0], "rows", split_axis=0, concat_axis=1, tiled=True),
        lax.all_to_all(col_pieces[1], "rows", split_axis=0, concat_axis=1, tiled=True),
        lax.all_to_all(col_pieces[2], "rows", split_axis=0, concat_axis=1, tiled=True),
        lax.all_to_all(col_pieces[3], "rows", split_axis=0, concat_axis=1, tiled=True),
    )
    lepe = depthwise(padded_value, taps, rows_here, cols_here, False)
    back_conv = depthwise(padded_grad, taps, rows_here, cols_here, True)
    attended16 = jnp.concatenate([out_row, out_col], axis=2)
    out = (attended16.astype(jnp.float32) + lepe).astype(jnp.bfloat16)
    dquery = jnp.concatenate([dq_row, dq_col], axis=2)
    dkey = jnp.concatenate([dk_row, dk_col], axis=2)
    dvalue_attn = jnp.concatenate([dv_row, dv_col], axis=2)
    dvalue = (dvalue_attn.astype(jnp.float32) + back_conv).astype(jnp.bfloat16)
    return (out, dquery, dkey, dvalue)


SUB = 8
VMEM_LIMIT = 28 << 20
MESH = pl.DeviceIdType.MESH


def attend(q, k, v, g, allow):
    scale = 1.0 / math.sqrt(HEAD_DIM)
    nt = (((1,), (1,)), ((), ()))
    nn = (((1,), (0,)), ((), ()))
    tn = (((0,), (0,)), ((), ()))
    dot = functools.partial(lax.dot_general, preferred_element_type=jnp.float32)
    s = jnp.where(allow, dot(q, k, nt) * scale, -jnp.inf)
    e = jnp.exp(s - jnp.max(s, axis=-1, keepdims=True))
    w = e * (1.0 / jnp.sum(e, axis=-1, keepdims=True))
    w16 = w.astype(jnp.bfloat16)
    att = dot(w16, v, nn)
    dw = dot(g, v, nt)
    delta = jnp.sum(g.astype(jnp.float32) * att, axis=-1, keepdims=True)
    ds = (w * (dw - delta) * scale).astype(jnp.bfloat16)
    return att, dot(ds, k, nn), dot(ds, q, tn), dot(w16, g, tn)


def dots():
    dot = functools.partial(lax.dot_general, preferred_element_type=jnp.float32)
    return (
        functools.partial(dot, dimension_numbers=(((1,), (1,)), ((), ()))),
        functools.partial(dot, dimension_numbers=(((1,), (0,)), ((), ()))),
        functools.partial(dot, dimension_numbers=(((0,), (0,)), ((), ()))),
    )


def softmax(q, k, allow):
    nt, _, _ = dots()
    s = jnp.where(allow, nt(q, k) * (1.0 / math.sqrt(HEAD_DIM)), -jnp.inf)
    e = jnp.exp(s - jnp.max(s, axis=-1, keepdims=True))
    return e * (1.0 / jnp.sum(e, axis=-1, keepdims=True))


def layer_kernel(dims, q_hbm, k_hbm, v_hbm, g_hbm, taps_hbm, row_hbm, col_hbm, ret, *rest):
    R, C, rows, groups, width = dims
    colbuf, colout, rowbuf, rowout, ext, conv, hop, land, weights, attended = rest[:10]
    sent, came, here_in, ends_in, lines_in, taps, row_mask, col_mask = rest[10:]
    half = width // 2
    share = half // C
    heads = half // HEAD_DIM
    me = lax.axis_index("rows")
    mc = lax.axis_index("cols")
    inputs = (q_hbm, k_hbm, v_hbm, g_hbm)
    f32 = jnp.float32
    first, second = pl.ds(0, half), pl.ds(half, half)

    def lanes(start, size):
        return pl.ds(pl.multiple_of(start, 128), size)

    def send(src, dst, send_sem, recv_sem, target):
        return pltpu.make_async_remote_copy(
            src_ref=src, dst_ref=dst, send_sem=send_sem, recv_sem=recv_sem,
            device_id=target, device_id_type=MESH)

    col_sent, back_sent, row_sent, row_back_sent, near_sent, cross_sent, far_sent, pass_sent, pass_far_sent, border_sent, right_sent, left_sent = (
        sent.at[i] for i in range(12))
    col_came = [came.at[t] for t in range(4)]
    back_came = [came.at[4], came.at[5], came.at[5], came.at[6]]
    row_came, hop_came, hop_far_came, near_came, cross_came, right_came, left_came = (came.at[7 + i] for i in range(7))

    def drain(semaphore, ref):
        pltpu.make_async_copy(ref, ref, semaphore).wait()

    def home(t):
        return land.at[t // 3] if t in (0, 3) else ret.at[t]

    def col_in(t, p, slot):
        return send(inputs[t].at[:, p, :, second], colbuf.at[t, slot],
                    col_sent, col_came[t], {"rows": p})

    def col_back(t, p, slot):
        if t == 1:
            pair = pl.ds(1, 2)
            src, dst = colout.at[pair, p], ret.at[pair, :, slot, :, second]
        else:
            src, dst = colout.at[t, p], land.at[t // 3, :, slot, :, second]
        return send(src, dst, back_sent, back_came[t], {"rows": p})

    def row_in(t, p, slot):
        return send(inputs[t].at[:, :, :, lanes(p * share, share)], rowbuf.at[t, :, slot],
                    row_sent, row_came, {"cols": p})

    def row_back(t, p, slot):
        return send(rowout.at[t, :, p], home(t).at[:, :, :, lanes(slot * share, share)],
                    row_back_sent, back_came[t], {"cols": p})

    odd = lax.rem(me, 2)
    sign = 2 * odd - 1
    crosses = jnp.logical_and(me + sign >= 0, me + sign < R)
    relays = jnp.logical_and(me - 2 * sign >= 0, me - 2 * sign < R)
    inner = pl.ds(1, groups)
    even_slot, odd_slot = (1 - odd) * (rows + 1), odd * (rows + 1)
    mid = R // 2
    side = me // mid
    gate = mid - 1 + side
    at_gate = me == gate
    beside_gate = me - sign == gate
    direct = 3 * half // 4
    extra = half - direct
    owned = pl.ds(side * mid, mid)
    away = jnp.logical_not(at_gate)
    has_right, has_left = mc < C - 1, mc > 0

    def cross(t):
        return send(inputs[2 + t].at[odd * (rows - 1), :, :, pl.ds(0, direct)],
                    ext.at[t, even_slot, inner, :, pl.ds(0, direct)], cross_sent, cross_came, {"rows": me + sign})

    def detour(t):
        return send(inputs[2 + t].at[odd * (rows - 1), :, :, pl.ds(direct, extra)],
                    hop.at[t, :, :, pl.ds(0, extra)], cross_sent, hop_came, {"rows": me - sign})

    def detour_far(t, span):
        return send(inputs[2 + t].at[odd * (rows - 1), span, :, second],
                    hop.at[t, span, :, pl.ds(extra, half)], far_sent, hop_far_came, {"rows": me - sign})

    def forward():
        return send(hop.at[:, :, :, pl.ds(0, extra)], ext.at[:, odd_slot, inner, :, pl.ds(direct, extra)],
                    pass_sent, cross_came, {"rows": me - 2 * sign})

    def forward_far(span):
        return send(hop.at[:, span, :, pl.ds(extra, half)], ext.at[:, odd_slot, inner].at[:, span, :, second],
                    pass_far_sent, cross_came, {"rows": me - 2 * sign})

    def near(t):
        return send(inputs[2 + t].at[(1 - odd) * (rows - 1)], ext.at[t, odd_slot, inner],
                    near_sent, near_came, {"rows": me - sign})

    def rightward(t):
        return send(inputs[2 + t].at[:, groups - 1], ext.at[t, pl.ds(1, rows), 0],
                    right_sent, right_came, {"cols": mc + 1})

    def leftward(t):
        return send(inputs[2 + t].at[:, 0], ext.at[t, pl.ds(1, rows), groups + 1],
                    left_sent, left_came, {"cols": mc - 1})

    def corner_right(r):
        return send(ext.at[:, r, groups], ext.at[:, r, 0], right_sent, right_came, {"cols": mc + 1})

    def corner_left(r):
        return send(ext.at[:, r, 1], ext.at[:, r, groups + 1], left_sent, left_came, {"cols": mc - 1})

    border_from = colbuf.at[pl.ds(2, 2), mid - side, side * (rows - 1)]
    border_to = ext.at[:, (1 - side) * (rows + 1), 1 + me, :, second]

    def border():
        return send(border_from, border_to, border_sent, cross_came, {"rows": gate})

    def by_gate(gone, act):
        pl.when(gone)(functools.partial(act, owned))
        pl.when(jnp.logical_not(gone))(functools.partial(act, pl.ds(0, groups)))

    def others_on(here, count, act, spread=False):
        def step(n, carry):
            d = n + 1
            if spread:
                d = count // 2 + jnp.where(lax.rem(n, 2) == 0, d // 2, -(d // 2))
            act(lax.rem(here + d, count))
            return carry

        lax.fori_loop(0, count - 1, step, 0)

    each_row = functools.partial(others_on, me, R)
    each_col = functools.partial(others_on, mc, C)

    quarter = R // 4
    in_mid = jnp.logical_and(me >= quarter, me < R - quarter)
    far_mid = mid - side * quarter
    near_mid = quarter + side * quarter
    far_end, near_end = (1 - side) * (R - quarter), side * (R - quarter)
    barrier = pltpu.get_barrier_semaphore()

    def group(bases, act):
        def step(n, carry):
            base = bases[-1]
            for i in range(len(bases) - 1, 0, -1):
                base = jnp.where(n < i * quarter, bases[i - 1], base)
            p = base + lax.rem(n, quarter)
            pl.when(p != me)(lambda: act(p))
            return carry

        lax.fori_loop(0, len(bases) * quarter, step, 0)

    def tell(semaphore, target):
        pl.semaphore_signal(semaphore, inc=1, device_id=target, device_id_type=MESH)

    @pl.when(in_mid)
    def _():
        each_row(lambda p: tell(barrier, {"rows": p}))
        pl.semaphore_wait(barrier, mid - 1)

    @pl.when(jnp.logical_not(in_mid))
    def _():
        group((far_end, near_end), lambda p: tell(barrier, {"rows": p}))
        each_col(lambda p: tell(barrier, {"cols": p}))
        pl.semaphore_wait(barrier, R - 1 + C - 1)
        each_col(lambda p: tell(lines_in, {"cols": p}))

    def send_cols(kinds, bases):
        for t in kinds:
            group(bases, lambda p: col_in(t, p, me).start())

    send_cols((0, 1), (far_mid, near_mid))

    @pl.when(jnp.logical_not(in_mid))
    def _():
        pl.semaphore_wait(lines_in, C - 1)
        group((far_mid, near_mid), lambda p: tell(ends_in, {"rows": p}))

    @pl.when(in_mid)
    def _():
        pl.semaphore_wait(ends_in, 2 * quarter)

    send_cols((0, 1), (far_end, near_end))
    send_cols((2, 3), (far_mid, far_end, near_mid, near_end))

    def send_halo():
        @pl.when(crosses)
        def _():
            for t in range(2):
                detour(t).start()
                by_gate(at_gate, lambda span: detour_far(t, span).start())
                cross(t).start()

        for t in range(2):
            near(t).start()

    def send_sides():
        @pl.when(has_right)
        def _():
            for t in range(2):
                rightward(t).start()

        @pl.when(has_left)
        def _():
            for t in range(2):
                leftward(t).start()

    def pass_halo():
        @pl.when(relays)
        def _():
            drain(hop_came, hop.at[:, :, :, pl.ds(0, extra)])
            forward().start()

            def act(span):
                drain(hop_far_came, hop.at[:, span, :, pl.ds(extra, half)])
                forward_far(span).start()

            by_gate(beside_gate, act)

    def send_rows(t):
        each_col(lambda p: row_in(t, p, mc).start(), spread=True)

    for t in range(4):
        send_rows(t)
    send_halo()
    send_sides()

    tables = [
        pltpu.make_async_copy(src, dst, here_in.at[i])
        for i, (src, dst) in enumerate(((taps_hbm, taps), (row_hbm, row_mask), (col_hbm, col_mask)))
    ]
    for c in tables:
        c.start()
    for t in range(4):
        pltpu.make_async_copy(inputs[t].at[:, :, :, lanes(mc * share, share)], rowbuf.at[t, :, mc], row_came).start()
        pltpu.make_async_copy(inputs[t].at[:, me, :, second], colbuf.at[t, me], col_came[t]).start()
    for t in range(2):
        pltpu.make_async_copy(inputs[2 + t], ext.at[t, pl.ds(1, rows), inner], here_in.at[3]).start()
    for edge, area in (
        (me == 0, (slice(None), 0, inner)),
        (me == R - 1, (slice(None), rows + 1, inner)),
        (mc == 0, (slice(None), slice(None), 0)),
        (mc == C - 1, (slice(None), slice(None), groups + 1)),
    ):
        @pl.when(edge)
        def _(area=area):
            for t in range(2):
                view = ext.at[(t,) + area[1:]]
                view[...] = jnp.zeros(view.shape, view.dtype)
    for c in tables:
        c.wait()

    length = R * rows * SUB
    col_size = length // COL_BLOCKS
    key_pos = lax.broadcasted_iota(jnp.int32, (SUB, length), 1)
    lane_col = lax.broadcasted_iota(jnp.int32, (SUB, length), 0)
    block = jnp.where(lax.rem(key_pos, SUB) == lane_col, key_pos // col_size, -1)
    col_tables = []
    for b in range(COL_BLOCKS):
        table = jnp.zeros((SUB, length), jnp.int32)
        for c in range(SUB):
            for j in range(COL_BLOCKS):
                here = jnp.logical_and(lane_col == c, block == j)
                table = jnp.where(here, col_mask[b, j, me * SUB + c], table)
        col_tables.append(table)

    pass_halo()

    drain(row_came, rowbuf)
    tokens = C * groups * SUB

    def row_step(n, carry):
        i, h = n // (share // HEAD_DIM), lax.rem(n, share // HEAD_DIM)
        cols = lanes(h * HEAD_DIM, HEAD_DIM)
        x = [rowbuf[t, i, :, :, :, cols].astype(f32).reshape(tokens, HEAD_DIM).astype(jnp.bfloat16) for t in range(4)]
        size = tokens // SHEET_ROW_BLOCKS
        place = lax.broadcasted_iota(jnp.int32, (SUB, tokens), 1) // size
        bands = []
        for b in range(SHEET_ROW_BLOCKS):
            table = jnp.zeros((SUB, tokens), jnp.int32)
            for j in range(SHEET_ROW_BLOCKS):
                table = jnp.where(place == j, row_mask[b, j, i], table)
            bands.append(jnp.broadcast_to(table[None], (size // SUB, SUB, tokens)).reshape(size, tokens))
        allow = jnp.concatenate(bands, axis=0) > 0
        for t, y in enumerate(attend(*x, allow)):
            rowout[t, i, :, :, :, cols] = y.reshape(C, groups, SUB, HEAD_DIM).astype(jnp.bfloat16)
        return carry

    lax.fori_loop(0, rows * (share // HEAD_DIM), row_step, 0)
    for t in (0, 3, 1, 2):
        each_col(lambda p: row_back(t, p, mc).start(), spread=True)
        pltpu.make_async_copy(rowout.at[t, :, mc], home(t).at[:, :, :, lanes(mc * share, share)], back_came[t]).start()

    nt, nn, tn = dots()

    def arrived(t):
        drain(col_came[t], colbuf.at[t])

    def give_back(t):
        each_row(lambda p: col_back(t, p, me).start(), spread=True)
        for u in (1, 2) if t == 1 else (t,):
            pltpu.make_async_copy(colout.at[u, me], home(u).at[:, me, :, second], back_came[u]).start()

    def column(t, h):
        return colbuf[t, :, :, :, lanes(h * HEAD_DIM, HEAD_DIM)].astype(f32).reshape(length, HEAD_DIM).astype(jnp.bfloat16)

    def give(t, h, y):
        colout[t, :, :, :, lanes(h * HEAD_DIM, HEAD_DIM)] = y.reshape(R, rows, SUB, HEAD_DIM).astype(jnp.bfloat16)

    def weigh(h, carry):
        allow = jnp.concatenate(
            [jnp.broadcast_to(t[None], (col_size // SUB, SUB, length)).reshape(col_size, length) for t in col_tables], axis=0) > 0
        weights[h] = softmax(column(0, h), column(1, h), allow)
        return carry

    def forward_step(h, carry):
        att = nn(weights[h].astype(jnp.bfloat16), column(2, h))
        attended[h] = att
        give(0, h, att)
        return carry

    def value_step(h, carry):
        give(3, h, tn(weights[h].astype(jnp.bfloat16), column(3, h)))
        return carry

    def score_step(h, carry):
        g = column(3, h)
        delta = jnp.sum(g.astype(f32) * attended[h], axis=-1, keepdims=True)
        ds = (weights[h] * (nt(g, column(2, h)) - delta) * (1.0 / math.sqrt(HEAD_DIM))).astype(jnp.bfloat16)
        give(1, h, nn(ds, column(1, h)))
        give(2, h, tn(ds, column(0, h)))
        return carry

    arrived(0)
    arrived(1)
    lax.fori_loop(0, heads, weigh, 0)
    arrived(2)
    lax.fori_loop(0, heads, forward_step, 0)
    give_back(0)
    arrived(3)

    @pl.when(away)
    def _():
        border().start()

    @pl.when(at_gate)
    def _():
        pltpu.make_async_copy(border_from, border_to, cross_came).start()

    lax.fori_loop(0, heads, value_step, 0)
    give_back(3)

    drain(near_came, ext.at[:, even_slot, inner])

    @pl.when(crosses)
    def _():
        drain(cross_came, ext.at[:, odd_slot, inner])

    for r in (0, rows + 1):
        @pl.when(has_right)
        def _(r=r):
            corner_right(r).start()

        @pl.when(has_left)
        def _(r=r):
            corner_left(r).start()

    lax.fori_loop(0, heads, score_step, 0)
    give_back(1)

    @pl.when(has_left)
    def _():
        drain(right_came, ext.at[:, :, 0])

    @pl.when(has_right)
    def _():
        drain(left_came, ext.at[:, :, groups + 1])

    drain(here_in.at[3], ext.at[:, pl.ds(1, rows), inner])
    long = groups * SUB

    def conv_step(n, carry):
        cols = lanes(n * 128, 128)
        taps_here = taps[:, cols].astype(f32)
        for t in range(2):
            sums = [None] * rows
            for r in range(rows + 2):
                line = ext[t, r, :, :, cols].astype(f32).reshape(long + 2 * SUB, 128)
                for b in range(3):
                    seen = line[SUB + b - 1 : SUB + b - 1 + long]
                    for a in range(3):
                        o = r - a
                        if 0 <= o < rows:
                            tap = 3 * a + b if t == 0 else 8 - 3 * a - b
                            term = taps_here[tap : tap + 1] * seen
                            sums[o] = term if sums[o] is None else sums[o] + term
            for o in range(rows):
                conv[t, o, :, :, cols] = sums[o].reshape(groups, SUB, 128)
        return carry

    lax.fori_loop(0, width // 128, conv_step, 0)

    drain(col_sent, colbuf.at[:, pl.ds(0, R - 1)])
    for semaphore in (row_sent, row_back_sent):
        drain(semaphore, rowbuf.at[:, :, pl.ds(0, C - 1)])
    drain(near_sent, ext.at[:, 0, inner])

    @pl.when(crosses)
    def _():
        drain(cross_sent, ext.at[:, 0, inner, :, first])
        by_gate(at_gate, lambda span: drain(far_sent, ext.at[:, 0, inner].at[:, span, :, second]))

    @pl.when(relays)
    def _():
        drain(pass_sent, hop.at[:, :, :, pl.ds(0, extra)])
        by_gate(beside_gate, lambda span: drain(pass_far_sent, hop.at[:, span, :, pl.ds(extra, half)]))

    @pl.when(away)
    def _():
        drain(border_sent, border_from)

    @pl.when(has_right)
    def _():
        drain(right_sent, ext.at[:, :, 0])

    @pl.when(has_left)
    def _():
        drain(left_sent, ext.at[:, :, 0])

    stored = []
    for t in range(2):
        drain(back_came[3 * t], land.at[t])

        def add_step(n, carry):
            cols = lanes(n * 128, 128)
            land[t, :, :, :, cols] = (land[t, :, :, :, cols].astype(f32) + conv[t, :, :, :, cols]).astype(jnp.bfloat16)
            return carry

        lax.fori_loop(0, width // 128, add_step, 0)
        stored.append(pltpu.make_async_copy(land.at[t], ret.at[3 * t], here_in.at[4 + t]))
        stored[t].start()
    drain(back_sent, colbuf.at[:, pl.ds(0, R - 1)])
    drain(back_came[1], ret.at[pl.ds(1, 2)])
    for c in stored:
        c.wait()


def finish_kernel(ret, *rest):
    copies = [pltpu.make_async_copy(ret.at[t], rest[t], rest[4].at[t]) for t in range(4)]
    for c in copies:
        c.start()
    for c in copies:
        c.wait()


def fused_body(query, key, value, cotangent, conv_weight, row_mask, col_mask):
    rows, cols_here, width = query.shape
    R, C = lax.axis_size("rows"), lax.axis_size("cols")
    groups = cols_here // SUB
    half = width // 2
    share = half // C
    views = [x.reshape(rows, groups, SUB, width) for x in (query, key, value, cotangent)]
    bf16 = jnp.bfloat16
    any_spec = pl.BlockSpec(memory_space=pl.ANY)
    dma = pltpu.SemaphoreType.DMA
    heads = half // HEAD_DIM
    length = R * rows * SUB
    row_table, col_table = jnp.transpose(row_mask, (1, 2, 0)), jnp.transpose(col_mask, (1, 2, 0))
    ret = pl.pallas_call(
        functools.partial(layer_kernel, (R, C, rows, groups, width)),
        out_shape=jax.ShapeDtypeStruct((4, rows, groups, SUB, width), bf16),
        in_specs=[any_spec] * 7,
        out_specs=any_spec,
        scratch_shapes=[
            pltpu.VMEM((4, R, rows, SUB, half), bf16),
            pltpu.VMEM((4, R, rows, SUB, half), bf16),
            pltpu.VMEM((4, rows, C, groups, SUB, share), bf16),
            pltpu.VMEM((4, rows, C, groups, SUB, share), bf16),
            pltpu.VMEM((2, rows + 2, groups + 2, SUB, width), bf16),
            pltpu.VMEM((2, rows, groups, SUB, width), jnp.float32),
            pltpu.VMEM((2, groups, SUB, half + half // 4), bf16),
            pltpu.VMEM((2, rows, groups, SUB, width), bf16),
            pltpu.VMEM((heads, length, length), jnp.float32),
            pltpu.VMEM((heads, length, HEAD_DIM), jnp.float32),
            dma((12,)), dma((14,)), dma((6,)), pltpu.SemaphoreType.REGULAR, pltpu.SemaphoreType.REGULAR,
            pltpu.VMEM(conv_weight.shape, bf16), pltpu.SMEM(row_table.shape, jnp.int32), pltpu.SMEM(col_table.shape, jnp.int32),
        ],
        compiler_params=pltpu.CompilerParams(collective_id=0, has_side_effects=True, vmem_limit_bytes=VMEM_LIMIT),
    )(*[pltpu.with_memory_space_constraint(x, pltpu.HBM) for x in (*views, conv_weight, row_table, col_table)])
    outs = pl.pallas_call(
        finish_kernel,
        out_shape=[jax.ShapeDtypeStruct((rows, groups, SUB, width), bf16)] * 4,
        in_specs=[any_spec],
        out_specs=[any_spec] * 4,
        scratch_shapes=[dma((4,))],
        compiler_params=pltpu.CompilerParams(vmem_limit_bytes=1 << 20),
    )(ret)
    return tuple(x.reshape(query.shape) for x in outs)


def any_body(query, key, value, cotangent, conv_weight, row_mask, col_mask):
    rows, cols_here, width = query.shape
    R, C = lax.axis_size("rows"), lax.axis_size("cols")
    fits = R % 4 == 0 and cols_here == R * SUB and (width // 2) % (C * HEAD_DIM) == 0 and (width // 2) % (4 * HEAD_DIM) == 0
    chosen = fused_body if fits else body
    return chosen(query, key, value, cotangent, conv_weight, row_mask, col_mask)


def solution(mesh):
    return jax.shard_map(
        any_body,
        mesh=mesh,
        in_specs=(
            P("rows", "cols", None),
            P("rows", "cols", None),
            P("rows", "cols", None),
            P("rows", "cols", None),
            P(),
            P("rows", None, None),
            P("cols", None, None),
        ),
        out_specs=(
            P("rows", "cols", None),
            P("rows", "cols", None),
            P("rows", "cols", None),
            P("rows", "cols", None),
        ),
        check_vma=False,
    )
```

```python
import functools
import math

import jax
import jax.numpy as jnp
from jax import lax
from jax.experimental import pallas as pl
from jax.experimental.pallas import tpu as pltpu
from jax.sharding import PartitionSpec as P

HEAD_DIM = 128
SHEET_ROW_BLOCKS = 2
COL_BLOCKS = 3


def padded(array, sides, width):
    for axis, dim in sides:
        devices, length = (lax.axis_size(axis), array.shape[dim])
        up = [(i, (i + 1) % devices) for i in range(devices - 1)]
        down = [(j, i) for i, j in up]
        last = lax.slice_in_dim(array, length - width, length, axis=dim)
        leading = lax.slice_in_dim(array, 0, width, axis=dim)
        before = lax.ppermute(last, axis, up)
        after = lax.ppermute(leading, axis, down)
        array = jnp.concatenate([before, array, after], axis=dim)
    return array


def block_allow(block_mask_table, query_pos, key_pos, block_len, block_count):
    labels = jnp.arange(block_count)
    query_onehot_rows = (query_pos[:, None] // block_len == labels[None, :]).astype(jnp.float32)
    key_onehot_rows = (key_pos[:, None] // block_len == labels[None, :]).astype(jnp.float32)
    merged_links = jnp.einsum(
        "xv,zvs,hs->zxh", query_onehot_rows, block_mask_table.astype(jnp.float32), key_onehot_rows
    )
    return merged_links > 0.5


def line_attention(query_part, key_part, value_part, grad_part, allowed, layout):
    if layout == "bq":
        query_form = "bqhd"
        key_layout_shape = "bkhd"
    else:
        query_form = "qbhd"
        key_layout_shape = "kbhd"
    score_scale = 1.0 / math.sqrt(query_part.shape[-1])
    pair_form = query_form + "," + key_layout_shape + "->bhqk"
    scores = (
        jnp.einsum(pair_form, query_part, key_part, preferred_element_type=jnp.float32)
        * score_scale
    )
    scores = jnp.where(allowed[:, None], scores, -jnp.inf)
    highest = jnp.max(scores, axis=-1, keepdims=True)
    weights = jnp.exp(scores - highest)
    weights = weights / jnp.sum(weights, axis=-1, keepdims=True)
    rounded = weights.astype(jnp.bfloat16)
    attended = jnp.einsum(
        "bhqk," + key_layout_shape + "->" + query_form,
        rounded,
        value_part,
        preferred_element_type=jnp.float32,
    )
    dweights = jnp.einsum(pair_form, grad_part, value_part, preferred_element_type=jnp.float32)
    delta = jnp.sum(grad_part.astype(jnp.float32) * attended, axis=-1)
    if layout == "bq":
        delta = jnp.transpose(delta, (0, 2, 1))
    else:
        delta = jnp.transpose(delta, (1, 2, 0))
    dscores = (weights * (dweights - delta[..., None]) * score_scale).astype(jnp.bfloat16)
    dquery = jnp.einsum(
        "bhqk," + key_layout_shape + "->" + query_form,
        dscores,
        key_part,
        preferred_element_type=jnp.float32,
    )
    dkey = jnp.einsum(
        "bhqk," + query_form + "->" + key_layout_shape,
        dscores,
        query_part,
        preferred_element_type=jnp.float32,
    )
    dvalue = jnp.einsum(
        "bhqk," + query_form + "->" + key_layout_shape,
        rounded,
        grad_part,
        preferred_element_type=jnp.float32,
    )
    return (attended, dquery, dkey, dvalue)


def depthwise(padded_field, taps, rows_count, cols_count, reverse_taps):
    summed = jnp.zeros((rows_count, cols_count, taps.shape[1]), jnp.float32)
    for row_offset_start in range(3):
        for offset_col in range(3):
            if reverse_taps:
                start_row = 2 - row_offset_start
                start_col = 2 - offset_col
            else:
                start_row = row_offset_start
                start_col = offset_col
            window = padded_field[
                start_row : start_row + rows_count, start_col : start_col + cols_count
            ]
            summed = summed + taps[row_offset_start * 3 + offset_col] * window.astype(jnp.float32)
    return summed


def body(query, key, value, cotangent, conv_weight, row_mask, col_mask):
    rows_here, cols_here, width = query.shape
    half_width = width // 2
    head_groups = half_width // HEAD_DIM
    row_devices = lax.axis_size("rows")
    col_devices = lax.axis_size("cols")
    sheet_rows = rows_here * row_devices
    sheet_cols = cols_here * col_devices
    taps = conv_weight.astype(jnp.float32)
    padded_value = padded(value, (("rows", 0), ("cols", 1)), 1)
    padded_grad = padded(cotangent, (("rows", 0), ("cols", 1)), 1)
    row_len = sheet_cols // SHEET_ROW_BLOCKS
    keys_row, values_row = (
        lax.all_gather(key[:, :, :half_width], "cols", axis=1, tiled=True),
        lax.all_gather(value[:, :, :half_width], "cols", axis=1, tiled=True),
    )
    col_start = lax.axis_index("cols") * cols_here
    allowed = block_allow(
        row_mask,
        col_start + jnp.arange(cols_here),
        jnp.arange(sheet_cols),
        row_len,
        SHEET_ROW_BLOCKS,
    )
    local_shape = (rows_here, cols_here, head_groups, HEAD_DIM)
    whole_shape = (rows_here, sheet_cols, head_groups, HEAD_DIM)
    results = line_attention(
        query[:, :, :half_width].reshape(local_shape),
        keys_row.reshape(whole_shape),
        values_row.reshape(whole_shape),
        cotangent[:, :, :half_width].reshape(local_shape),
        allowed,
        "bq",
    )
    key_terms = results[2].reshape(rows_here, sheet_cols, half_width)
    value_terms = results[3].reshape(rows_here, sheet_cols, half_width)
    key_grads, value_grads = (
        lax.psum_scatter(key_terms, "cols", scatter_dimension=1, tiled=True),
        lax.psum_scatter(value_terms, "cols", scatter_dimension=1, tiled=True),
    )
    out_row = results[0].reshape(rows_here, cols_here, half_width).astype(jnp.bfloat16)
    dq_row = results[1].reshape(rows_here, cols_here, half_width).astype(jnp.bfloat16)
    dk_row = key_grads.astype(jnp.bfloat16)
    dv_row = value_grads.astype(jnp.bfloat16)
    columns_each = cols_here // row_devices
    moved = (
        lax.all_to_all(query[:, :, half_width:], "rows", split_axis=1, concat_axis=0, tiled=True),
        lax.all_to_all(key[:, :, half_width:], "rows", split_axis=1, concat_axis=0, tiled=True),
        lax.all_to_all(value[:, :, half_width:], "rows", split_axis=1, concat_axis=0, tiled=True),
        lax.all_to_all(
            cotangent[:, :, half_width:], "rows", split_axis=1, concat_axis=0, tiled=True
        ),
    )
    column_shape = (sheet_rows, columns_each, head_groups, HEAD_DIM)
    my_tables = lax.dynamic_slice_in_dim(
        col_mask, lax.axis_index("rows") * columns_each, columns_each, 0
    )
    col_len = sheet_rows // COL_BLOCKS
    positions = jnp.arange(sheet_rows)
    col_allowed = block_allow(my_tables, positions, positions, col_len, COL_BLOCKS)
    col_results = line_attention(
        moved[0].reshape(column_shape),
        moved[1].reshape(column_shape),
        moved[2].reshape(column_shape),
        moved[3].reshape(column_shape),
        col_allowed,
        "qb",
    )
    column_flat = (sheet_rows, columns_each, half_width)
    col_pieces = [piece.reshape(column_flat).astype(jnp.bfloat16) for piece in col_results]
    out_col, dq_col, dk_col, dv_col = (
        lax.all_to_all(col_pieces[0], "rows", split_axis=0, concat_axis=1, tiled=True),
        lax.all_to_all(col_pieces[1], "rows", split_axis=0, concat_axis=1, tiled=True),
        lax.all_to_all(col_pieces[2], "rows", split_axis=0, concat_axis=1, tiled=True),
        lax.all_to_all(col_pieces[3], "rows", split_axis=0, concat_axis=1, tiled=True),
    )
    lepe = depthwise(padded_value, taps, rows_here, cols_here, False)
    back_conv = depthwise(padded_grad, taps, rows_here, cols_here, True)
    attended16 = jnp.concatenate([out_row, out_col], axis=2)
    out = (attended16.astype(jnp.float32) + lepe).astype(jnp.bfloat16)
    dquery = jnp.concatenate([dq_row, dq_col], axis=2)
    dkey = jnp.concatenate([dk_row, dk_col], axis=2)
    dvalue_attn = jnp.concatenate([dv_row, dv_col], axis=2)
    dvalue = (dvalue_attn.astype(jnp.float32) + back_conv).astype(jnp.bfloat16)
    return (out, dquery, dkey, dvalue)


SUB = 8
VMEM_LIMIT = 28 << 20
MESH = pl.DeviceIdType.MESH


def attend(q, k, v, g, allow):
    scale = 1.0 / math.sqrt(HEAD_DIM)
    nt = (((1,), (1,)), ((), ()))
    nn = (((1,), (0,)), ((), ()))
    tn = (((0,), (0,)), ((), ()))
    dot = functools.partial(lax.dot_general, preferred_element_type=jnp.float32)
    s = jnp.where(allow, dot(q, k, nt) * scale, -jnp.inf)
    e = jnp.exp(s - jnp.max(s, axis=-1, keepdims=True))
    w = e * (1.0 / jnp.sum(e, axis=-1, keepdims=True))
    w16 = w.astype(jnp.bfloat16)
    att = dot(w16, v, nn)
    dw = dot(g, v, nt)
    delta = jnp.sum(g.astype(jnp.float32) * att, axis=-1, keepdims=True)
    ds = (w * (dw - delta) * scale).astype(jnp.bfloat16)
    return att, dot(ds, k, nn), dot(ds, q, tn), dot(w16, g, tn)


def dots():
    dot = functools.partial(lax.dot_general, preferred_element_type=jnp.float32)
    return (
        functools.partial(dot, dimension_numbers=(((1,), (1,)), ((), ()))),
        functools.partial(dot, dimension_numbers=(((1,), (0,)), ((), ()))),
        functools.partial(dot, dimension_numbers=(((0,), (0,)), ((), ()))),
    )


def softmax(q, k, allow):
    nt, _, _ = dots()
    s = jnp.where(allow, nt(q, k) * (1.0 / math.sqrt(HEAD_DIM)), -jnp.inf)
    e = jnp.exp(s - jnp.max(s, axis=-1, keepdims=True))
    return e * (1.0 / jnp.sum(e, axis=-1, keepdims=True))


def layer_kernel(dims, q_hbm, k_hbm, v_hbm, g_hbm, taps_hbm, row_hbm, col_hbm, ret, *rest):
    R, C, rows, groups, width = dims
    colbuf, colout, rowbuf, rowout, ext, conv, hop, land, weights, attended, spill, spilled = rest[:12]
    sent, came, here_in, ends_in, lines_in, taps, row_mask, col_mask = rest[12:]
    half = width // 2
    share = half // C
    heads = half // HEAD_DIM
    me = lax.axis_index("rows")
    mc = lax.axis_index("cols")
    inputs = (q_hbm, k_hbm, v_hbm, g_hbm)
    f32 = jnp.float32
    first, second = pl.ds(0, half), pl.ds(half, half)

    def lanes(start, size):
        return pl.ds(pl.multiple_of(start, 128), size)

    def send(src, dst, send_sem, recv_sem, target):
        return pltpu.make_async_remote_copy(
            src_ref=src, dst_ref=dst, send_sem=send_sem, recv_sem=recv_sem,
            device_id=target, device_id_type=MESH)

    col_sent, back_sent, row_sent, row_back_sent, near_sent, cross_sent, far_sent, pass_sent, pass_far_sent, border_sent, right_sent, left_sent, spill_sent = (
        sent.at[i] for i in range(13))
    col_came = [came.at[t] for t in range(4)]
    back_came = [came.at[4], came.at[5], came.at[5], came.at[6]]
    row_came, hop_came, hop_far_came, near_came, cross_came, right_came, left_came, spill_came = (came.at[7 + i] for i in range(8))

    def drain(semaphore, ref):
        pltpu.make_async_copy(ref, ref, semaphore).wait()

    def home(t):
        return land.at[t // 3] if t in (0, 3) else ret.at[t]

    def col_in(t, p, slot):
        return send(inputs[t].at[:, p, :, second], colbuf.at[t, slot],
                    col_sent, col_came[t], {"rows": p})

    def col_back(t, p, slot):
        if t == 1:
            pair = pl.ds(1, 2)
            src, dst = colout.at[pair, p], ret.at[pair, :, slot, :, second]
        else:
            src, dst = colout.at[t, p], land.at[t // 3, :, slot, :, second]
        return send(src, dst, back_sent, back_came[t], {"rows": p})

    def row_in(t, p, slot):
        return send(inputs[t].at[:, :, :, lanes(p * share, share)], rowbuf.at[t, :, slot],
                    row_sent, row_came, {"cols": p})

    def row_back(t, p, slot):
        return send(rowout.at[t, :, p], home(t).at[:, :, :, lanes(slot * share, share)],
                    row_back_sent, back_came[t], {"cols": p})

    odd = lax.rem(me, 2)
    sign = 2 * odd - 1
    crosses = jnp.logical_and(me + sign >= 0, me + sign < R)
    relays = jnp.logical_and(me - 2 * sign >= 0, me - 2 * sign < R)
    inner = pl.ds(1, groups)
    even_slot, odd_slot = (1 - odd) * (rows + 1), odd * (rows + 1)
    mid = R // 2
    side = me // mid
    gate = mid - 1 + side
    at_gate = me == gate
    beside_gate = me - sign == gate
    direct = 5 * half // 8
    extra = half - direct
    base = side * mid
    away = jnp.logical_not(at_gate)
    has_right, has_left = mc < C - 1, mc > 0

    def cross(t):
        return send(inputs[2 + t].at[odd * (rows - 1), :, :, pl.ds(0, direct)],
                    ext.at[t, even_slot, inner, :, pl.ds(0, direct)], cross_sent, cross_came, {"rows": me + sign})

    def detour(t):
        return send(inputs[2 + t].at[odd * (rows - 1), :, :, pl.ds(direct, extra)],
                    hop.at[t, :, :, pl.ds(0, extra)], cross_sent, hop_came, {"rows": me - sign})

    def detour_far(t, span):
        return send(inputs[2 + t].at[odd * (rows - 1), span, :, second],
                    hop.at[t, span, :, pl.ds(extra, half)], far_sent, hop_far_came, {"rows": me - sign})

    def forward():
        return send(hop.at[:, :, :, pl.ds(0, extra)], ext.at[:, odd_slot, inner, :, pl.ds(direct, extra)],
                    pass_sent, cross_came, {"rows": me - 2 * sign})

    def forward_far(span):
        return send(hop.at[:, span, :, pl.ds(extra, half)], ext.at[:, odd_slot, inner].at[:, span, :, second],
                    pass_far_sent, cross_came, {"rows": me - 2 * sign})

    def near(t):
        return send(inputs[2 + t].at[(1 - odd) * (rows - 1)], ext.at[t, odd_slot, inner],
                    near_sent, near_came, {"rows": me - sign})

    def rightward(t):
        return send(inputs[2 + t].at[:, groups - 1], ext.at[t, pl.ds(1, rows), 0],
                    right_sent, right_came, {"cols": mc + 1})

    def leftward(t):
        return send(inputs[2 + t].at[:, 0], ext.at[t, pl.ds(1, rows), groups + 1],
                    left_sent, left_came, {"cols": mc - 1})

    def corner_right(r):
        return send(ext.at[:, r, groups], ext.at[:, r, 0], right_sent, right_came, {"cols": mc + 1})

    def corner_left(r):
        return send(ext.at[:, r, 1], ext.at[:, r, groups + 1], left_sent, left_came, {"cols": mc - 1})

    border_from = colbuf.at[pl.ds(2, 2), mid - side, side * (rows - 1)]
    border_to = ext.at[:, (1 - side) * (rows + 1), 1 + me, :, second]

    def border():
        return send(border_from, border_to, border_sent, cross_came, {"rows": gate})

    def by_gate(gone, act):
        @pl.when(gone)
        def _():
            act(pl.ds(base, 1))
            act(pl.ds(base + mid - 1, 1))

        pl.when(jnp.logical_not(gone))(lambda: act(pl.ds(0, groups)))

    def drain_far(gone, semaphore):
        pl.when(gone)(lambda: drain(semaphore, hop.at[:, pl.ds(0, 2), :, pl.ds(extra, half)]))
        pl.when(jnp.logical_not(gone))(lambda: drain(semaphore, hop.at[:, :, :, pl.ds(extra, half)]))

    def spill_copy(p):
        return send(spill.at[:, p - base], spilled, spill_sent, spill_came, {"rows": p})

    def others_on(here, count, act, spread=False):
        def step(n, carry):
            d = n + 1
            if spread:
                d = count // 2 + jnp.where(lax.rem(n, 2) == 0, d // 2, -(d // 2))
            act(lax.rem(here + d, count))
            return carry

        lax.fori_loop(0, count - 1, step, 0)

    each_row = functools.partial(others_on, me, R)
    each_col = functools.partial(others_on, mc, C)

    quarter = R // 4
    in_mid = jnp.logical_and(me >= quarter, me < R - quarter)
    far_mid = mid - side * quarter
    near_mid = quarter + side * quarter
    far_end, near_end = (1 - side) * (R - quarter), side * (R - quarter)
    barrier = pltpu.get_barrier_semaphore()

    def group(bases, act):
        def step(n, carry):
            base = bases[-1]
            for i in range(len(bases) - 1, 0, -1):
                base = jnp.where(n < i * quarter, bases[i - 1], base)
            p = base + lax.rem(n, quarter)
            pl.when(p != me)(lambda: act(p))
            return carry

        lax.fori_loop(0, len(bases) * quarter, step, 0)

    def tell(semaphore, target):
        pl.semaphore_signal(semaphore, inc=1, device_id=target, device_id_type=MESH)

    @pl.when(in_mid)
    def _():
        each_row(lambda p: tell(barrier, {"rows": p}))
        pl.semaphore_wait(barrier, mid - 1)

    @pl.when(jnp.logical_not(in_mid))
    def _():
        group((far_end, near_end), lambda p: tell(barrier, {"rows": p}))
        each_col(lambda p: tell(barrier, {"cols": p}))
        pl.semaphore_wait(barrier, R - 1 + C - 1)
        each_col(lambda p: tell(lines_in, {"cols": p}))

    def send_cols(kinds, bases):
        for t in kinds:
            group(bases, lambda p: col_in(t, p, me).start())

    send_cols((0, 1), (far_mid, near_mid))

    @pl.when(jnp.logical_not(in_mid))
    def _():
        pl.semaphore_wait(lines_in, C - 1)
        group((far_mid, near_mid), lambda p: tell(ends_in, {"rows": p}))

    @pl.when(in_mid)
    def _():
        pl.semaphore_wait(ends_in, 2 * quarter)

    send_cols((0, 1), (far_end, near_end))
    send_cols((2, 3), (far_mid, far_end, near_mid, near_end))

    def send_halo():
        @pl.when(crosses)
        def _():
            for t in range(2):
                detour(t).start()
                by_gate(at_gate, lambda span: detour_far(t, span).start())
                cross(t).start()

        for t in range(2):
            near(t).start()

    def send_sides():
        @pl.when(has_right)
        def _():
            for t in range(2):
                rightward(t).start()

        @pl.when(has_left)
        def _():
            for t in range(2):
                leftward(t).start()

    def pass_halo():
        @pl.when(relays)
        def _():
            drain(hop_came, hop.at[:, :, :, pl.ds(0, extra)])
            forward().start()

            drain_far(beside_gate, hop_far_came)
            by_gate(beside_gate, lambda span: forward_far(span).start())

    def send_rows(t):
        each_col(lambda p: row_in(t, p, mc).start(), spread=True)

    for t in range(4):
        send_rows(t)
    send_halo()
    send_sides()

    tables = [
        pltpu.make_async_copy(src, dst, here_in.at[i])
        for i, (src, dst) in enumerate(((taps_hbm, taps), (row_hbm, row_mask), (col_hbm, col_mask)))
    ]
    for c in tables:
        c.start()
    for t in range(4):
        pltpu.make_async_copy(inputs[t].at[:, :, :, lanes(mc * share, share)], rowbuf.at[t, :, mc], row_came).start()
        pltpu.make_async_copy(inputs[t].at[:, me, :, second], colbuf.at[t, me], col_came[t]).start()
    for t in range(2):
        pltpu.make_async_copy(inputs[2 + t], ext.at[t, pl.ds(1, rows), inner], here_in.at[3]).start()
    for edge, area in (
        (me == 0, (slice(None), 0, inner)),
        (me == R - 1, (slice(None), rows + 1, inner)),
        (mc == 0, (slice(None), slice(None), 0)),
        (mc == C - 1, (slice(None), slice(None), groups + 1)),
    ):
        @pl.when(edge)
        def _(area=area):
            for t in range(2):
                view = ext.at[(t,) + area[1:]]
                view[...] = jnp.zeros(view.shape, view.dtype)

    @pl.when(at_gate)
    def _():
        for t in range(2):
            view = ext.at[t, (1 - side) * (rows + 1), pl.ds(1 + mid - base + 1, mid - 2), :, second]
            view[...] = jnp.zeros(view.shape, view.dtype)
    for c in tables:
        c.wait()
    drain(here_in.at[3], ext.at[:, pl.ds(1, rows), inner])

    def spill_step(n, carry):
        cols = lanes(half + n * 128, 128)
        taps_here = taps[:, cols].astype(f32)
        for t in range(2):
            source = ext[t, rows - side * (rows - 1), pl.ds(1 + base + 1, mid - 2), :, cols].astype(f32)
            edge = jnp.zeros((2 * SUB, 128), f32)
            line = jnp.concatenate([edge, source.reshape((mid - 2) * SUB, 128), edge], axis=0)
            total = jnp.zeros((mid * SUB, 128), f32)
            for b in range(3):
                above, below = (b, 6 + b) if t == 0 else (8 - b, 2 - b)
                tap = jnp.where(side == 1, taps_here[below : below + 1], taps_here[above : above + 1])
                total = total + tap * line[SUB + b - 1 : SUB + b - 1 + mid * SUB]
            spill[t, :, :, lanes(n * 128, 128)] = total.reshape(mid, SUB, 128)
        return carry

    @pl.when(at_gate)
    def _():
        lax.fori_loop(0, half // 128, spill_step, 0)
        pltpu.make_async_copy(spill.at[:, me - base], spilled, spill_came).start()
        for j in range(mid):
            @pl.when(base + j != me)
            def _(p=base + j):
                spill_copy(p).start()

    length = R * rows * SUB
    col_size = length // COL_BLOCKS
    key_pos = lax.broadcasted_iota(jnp.int32, (SUB, length), 1)
    lane_col = lax.broadcasted_iota(jnp.int32, (SUB, length), 0)
    block = jnp.where(lax.rem(key_pos, SUB) == lane_col, key_pos // col_size, -1)
    col_tables = []
    for b in range(COL_BLOCKS):
        table = jnp.zeros((SUB, length), jnp.int32)
        for c in range(SUB):
            for j in range(COL_BLOCKS):
                here = jnp.logical_and(lane_col == c, block == j)
                table = jnp.where(here, col_mask[b, j, me * SUB + c], table)
        col_tables.append(table)

    pass_halo()

    drain(row_came, rowbuf)
    tokens = C * groups * SUB

    def row_step(n, carry):
        i, h = n // (share // HEAD_DIM), lax.rem(n, share // HEAD_DIM)
        cols = lanes(h * HEAD_DIM, HEAD_DIM)
        x = [rowbuf[t, i, :, :, :, cols].astype(f32).reshape(tokens, HEAD_DIM).astype(jnp.bfloat16) for t in range(4)]
        size = tokens // SHEET_ROW_BLOCKS
        place = lax.broadcasted_iota(jnp.int32, (SUB, tokens), 1) // size
        bands = []
        for b in range(SHEET_ROW_BLOCKS):
            table = jnp.zeros((SUB, tokens), jnp.int32)
            for j in range(SHEET_ROW_BLOCKS):
                table = jnp.where(place == j, row_mask[b, j, i], table)
            bands.append(jnp.broadcast_to(table[None], (size // SUB, SUB, tokens)).reshape(size, tokens))
        allow = jnp.concatenate(bands, axis=0) > 0
        for t, y in enumerate(attend(*x, allow)):
            rowout[t, i, :, :, :, cols] = y.reshape(C, groups, SUB, HEAD_DIM).astype(jnp.bfloat16)
        return carry

    lax.fori_loop(0, rows * (share // HEAD_DIM), row_step, 0)
    for t in (0, 3, 1, 2):
        each_col(lambda p: row_back(t, p, mc).start(), spread=True)
        pltpu.make_async_copy(rowout.at[t, :, mc], home(t).at[:, :, :, lanes(mc * share, share)], back_came[t]).start()

    nt, nn, tn = dots()

    def arrived(t):
        drain(col_came[t], colbuf.at[t])

    def give_back(t):
        @pl.when(side == 1)
        def _():
            each_row(lambda p: col_back(t, p, me).start(), spread=True)

        @pl.when(side == 0)
        def _():
            def step(n, carry):
                i = n // 2
                p = jnp.where(lax.rem(n, 2) == 0, mid + lax.rem(i + 2, mid), lax.rem(me + i + 1, mid))
                col_back(t, p, me).start()
                return carry

            lax.fori_loop(0, R - 1, step, 0)

        for u in (1, 2) if t == 1 else (t,):
            pltpu.make_async_copy(colout.at[u, me], home(u).at[:, me, :, second], back_came[u]).start()

    def column(t, h):
        return colbuf[t, :, :, :, lanes(h * HEAD_DIM, HEAD_DIM)].astype(f32).reshape(length, HEAD_DIM).astype(jnp.bfloat16)

    def give(t, h, y):
        colout[t, :, :, :, lanes(h * HEAD_DIM, HEAD_DIM)] = y.reshape(R, rows, SUB, HEAD_DIM).astype(jnp.bfloat16)

    def weigh(h, carry):
        allow = jnp.concatenate(
            [jnp.broadcast_to(t[None], (col_size // SUB, SUB, length)).reshape(col_size, length) for t in col_tables], axis=0) > 0
        weights[h] = softmax(column(0, h), column(1, h), allow)
        return carry

    def forward_step(h, carry):
        att = nn(weights[h].astype(jnp.bfloat16), column(2, h))
        attended[h] = att
        give(0, h, att)
        return carry

    def value_step(h, carry):
        give(3, h, tn(weights[h].astype(jnp.bfloat16), column(3, h)))
        return carry

    def score_step(h, carry):
        g = column(3, h)
        delta = jnp.sum(g.astype(f32) * attended[h], axis=-1, keepdims=True)
        ds = (weights[h] * (nt(g, column(2, h)) - delta) * (1.0 / math.sqrt(HEAD_DIM))).astype(jnp.bfloat16)
        give(1, h, nn(ds, column(1, h)))
        give(2, h, tn(ds, column(0, h)))
        return carry

    arrived(0)
    arrived(1)
    lax.fori_loop(0, heads, weigh, 0)
    arrived(2)
    lax.fori_loop(0, heads, forward_step, 0)

    def add_spill(t, u):
        place = colout.at[t, mid - side, side * (rows - 1)]
        place[...] = (place[...].astype(f32) + spilled[u]).astype(jnp.bfloat16)

    drain(spill_came, spilled)
    add_spill(0, 0)
    give_back(0)
    arrived(3)

    @pl.when(away)
    def _():
        border().start()

    @pl.when(at_gate)
    def _():
        pltpu.make_async_copy(border_from, border_to, cross_came).start()

    lax.fori_loop(0, heads, value_step, 0)
    add_spill(3, 1)
    give_back(3)

    drain(near_came, ext.at[:, even_slot, inner])

    @pl.when(crosses)
    def _():
        pl.when(at_gate)(lambda: drain(cross_came, ext.at[:, odd_slot, pl.ds(0, (groups + mid + 2) // 2)]))
        pl.when(away)(lambda: drain(cross_came, ext.at[:, odd_slot, inner]))

    for r in (0, rows + 1):
        @pl.when(has_right)
        def _(r=r):
            corner_right(r).start()

        @pl.when(has_left)
        def _(r=r):
            corner_left(r).start()

    lax.fori_loop(0, heads, score_step, 0)
    give_back(1)

    @pl.when(has_left)
    def _():
        drain(right_came, ext.at[:, :, 0])

    @pl.when(has_right)
    def _():
        drain(left_came, ext.at[:, :, groups + 1])

    long = groups * SUB

    def conv_step(n, carry):
        cols = lanes(n * 128, 128)
        taps_here = taps[:, cols].astype(f32)
        for t in range(2):
            sums = [None] * rows
            for r in range(rows + 2):
                line = ext[t, r, :, :, cols].astype(f32).reshape(long + 2 * SUB, 128)
                for b in range(3):
                    seen = line[SUB + b - 1 : SUB + b - 1 + long]
                    for a in range(3):
                        o = r - a
                        if 0 <= o < rows:
                            tap = 3 * a + b if t == 0 else 8 - 3 * a - b
                            term = taps_here[tap : tap + 1] * seen
                            sums[o] = term if sums[o] is None else sums[o] + term
            for o in range(rows):
                conv[t, o, :, :, cols] = sums[o].reshape(groups, SUB, 128)
        return carry

    lax.fori_loop(0, width // 128, conv_step, 0)

    drain(col_sent, colbuf.at[:, pl.ds(0, R - 1)])
    for semaphore in (row_sent, row_back_sent):
        drain(semaphore, rowbuf.at[:, :, pl.ds(0, C - 1)])
    drain(near_sent, ext.at[:, 0, inner])

    @pl.when(crosses)
    def _():
        drain(cross_sent, ext.at[:, 0, inner, :, first])
        drain_far(at_gate, far_sent)

    @pl.when(relays)
    def _():
        drain(pass_sent, hop.at[:, :, :, pl.ds(0, extra)])
        drain_far(beside_gate, pass_far_sent)

    @pl.when(away)
    def _():
        drain(border_sent, border_from)

    @pl.when(at_gate)
    def _():
        drain(spill_sent, spill.at[:, pl.ds(0, mid - 1)])

    @pl.when(has_right)
    def _():
        drain(right_sent, ext.at[:, :, 0])

    @pl.when(has_left)
    def _():
        drain(left_sent, ext.at[:, :, 0])

    stored = []
    for t in range(2):
        drain(back_came[3 * t], land.at[t])

        def add_step(n, carry):
            cols = lanes(n * 128, 128)
            land[t, :, :, :, cols] = (land[t, :, :, :, cols].astype(f32) + conv[t, :, :, :, cols]).astype(jnp.bfloat16)
            return carry

        lax.fori_loop(0, width // 128, add_step, 0)
        stored.append(pltpu.make_async_copy(land.at[t], ret.at[3 * t], here_in.at[4 + t]))
        stored[t].start()
    drain(back_sent, colbuf.at[:, pl.ds(0, R - 1)])
    drain(back_came[1], ret.at[pl.ds(1, 2)])
    for c in stored:
        c.wait()


def finish_kernel(ret, *rest):
    copies = [pltpu.make_async_copy(ret.at[t], rest[t], rest[4].at[t]) for t in range(4)]
    for c in copies:
        c.start()
    for c in copies:
        c.wait()


def fused_body(query, key, value, cotangent, conv_weight, row_mask, col_mask):
    rows, cols_here, width = query.shape
    R, C = lax.axis_size("rows"), lax.axis_size("cols")
    groups = cols_here // SUB
    half = width // 2
    share = half // C
    views = [x.reshape(rows, groups, SUB, width) for x in (query, key, value, cotangent)]
    bf16 = jnp.bfloat16
    any_spec = pl.BlockSpec(memory_space=pl.ANY)
    dma = pltpu.SemaphoreType.DMA
    heads = half // HEAD_DIM
    length = R * rows * SUB
    row_table, col_table = jnp.transpose(row_mask, (1, 2, 0)), jnp.transpose(col_mask, (1, 2, 0))
    ret = pl.pallas_call(
        functools.partial(layer_kernel, (R, C, rows, groups, width)),
        out_shape=jax.ShapeDtypeStruct((4, rows, groups, SUB, width), bf16),
        in_specs=[any_spec] * 7,
        out_specs=any_spec,
        scratch_shapes=[
            pltpu.VMEM((4, R, rows, SUB, half), bf16),
            pltpu.VMEM((4, R, rows, SUB, half), bf16),
            pltpu.VMEM((4, rows, C, groups, SUB, share), bf16),
            pltpu.VMEM((4, rows, C, groups, SUB, share), bf16),
            pltpu.VMEM((2, rows + 2, groups + 2, SUB, width), bf16),
            pltpu.VMEM((2, rows, groups, SUB, width), jnp.float32),
            pltpu.VMEM((2, groups, SUB, half + half - 5 * half // 8), bf16),
            pltpu.VMEM((2, rows, groups, SUB, width), bf16),
            pltpu.VMEM((heads, length, length), jnp.float32),
            pltpu.VMEM((heads, length, HEAD_DIM), jnp.float32),
            pltpu.VMEM((2, R // 2, SUB, half), jnp.float32),
            pltpu.VMEM((2, SUB, half), jnp.float32),
            dma((13,)), dma((15,)), dma((6,)), pltpu.SemaphoreType.REGULAR, pltpu.SemaphoreType.REGULAR,
            pltpu.VMEM(conv_weight.shape, bf16), pltpu.SMEM(row_table.shape, jnp.int32), pltpu.SMEM(col_table.shape, jnp.int32),
        ],
        compiler_params=pltpu.CompilerParams(collective_id=0, has_side_effects=True, vmem_limit_bytes=VMEM_LIMIT),
    )(*[pltpu.with_memory_space_constraint(x, pltpu.HBM) for x in (*views, conv_weight, row_table, col_table)])
    outs = pl.pallas_call(
        finish_kernel,
        out_shape=[jax.ShapeDtypeStruct((rows, groups, SUB, width), bf16)] * 4,
        in_specs=[any_spec],
        out_specs=[any_spec] * 4,
        scratch_shapes=[dma((4,))],
        compiler_params=pltpu.CompilerParams(vmem_limit_bytes=1 << 20),
    )(ret)
    return tuple(x.reshape(query.shape) for x in outs)


def any_body(query, key, value, cotangent, conv_weight, row_mask, col_mask):
    rows, cols_here, width = query.shape
    R, C = lax.axis_size("rows"), lax.axis_size("cols")
    fits = R % 8 == 0 and cols_here == R * SUB and (width // 2) % (C * HEAD_DIM) == 0 and (width // 2) % (8 * HEAD_DIM) == 0
    chosen = fused_body if fits else body
    return chosen(query, key, value, cotangent, conv_weight, row_mask, col_mask)


def solution(mesh):
    return jax.shard_map(
        any_body,
        mesh=mesh,
        in_specs=(
            P("rows", "cols", None),
            P("rows", "cols", None),
            P("rows", "cols", None),
            P("rows", "cols", None),
            P(),
            P("rows", None, None),
            P("cols", None, None),
        ),
        out_specs=(
            P("rows", "cols", None),
            P("rows", "cols", None),
            P("rows", "cols", None),
            P("rows", "cols", None),
        ),
        check_vma=False,
    )
```

```python
import functools
import math

import jax
import jax.numpy as jnp
from jax import lax
from jax.experimental import pallas as pl
from jax.experimental.pallas import tpu as pltpu
from jax.sharding import PartitionSpec as P

HEAD_DIM = 128
SHEET_ROW_BLOCKS = 2
COL_BLOCKS = 3


def padded(array, sides, width):
    for axis, dim in sides:
        devices, length = (lax.axis_size(axis), array.shape[dim])
        up = [(i, (i + 1) % devices) for i in range(devices - 1)]
        down = [(j, i) for i, j in up]
        last = lax.slice_in_dim(array, length - width, length, axis=dim)
        leading = lax.slice_in_dim(array, 0, width, axis=dim)
        before = lax.ppermute(last, axis, up)
        after = lax.ppermute(leading, axis, down)
        array = jnp.concatenate([before, array, after], axis=dim)
    return array


def block_allow(block_mask_table, query_pos, key_pos, block_len, block_count):
    labels = jnp.arange(block_count)
    query_onehot_rows = (query_pos[:, None] // block_len == labels[None, :]).astype(jnp.float32)
    key_onehot_rows = (key_pos[:, None] // block_len == labels[None, :]).astype(jnp.float32)
    merged_links = jnp.einsum(
        "xv,zvs,hs->zxh", query_onehot_rows, block_mask_table.astype(jnp.float32), key_onehot_rows
    )
    return merged_links > 0.5


def line_attention(query_part, key_part, value_part, grad_part, allowed, layout):
    if layout == "bq":
        query_form = "bqhd"
        key_layout_shape = "bkhd"
    else:
        query_form = "qbhd"
        key_layout_shape = "kbhd"
    score_scale = 1.0 / math.sqrt(query_part.shape[-1])
    pair_form = query_form + "," + key_layout_shape + "->bhqk"
    scores = (
        jnp.einsum(pair_form, query_part, key_part, preferred_element_type=jnp.float32)
        * score_scale
    )
    scores = jnp.where(allowed[:, None], scores, -jnp.inf)
    highest = jnp.max(scores, axis=-1, keepdims=True)
    weights = jnp.exp(scores - highest)
    weights = weights / jnp.sum(weights, axis=-1, keepdims=True)
    rounded = weights.astype(jnp.bfloat16)
    attended = jnp.einsum(
        "bhqk," + key_layout_shape + "->" + query_form,
        rounded,
        value_part,
        preferred_element_type=jnp.float32,
    )
    dweights = jnp.einsum(pair_form, grad_part, value_part, preferred_element_type=jnp.float32)
    delta = jnp.sum(grad_part.astype(jnp.float32) * attended, axis=-1)
    if layout == "bq":
        delta = jnp.transpose(delta, (0, 2, 1))
    else:
        delta = jnp.transpose(delta, (1, 2, 0))
    dscores = (weights * (dweights - delta[..., None]) * score_scale).astype(jnp.bfloat16)
    dquery = jnp.einsum(
        "bhqk," + key_layout_shape + "->" + query_form,
        dscores,
        key_part,
        preferred_element_type=jnp.float32,
    )
    dkey = jnp.einsum(
        "bhqk," + query_form + "->" + key_layout_shape,
        dscores,
        query_part,
        preferred_element_type=jnp.float32,
    )
    dvalue = jnp.einsum(
        "bhqk," + query_form + "->" + key_layout_shape,
        rounded,
        grad_part,
        preferred_element_type=jnp.float32,
    )
    return (attended, dquery, dkey, dvalue)


def depthwise(padded_field, taps, rows_count, cols_count, reverse_taps):
    summed = jnp.zeros((rows_count, cols_count, taps.shape[1]), jnp.float32)
    for row_offset_start in range(3):
        for offset_col in range(3):
            if reverse_taps:
                start_row = 2 - row_offset_start
                start_col = 2 - offset_col
            else:
                start_row = row_offset_start
                start_col = offset_col
            window = padded_field[
                start_row : start_row + rows_count, start_col : start_col + cols_count
            ]
            summed = summed + taps[row_offset_start * 3 + offset_col] * window.astype(jnp.float32)
    return summed


def body(query, key, value, cotangent, conv_weight, row_mask, col_mask):
    rows_here, cols_here, width = query.shape
    half_width = width // 2
    head_groups = half_width // HEAD_DIM
    row_devices = lax.axis_size("rows")
    col_devices = lax.axis_size("cols")
    sheet_rows = rows_here * row_devices
    sheet_cols = cols_here * col_devices
    taps = conv_weight.astype(jnp.float32)
    padded_value = padded(value, (("rows", 0), ("cols", 1)), 1)
    padded_grad = padded(cotangent, (("rows", 0), ("cols", 1)), 1)
    row_len = sheet_cols // SHEET_ROW_BLOCKS
    keys_row, values_row = (
        lax.all_gather(key[:, :, :half_width], "cols", axis=1, tiled=True),
        lax.all_gather(value[:, :, :half_width], "cols", axis=1, tiled=True),
    )
    col_start = lax.axis_index("cols") * cols_here
    allowed = block_allow(
        row_mask,
        col_start + jnp.arange(cols_here),
        jnp.arange(sheet_cols),
        row_len,
        SHEET_ROW_BLOCKS,
    )
    local_shape = (rows_here, cols_here, head_groups, HEAD_DIM)
    whole_shape = (rows_here, sheet_cols, head_groups, HEAD_DIM)
    results = line_attention(
        query[:, :, :half_width].reshape(local_shape),
        keys_row.reshape(whole_shape),
        values_row.reshape(whole_shape),
        cotangent[:, :, :half_width].reshape(local_shape),
        allowed,
        "bq",
    )
    key_terms = results[2].reshape(rows_here, sheet_cols, half_width)
    value_terms = results[3].reshape(rows_here, sheet_cols, half_width)
    key_grads, value_grads = (
        lax.psum_scatter(key_terms, "cols", scatter_dimension=1, tiled=True),
        lax.psum_scatter(value_terms, "cols", scatter_dimension=1, tiled=True),
    )
    out_row = results[0].reshape(rows_here, cols_here, half_width).astype(jnp.bfloat16)
    dq_row = results[1].reshape(rows_here, cols_here, half_width).astype(jnp.bfloat16)
    dk_row = key_grads.astype(jnp.bfloat16)
    dv_row = value_grads.astype(jnp.bfloat16)
    columns_each = cols_here // row_devices
    moved = (
        lax.all_to_all(query[:, :, half_width:], "rows", split_axis=1, concat_axis=0, tiled=True),
        lax.all_to_all(key[:, :, half_width:], "rows", split_axis=1, concat_axis=0, tiled=True),
        lax.all_to_all(value[:, :, half_width:], "rows", split_axis=1, concat_axis=0, tiled=True),
        lax.all_to_all(
            cotangent[:, :, half_width:], "rows", split_axis=1, concat_axis=0, tiled=True
        ),
    )
    column_shape = (sheet_rows, columns_each, head_groups, HEAD_DIM)
    my_tables = lax.dynamic_slice_in_dim(
        col_mask, lax.axis_index("rows") * columns_each, columns_each, 0
    )
    col_len = sheet_rows // COL_BLOCKS
    positions = jnp.arange(sheet_rows)
    col_allowed = block_allow(my_tables, positions, positions, col_len, COL_BLOCKS)
    col_results = line_attention(
        moved[0].reshape(column_shape),
        moved[1].reshape(column_shape),
        moved[2].reshape(column_shape),
        moved[3].reshape(column_shape),
        col_allowed,
        "qb",
    )
    column_flat = (sheet_rows, columns_each, half_width)
    col_pieces = [piece.reshape(column_flat).astype(jnp.bfloat16) for piece in col_results]
    out_col, dq_col, dk_col, dv_col = (
        lax.all_to_all(col_pieces[0], "rows", split_axis=0, concat_axis=1, tiled=True),
        lax.all_to_all(col_pieces[1], "rows", split_axis=0, concat_axis=1, tiled=True),
        lax.all_to_all(col_pieces[2], "rows", split_axis=0, concat_axis=1, tiled=True),
        lax.all_to_all(col_pieces[3], "rows", split_axis=0, concat_axis=1, tiled=True),
    )
    lepe = depthwise(padded_value, taps, rows_here, cols_here, False)
    back_conv = depthwise(padded_grad, taps, rows_here, cols_here, True)
    attended16 = jnp.concatenate([out_row, out_col], axis=2)
    out = (attended16.astype(jnp.float32) + lepe).astype(jnp.bfloat16)
    dquery = jnp.concatenate([dq_row, dq_col], axis=2)
    dkey = jnp.concatenate([dk_row, dk_col], axis=2)
    dvalue_attn = jnp.concatenate([dv_row, dv_col], axis=2)
    dvalue = (dvalue_attn.astype(jnp.float32) + back_conv).astype(jnp.bfloat16)
    return (out, dquery, dkey, dvalue)


SUB = 8
VMEM_LIMIT = 28 << 20
MESH = pl.DeviceIdType.MESH


def attend(q, k, v, g, allow):
    scale = 1.0 / math.sqrt(HEAD_DIM)
    nt = (((1,), (1,)), ((), ()))
    nn = (((1,), (0,)), ((), ()))
    tn = (((0,), (0,)), ((), ()))
    dot = functools.partial(lax.dot_general, preferred_element_type=jnp.float32)
    s = jnp.where(allow, dot(q, k, nt) * scale, -jnp.inf)
    e = jnp.exp(s - jnp.max(s, axis=-1, keepdims=True))
    w = e * (1.0 / jnp.sum(e, axis=-1, keepdims=True))
    w16 = w.astype(jnp.bfloat16)
    att = dot(w16, v, nn)
    dw = dot(g, v, nt)
    delta = jnp.sum(g.astype(jnp.float32) * att, axis=-1, keepdims=True)
    ds = (w * (dw - delta) * scale).astype(jnp.bfloat16)
    return att, dot(ds, k, nn), dot(ds, q, tn), dot(w16, g, tn)


def dots():
    dot = functools.partial(lax.dot_general, preferred_element_type=jnp.float32)
    return (
        functools.partial(dot, dimension_numbers=(((1,), (1,)), ((), ()))),
        functools.partial(dot, dimension_numbers=(((1,), (0,)), ((), ()))),
        functools.partial(dot, dimension_numbers=(((0,), (0,)), ((), ()))),
    )


def softmax(q, k, allow):
    nt, _, _ = dots()
    s = jnp.where(allow, nt(q, k) * (1.0 / math.sqrt(HEAD_DIM)), -jnp.inf)
    e = jnp.exp(s - jnp.max(s, axis=-1, keepdims=True))
    return e * (1.0 / jnp.sum(e, axis=-1, keepdims=True))


def layer_kernel(dims, q_hbm, k_hbm, v_hbm, g_hbm, taps_hbm, row_hbm, col_hbm, ret, *rest):
    R, C, rows, groups, width = dims
    colbuf, colout, rowbuf, rowout, ext, conv, hop, land, weights, attended, spill, spilled = rest[:12]
    sent, came, here_in, ends_in, lines_in, late_in, taps, row_mask, col_mask = rest[12:]
    half = width // 2
    share = half // C
    heads = half // HEAD_DIM
    me = lax.axis_index("rows")
    mc = lax.axis_index("cols")
    inputs = (q_hbm, k_hbm, v_hbm, g_hbm)
    f32 = jnp.float32
    first, second = pl.ds(0, half), pl.ds(half, half)

    def lanes(start, size):
        return pl.ds(pl.multiple_of(start, 128), size)

    def send(src, dst, send_sem, recv_sem, target):
        return pltpu.make_async_remote_copy(
            src_ref=src, dst_ref=dst, send_sem=send_sem, recv_sem=recv_sem,
            device_id=target, device_id_type=MESH)

    col_sent, back_sent, row_sent, row_back_sent, near_sent, cross_sent, far_sent, pass_sent, pass_far_sent, border_sent, right_sent, left_sent, spill_sent = (
        sent.at[i] for i in range(13))
    col_came = [came.at[t] for t in range(4)]
    back_came = [came.at[4], came.at[5], came.at[5], came.at[6]]
    row_came, hop_came, hop_far_came, near_came, cross_came, right_came, left_came, spill_came = (came.at[7 + i] for i in range(8))

    def drain(semaphore, ref):
        pltpu.make_async_copy(ref, ref, semaphore).wait()

    def home(t):
        return land.at[t // 3] if t in (0, 3) else ret.at[t]

    def col_in(t, p, slot):
        return send(inputs[t].at[:, p, :, second], colbuf.at[t, slot],
                    col_sent, col_came[t], {"rows": p})

    def col_back(t, p, slot):
        if t == 1:
            pair = pl.ds(1, 2)
            src, dst = colout.at[pair, p], ret.at[pair, :, slot, :, second]
        else:
            src, dst = colout.at[t, p], land.at[t // 3, :, slot, :, second]
        return send(src, dst, back_sent, back_came[t], {"rows": p})

    def row_in(t, p, slot):
        return send(inputs[t].at[:, :, :, lanes(p * share, share)], rowbuf.at[t, :, slot],
                    row_sent, row_came, {"cols": p})

    def row_back(t, p, slot):
        return send(rowout.at[t, :, p], home(t).at[:, :, :, lanes(slot * share, share)],
                    row_back_sent, back_came[t], {"cols": p})

    odd = lax.rem(me, 2)
    sign = 2 * odd - 1
    crosses = jnp.logical_and(me + sign >= 0, me + sign < R)
    relays = jnp.logical_and(me - 2 * sign >= 0, me - 2 * sign < R)
    inner = pl.ds(1, groups)
    even_slot, odd_slot = (1 - odd) * (rows + 1), odd * (rows + 1)
    mid = R // 2
    side = me // mid
    gate = mid - 1 + side
    at_gate = me == gate
    beside_gate = me - sign == gate
    shares = (6 * half // 8, 5 * half // 8)
    room = half - min(shares)
    base = side * mid
    away = jnp.logical_not(at_gate)
    has_right, has_left = mc < C - 1, mc > 0

    def by_side(act):
        for s in range(2):
            pl.when(side == s)(functools.partial(act, shares[s]))

    def cross(t, direct):
        return send(inputs[2 + t].at[odd * (rows - 1), :, :, pl.ds(0, direct)],
                    ext.at[t, even_slot, inner, :, pl.ds(0, direct)], cross_sent, cross_came, {"rows": me + sign})

    def detour(t, direct):
        return send(inputs[2 + t].at[odd * (rows - 1), :, :, pl.ds(direct, half - direct)],
                    hop.at[t, :, :, pl.ds(0, half - direct)], cross_sent, hop_came, {"rows": me - sign})

    def detour_far(t, span):
        return send(inputs[2 + t].at[odd * (rows - 1), span, :, second],
                    hop.at[t, span, :, pl.ds(room, half)], far_sent, hop_far_came, {"rows": me - sign})

    def forward(direct):
        return send(hop.at[:, :, :, pl.ds(0, half - direct)], ext.at[:, odd_slot, inner, :, pl.ds(direct, half - direct)],
                    pass_sent, cross_came, {"rows": me - 2 * sign})

    def forward_far(span):
        return send(hop.at[:, span, :, pl.ds(room, half)], ext.at[:, odd_slot, inner].at[:, span, :, second],
                    pass_far_sent, cross_came, {"rows": me - 2 * sign})

    def near(t):
        return send(inputs[2 + t].at[(1 - odd) * (rows - 1)], ext.at[t, odd_slot, inner],
                    near_sent, near_came, {"rows": me - sign})

    def rightward(t):
        return send(inputs[2 + t].at[:, groups - 1], ext.at[t, pl.ds(1, rows), 0],
                    right_sent, right_came, {"cols": mc + 1})

    def leftward(t):
        return send(inputs[2 + t].at[:, 0], ext.at[t, pl.ds(1, rows), groups + 1],
                    left_sent, left_came, {"cols": mc - 1})

    def corner_right(r):
        return send(ext.at[:, r, groups], ext.at[:, r, 0], right_sent, right_came, {"cols": mc + 1})

    def corner_left(r):
        return send(ext.at[:, r, 1], ext.at[:, r, groups + 1], left_sent, left_came, {"cols": mc - 1})

    border_from = colbuf.at[pl.ds(2, 2), mid - side, side * (rows - 1)]
    border_to = ext.at[:, (1 - side) * (rows + 1), 1 + me, :, second]

    def border():
        return send(border_from, border_to, border_sent, cross_came, {"rows": gate})

    def by_gate(gone, act):
        @pl.when(gone)
        def _():
            act(pl.ds(base, 1))
            act(pl.ds(base + mid - 1, 1))

        pl.when(jnp.logical_not(gone))(lambda: act(pl.ds(0, groups)))

    def drain_far(gone, semaphore):
        pl.when(gone)(lambda: drain(semaphore, hop.at[:, pl.ds(0, 2), :, pl.ds(room, half)]))
        pl.when(jnp.logical_not(gone))(lambda: drain(semaphore, hop.at[:, :, :, pl.ds(room, half)]))

    def spill_copy(p):
        return send(spill.at[:, p - base], spilled, spill_sent, spill_came, {"rows": p})

    def others_on(here, count, act, spread=False):
        def step(n, carry):
            d = n + 1
            if spread:
                d = count // 2 + jnp.where(lax.rem(n, 2) == 0, d // 2, -(d // 2))
            act(lax.rem(here + d, count))
            return carry

        lax.fori_loop(0, count - 1, step, 0)

    each_row = functools.partial(others_on, me, R)
    each_col = functools.partial(others_on, mc, C)

    quarter = R // 4
    in_mid = jnp.logical_and(me >= quarter, me < R - quarter)
    far_mid = mid - side * quarter
    near_mid = quarter + side * quarter
    far_end, near_end = (1 - side) * (R - quarter), side * (R - quarter)
    early = jnp.logical_and(in_mid, me == near_mid)
    barrier = pltpu.get_barrier_semaphore()

    def group(bases, act):
        def step(n, carry):
            base = bases[-1]
            for i in range(len(bases) - 1, 0, -1):
                base = jnp.where(n < i * quarter, bases[i - 1], base)
            p = base + lax.rem(n, quarter)
            pl.when(p != me)(lambda: act(p))
            return carry

        lax.fori_loop(0, len(bases) * quarter, step, 0)

    def tell(semaphore, target):
        pl.semaphore_signal(semaphore, inc=1, device_id=target, device_id_type=MESH)

    @pl.when(in_mid)
    def _():
        @pl.when(early)
        def _():
            group((far_mid, near_mid, far_end, near_end), lambda p: tell(barrier, {"rows": p}))
            pl.semaphore_wait(barrier, 1)

        @pl.when(jnp.logical_not(early))
        def _():
            for start in (far_mid, near_mid):
                for j in range(1, quarter):
                    @pl.when(start + j != me)
                    def _(p=start + j):
                        tell(barrier, {"rows": p})
            group((far_end, near_end), lambda p: tell(barrier, {"rows": p}))
            pl.semaphore_wait(barrier, mid - 1)
            tell(late_in, {"rows": far_mid})
            tell(late_in, {"rows": near_mid})

    @pl.when(jnp.logical_not(in_mid))
    def _():
        group((far_end, near_end), lambda p: tell(barrier, {"rows": p}))
        each_col(lambda p: tell(barrier, {"cols": p}))
        pl.semaphore_wait(barrier, R - 1 + C - 1)
        each_col(lambda p: tell(lines_in, {"cols": p}))

    def send_cols(kinds, bases):
        for t in kinds:
            group(bases, lambda p: col_in(t, p, me).start())

    @pl.when(early)
    def _():
        for t in (0, 1):
            col_in(t, far_mid, me).start()
        pl.semaphore_wait(late_in, mid - 2)
        for start in (far_mid, near_mid):
            for j in range(1, quarter):
                for t in (0, 1):
                    col_in(t, start + j, me).start()

    @pl.when(jnp.logical_not(early))
    def _():
        send_cols((0, 1), (far_mid, near_mid))

    @pl.when(jnp.logical_not(in_mid))
    def _():
        pl.semaphore_wait(lines_in, C - 1)
        group((far_mid, near_mid), lambda p: tell(ends_in, {"rows": p}))

    @pl.when(in_mid)
    def _():
        pl.semaphore_wait(ends_in, 2 * quarter)

    send_cols((0, 1), (far_end, near_end))
    send_cols((2, 3), (far_mid, far_end, near_mid, near_end))

    def send_halo():
        @pl.when(crosses)
        def _():
            for t in range(2):
                by_side(lambda direct: detour(t, direct).start())
                by_gate(at_gate, lambda span: detour_far(t, span).start())
                by_side(lambda direct: cross(t, direct).start())

        for t in range(2):
            near(t).start()

    def send_sides():
        @pl.when(has_right)
        def _():
            for t in range(2):
                rightward(t).start()

        @pl.when(has_left)
        def _():
            for t in range(2):
                leftward(t).start()

    def pass_halo():
        @pl.when(relays)
        def _():
            def hand_on(direct):
                drain(hop_came, hop.at[:, :, :, pl.ds(0, half - direct)])
                forward(direct).start()

            by_side(hand_on)

            drain_far(beside_gate, hop_far_came)
            by_gate(beside_gate, lambda span: forward_far(span).start())

    def send_rows(t):
        each_col(lambda p: row_in(t, p, mc).start(), spread=True)

    for t in range(4):
        send_rows(t)
    send_halo()
    send_sides()

    tables = [
        pltpu.make_async_copy(src, dst, here_in.at[i])
        for i, (src, dst) in enumerate(((taps_hbm, taps), (row_hbm, row_mask), (col_hbm, col_mask)))
    ]
    for c in tables:
        c.start()
    for t in range(4):
        pltpu.make_async_copy(inputs[t].at[:, :, :, lanes(mc * share, share)], rowbuf.at[t, :, mc], row_came).start()
        pltpu.make_async_copy(inputs[t].at[:, me, :, second], colbuf.at[t, me], col_came[t]).start()
    for t in range(2):
        pltpu.make_async_copy(inputs[2 + t], ext.at[t, pl.ds(1, rows), inner], here_in.at[3]).start()
    for edge, area in (
        (me == 0, (slice(None), 0, inner)),
        (me == R - 1, (slice(None), rows + 1, inner)),
        (mc == 0, (slice(None), slice(None), 0)),
        (mc == C - 1, (slice(None), slice(None), groups + 1)),
    ):
        @pl.when(edge)
        def _(area=area):
            for t in range(2):
                view = ext.at[(t,) + area[1:]]
                view[...] = jnp.zeros(view.shape, view.dtype)

    @pl.when(at_gate)
    def _():
        for t in range(2):
            view = ext.at[t, (1 - side) * (rows + 1), pl.ds(1 + mid - base + 1, mid - 2), :, second]
            view[...] = jnp.zeros(view.shape, view.dtype)
    for c in tables:
        c.wait()
    drain(here_in.at[3], ext.at[:, pl.ds(1, rows), inner])

    def spill_step(n, carry):
        cols = lanes(half + n * 128, 128)
        taps_here = taps[:, cols].astype(f32)
        for t in range(2):
            source = ext[t, rows - side * (rows - 1), pl.ds(1 + base + 1, mid - 2), :, cols].astype(f32)
            edge = jnp.zeros((2 * SUB, 128), f32)
            line = jnp.concatenate([edge, source.reshape((mid - 2) * SUB, 128), edge], axis=0)
            total = jnp.zeros((mid * SUB, 128), f32)
            for b in range(3):
                above, below = (b, 6 + b) if t == 0 else (8 - b, 2 - b)
                tap = jnp.where(side == 1, taps_here[below : below + 1], taps_here[above : above + 1])
                total = total + tap * line[SUB + b - 1 : SUB + b - 1 + mid * SUB]
            spill[t, :, :, lanes(n * 128, 128)] = total.reshape(mid, SUB, 128)
        return carry

    @pl.when(at_gate)
    def _():
        lax.fori_loop(0, half // 128, spill_step, 0)
        pltpu.make_async_copy(spill.at[:, me - base], spilled, spill_came).start()
        for j in range(mid):
            @pl.when(base + j != me)
            def _(p=base + j):
                spill_copy(p).start()

    length = R * rows * SUB
    col_size = length // COL_BLOCKS
    key_pos = lax.broadcasted_iota(jnp.int32, (SUB, length), 1)
    lane_col = lax.broadcasted_iota(jnp.int32, (SUB, length), 0)
    block = jnp.where(lax.rem(key_pos, SUB) == lane_col, key_pos // col_size, -1)
    col_tables = []
    for b in range(COL_BLOCKS):
        table = jnp.zeros((SUB, length), jnp.int32)
        for c in range(SUB):
            for j in range(COL_BLOCKS):
                here = jnp.logical_and(lane_col == c, block == j)
                table = jnp.where(here, col_mask[b, j, me * SUB + c], table)
        col_tables.append(table)

    pass_halo()

    drain(row_came, rowbuf)
    tokens = C * groups * SUB

    def row_step(n, carry):
        i, h = n // (share // HEAD_DIM), lax.rem(n, share // HEAD_DIM)
        cols = lanes(h * HEAD_DIM, HEAD_DIM)
        x = [rowbuf[t, i, :, :, :, cols].astype(f32).reshape(tokens, HEAD_DIM).astype(jnp.bfloat16) for t in range(4)]
        size = tokens // SHEET_ROW_BLOCKS
        place = lax.broadcasted_iota(jnp.int32, (SUB, tokens), 1) // size
        bands = []
        for b in range(SHEET_ROW_BLOCKS):
            table = jnp.zeros((SUB, tokens), jnp.int32)
            for j in range(SHEET_ROW_BLOCKS):
                table = jnp.where(place == j, row_mask[b, j, i], table)
            bands.append(jnp.broadcast_to(table[None], (size // SUB, SUB, tokens)).reshape(size, tokens))
        allow = jnp.concatenate(bands, axis=0) > 0
        for t, y in enumerate(attend(*x, allow)):
            rowout[t, i, :, :, :, cols] = y.reshape(C, groups, SUB, HEAD_DIM).astype(jnp.bfloat16)
        return carry

    lax.fori_loop(0, rows * (share // HEAD_DIM), row_step, 0)
    for t in (0, 3, 1, 2):
        each_col(lambda p: row_back(t, p, mc).start(), spread=True)
        pltpu.make_async_copy(rowout.at[t, :, mc], home(t).at[:, :, :, lanes(mc * share, share)], back_came[t]).start()

    nt, nn, tn = dots()

    def arrived(t):
        drain(col_came[t], colbuf.at[t])

    def give_back(t):
        @pl.when(side == 1)
        def _():
            each_row(lambda p: col_back(t, p, me).start(), spread=True)

        @pl.when(side == 0)
        def _():
            def step(n, carry):
                i = n // 2
                p = jnp.where(lax.rem(n, 2) == 0, mid + lax.rem(i + 2, mid), lax.rem(me + i + 1, mid))
                col_back(t, p, me).start()
                return carry

            lax.fori_loop(0, R - 1, step, 0)

        for u in (1, 2) if t == 1 else (t,):
            pltpu.make_async_copy(colout.at[u, me], home(u).at[:, me, :, second], back_came[u]).start()

    def column(t, h):
        return colbuf[t, :, :, :, lanes(h * HEAD_DIM, HEAD_DIM)].astype(f32).reshape(length, HEAD_DIM).astype(jnp.bfloat16)

    def give(t, h, y):
        colout[t, :, :, :, lanes(h * HEAD_DIM, HEAD_DIM)] = y.reshape(R, rows, SUB, HEAD_DIM).astype(jnp.bfloat16)

    def weigh(h, carry):
        allow = jnp.concatenate(
            [jnp.broadcast_to(t[None], (col_size // SUB, SUB, length)).reshape(col_size, length) for t in col_tables], axis=0) > 0
        weights[h] = softmax(column(0, h), column(1, h), allow)
        return carry

    def forward_step(h, carry):
        att = nn(weights[h].astype(jnp.bfloat16), column(2, h))
        attended[h] = att
        give(0, h, att)
        return carry

    def value_step(h, carry):
        give(3, h, tn(weights[h].astype(jnp.bfloat16), column(3, h)))
        return carry

    def score_step(h, carry):
        g = column(3, h)
        delta = jnp.sum(g.astype(f32) * attended[h], axis=-1, keepdims=True)
        ds = (weights[h] * (nt(g, column(2, h)) - delta) * (1.0 / math.sqrt(HEAD_DIM))).astype(jnp.bfloat16)
        give(1, h, nn(ds, column(1, h)))
        give(2, h, tn(ds, column(0, h)))
        return carry

    arrived(0)
    arrived(1)
    lax.fori_loop(0, heads, weigh, 0)
    arrived(2)
    lax.fori_loop(0, heads, forward_step, 0)

    def add_spill(t, u):
        place = colout.at[t, mid - side, side * (rows - 1)]
        place[...] = (place[...].astype(f32) + spilled[u]).astype(jnp.bfloat16)

    drain(spill_came, spilled)
    add_spill(0, 0)
    give_back(0)
    arrived(3)

    @pl.when(away)
    def _():
        border().start()

    @pl.when(at_gate)
    def _():
        pltpu.make_async_copy(border_from, border_to, cross_came).start()

    lax.fori_loop(0, heads, value_step, 0)
    add_spill(3, 1)
    give_back(3)

    drain(near_came, ext.at[:, even_slot, inner])

    @pl.when(crosses)
    def _():
        pl.when(at_gate)(lambda: drain(cross_came, ext.at[:, odd_slot, pl.ds(0, (groups + mid + 2) // 2)]))
        pl.when(away)(lambda: drain(cross_came, ext.at[:, odd_slot, inner]))

    for r in (0, rows + 1):
        @pl.when(has_right)
        def _(r=r):
            corner_right(r).start()

        @pl.when(has_left)
        def _(r=r):
            corner_left(r).start()

    lax.fori_loop(0, heads, score_step, 0)
    give_back(1)

    @pl.when(has_left)
    def _():
        drain(right_came, ext.at[:, :, 0])

    @pl.when(has_right)
    def _():
        drain(left_came, ext.at[:, :, groups + 1])

    long = groups * SUB

    def conv_step(n, carry):
        cols = lanes(n * 128, 128)
        taps_here = taps[:, cols].astype(f32)
        for t in range(2):
            sums = [None] * rows
            for r in range(rows + 2):
                line = ext[t, r, :, :, cols].astype(f32).reshape(long + 2 * SUB, 128)
                for b in range(3):
                    seen = line[SUB + b - 1 : SUB + b - 1 + long]
                    for a in range(3):
                        o = r - a
                        if 0 <= o < rows:
                            tap = 3 * a + b if t == 0 else 8 - 3 * a - b
                            term = taps_here[tap : tap + 1] * seen
                            sums[o] = term if sums[o] is None else sums[o] + term
            for o in range(rows):
                conv[t, o, :, :, cols] = sums[o].reshape(groups, SUB, 128)
        return carry

    lax.fori_loop(0, width // 128, conv_step, 0)

    drain(col_sent, colbuf.at[:, pl.ds(0, R - 1)])
    for semaphore in (row_sent, row_back_sent):
        drain(semaphore, rowbuf.at[:, :, pl.ds(0, C - 1)])
    drain(near_sent, ext.at[:, 0, inner])

    @pl.when(crosses)
    def _():
        drain(cross_sent, ext.at[:, 0, inner, :, first])
        drain_far(at_gate, far_sent)

    @pl.when(relays)
    def _():
        by_side(lambda direct: drain(pass_sent, hop.at[:, :, :, pl.ds(0, half - direct)]))
        drain_far(beside_gate, pass_far_sent)

    @pl.when(away)
    def _():
        drain(border_sent, border_from)

    @pl.when(at_gate)
    def _():
        drain(spill_sent, spill.at[:, pl.ds(0, mid - 1)])

    @pl.when(has_right)
    def _():
        drain(right_sent, ext.at[:, :, 0])

    @pl.when(has_left)
    def _():
        drain(left_sent, ext.at[:, :, 0])

    stored = []
    for t in range(2):
        drain(back_came[3 * t], land.at[t])

        def add_step(n, carry):
            cols = lanes(n * 128, 128)
            land[t, :, :, :, cols] = (land[t, :, :, :, cols].astype(f32) + conv[t, :, :, :, cols]).astype(jnp.bfloat16)
            return carry

        lax.fori_loop(0, width // 128, add_step, 0)
        stored.append(pltpu.make_async_copy(land.at[t], ret.at[3 * t], here_in.at[4 + t]))
        stored[t].start()
    drain(back_sent, colbuf.at[:, pl.ds(0, R - 1)])
    drain(back_came[1], ret.at[pl.ds(1, 2)])
    for c in stored:
        c.wait()


def finish_kernel(ret, *rest):
    for t in range(4):
        pltpu.make_async_copy(ret.at[t], rest[t], rest[4]).start()
    pltpu.make_async_copy(ret, ret, rest[4]).wait()


def fused_body(query, key, value, cotangent, conv_weight, row_mask, col_mask):
    rows, cols_here, width = query.shape
    R, C = lax.axis_size("rows"), lax.axis_size("cols")
    groups = cols_here // SUB
    half = width // 2
    share = half // C
    views = [x.reshape(rows, groups, SUB, width) for x in (query, key, value, cotangent)]
    bf16 = jnp.bfloat16
    any_spec = pl.BlockSpec(memory_space=pl.ANY)
    dma = pltpu.SemaphoreType.DMA
    heads = half // HEAD_DIM
    length = R * rows * SUB
    row_table, col_table = jnp.transpose(row_mask, (1, 2, 0)), jnp.transpose(col_mask, (1, 2, 0))
    ret = pl.pallas_call(
        functools.partial(layer_kernel, (R, C, rows, groups, width)),
        out_shape=jax.ShapeDtypeStruct((4, rows, groups, SUB, width), bf16),
        in_specs=[any_spec] * 7,
        out_specs=any_spec,
        scratch_shapes=[
            pltpu.VMEM((4, R, rows, SUB, half), bf16),
            pltpu.VMEM((4, R, rows, SUB, half), bf16),
            pltpu.VMEM((4, rows, C, groups, SUB, share), bf16),
            pltpu.VMEM((4, rows, C, groups, SUB, share), bf16),
            pltpu.VMEM((2, rows + 2, groups + 2, SUB, width), bf16),
            pltpu.VMEM((2, rows, groups, SUB, width), jnp.float32),
            pltpu.VMEM((2, groups, SUB, half + half - 5 * half // 8), bf16),
            pltpu.VMEM((2, rows, groups, SUB, width), bf16),
            pltpu.VMEM((heads, length, length), jnp.float32),
            pltpu.VMEM((heads, length, HEAD_DIM), jnp.float32),
            pltpu.VMEM((2, R // 2, SUB, half), jnp.float32),
            pltpu.VMEM((2, SUB, half), jnp.float32),
            dma((13,)), dma((15,)), dma((6,)), pltpu.SemaphoreType.REGULAR, pltpu.SemaphoreType.REGULAR, pltpu.SemaphoreType.REGULAR,
            pltpu.VMEM(conv_weight.shape, bf16), pltpu.SMEM(row_table.shape, jnp.int32), pltpu.SMEM(col_table.shape, jnp.int32),
        ],
        compiler_params=pltpu.CompilerParams(collective_id=0, has_side_effects=True, vmem_limit_bytes=VMEM_LIMIT),
    )(*[pltpu.with_memory_space_constraint(x, pltpu.HBM) for x in (*views, conv_weight, row_table, col_table)])
    outs = pl.pallas_call(
        finish_kernel,
        out_shape=[jax.ShapeDtypeStruct((rows, groups, SUB, width), bf16)] * 4,
        in_specs=[any_spec],
        out_specs=[any_spec] * 4,
        scratch_shapes=[dma(())],
        compiler_params=pltpu.CompilerParams(vmem_limit_bytes=1 << 20),
    )(ret)
    return tuple(x.reshape(query.shape) for x in outs)


def any_body(query, key, value, cotangent, conv_weight, row_mask, col_mask):
    rows, cols_here, width = query.shape
    R, C = lax.axis_size("rows"), lax.axis_size("cols")
    fits = R % 8 == 0 and cols_here == R * SUB and (width // 2) % (C * HEAD_DIM) == 0 and (width // 2) % (8 * HEAD_DIM) == 0
    chosen = fused_body if fits else body
    return chosen(query, key, value, cotangent, conv_weight, row_mask, col_mask)


def solution(mesh):
    return jax.shard_map(
        any_body,
        mesh=mesh,
        in_specs=(
            P("rows", "cols", None),
            P("rows", "cols", None),
            P("rows", "cols", None),
            P("rows", "cols", None),
            P(),
            P("rows", None, None),
            P("cols", None, None),
        ),
        out_specs=(
            P("rows", "cols", None),
            P("rows", "cols", None),
            P("rows", "cols", None),
            P("rows", "cols", None),
        ),
        check_vma=False,
    )
```

```python
import functools
import math

import jax
import jax.numpy as jnp
from jax import lax
from jax.experimental import pallas as pl
from jax.experimental.pallas import tpu as pltpu
from jax.sharding import PartitionSpec as P

HEAD_DIM = 128
SHEET_ROW_BLOCKS = 2
COL_BLOCKS = 3


def padded(array, sides, width):
    for axis, dim in sides:
        devices, length = (lax.axis_size(axis), array.shape[dim])
        up = [(i, (i + 1) % devices) for i in range(devices - 1)]
        down = [(j, i) for i, j in up]
        last = lax.slice_in_dim(array, length - width, length, axis=dim)
        leading = lax.slice_in_dim(array, 0, width, axis=dim)
        before = lax.ppermute(last, axis, up)
        after = lax.ppermute(leading, axis, down)
        array = jnp.concatenate([before, array, after], axis=dim)
    return array


def block_allow(block_mask_table, query_pos, key_pos, block_len, block_count):
    labels = jnp.arange(block_count)
    query_onehot_rows = (query_pos[:, None] // block_len == labels[None, :]).astype(jnp.float32)
    key_onehot_rows = (key_pos[:, None] // block_len == labels[None, :]).astype(jnp.float32)
    merged_links = jnp.einsum(
        "xv,zvs,hs->zxh", query_onehot_rows, block_mask_table.astype(jnp.float32), key_onehot_rows
    )
    return merged_links > 0.5


def line_attention(query_part, key_part, value_part, grad_part, allowed, layout):
    if layout == "bq":
        query_form = "bqhd"
        key_layout_shape = "bkhd"
    else:
        query_form = "qbhd"
        key_layout_shape = "kbhd"
    score_scale = 1.0 / math.sqrt(query_part.shape[-1])
    pair_form = query_form + "," + key_layout_shape + "->bhqk"
    scores = (
        jnp.einsum(pair_form, query_part, key_part, preferred_element_type=jnp.float32)
        * score_scale
    )
    scores = jnp.where(allowed[:, None], scores, -jnp.inf)
    highest = jnp.max(scores, axis=-1, keepdims=True)
    weights = jnp.exp(scores - highest)
    weights = weights / jnp.sum(weights, axis=-1, keepdims=True)
    rounded = weights.astype(jnp.bfloat16)
    attended = jnp.einsum(
        "bhqk," + key_layout_shape + "->" + query_form,
        rounded,
        value_part,
        preferred_element_type=jnp.float32,
    )
    dweights = jnp.einsum(pair_form, grad_part, value_part, preferred_element_type=jnp.float32)
    delta = jnp.sum(grad_part.astype(jnp.float32) * attended, axis=-1)
    if layout == "bq":
        delta = jnp.transpose(delta, (0, 2, 1))
    else:
        delta = jnp.transpose(delta, (1, 2, 0))
    dscores = (weights * (dweights - delta[..., None]) * score_scale).astype(jnp.bfloat16)
    dquery = jnp.einsum(
        "bhqk," + key_layout_shape + "->" + query_form,
        dscores,
        key_part,
        preferred_element_type=jnp.float32,
    )
    dkey = jnp.einsum(
        "bhqk," + query_form + "->" + key_layout_shape,
        dscores,
        query_part,
        preferred_element_type=jnp.float32,
    )
    dvalue = jnp.einsum(
        "bhqk," + query_form + "->" + key_layout_shape,
        rounded,
        grad_part,
        preferred_element_type=jnp.float32,
    )
    return (attended, dquery, dkey, dvalue)


def depthwise(padded_field, taps, rows_count, cols_count, reverse_taps):
    summed = jnp.zeros((rows_count, cols_count, taps.shape[1]), jnp.float32)
    for row_offset_start in range(3):
        for offset_col in range(3):
            if reverse_taps:
                start_row = 2 - row_offset_start
                start_col = 2 - offset_col
            else:
                start_row = row_offset_start
                start_col = offset_col
            window = padded_field[
                start_row : start_row + rows_count, start_col : start_col + cols_count
            ]
            summed = summed + taps[row_offset_start * 3 + offset_col] * window.astype(jnp.float32)
    return summed


def body(query, key, value, cotangent, conv_weight, row_mask, col_mask):
    rows_here, cols_here, width = query.shape
    half_width = width // 2
    head_groups = half_width // HEAD_DIM
    row_devices = lax.axis_size("rows")
    col_devices = lax.axis_size("cols")
    sheet_rows = rows_here * row_devices
    sheet_cols = cols_here * col_devices
    taps = conv_weight.astype(jnp.float32)
    padded_value = padded(value, (("rows", 0), ("cols", 1)), 1)
    padded_grad = padded(cotangent, (("rows", 0), ("cols", 1)), 1)
    row_len = sheet_cols // SHEET_ROW_BLOCKS
    keys_row, values_row = (
        lax.all_gather(key[:, :, :half_width], "cols", axis=1, tiled=True),
        lax.all_gather(value[:, :, :half_width], "cols", axis=1, tiled=True),
    )
    col_start = lax.axis_index("cols") * cols_here
    allowed = block_allow(
        row_mask,
        col_start + jnp.arange(cols_here),
        jnp.arange(sheet_cols),
        row_len,
        SHEET_ROW_BLOCKS,
    )
    local_shape = (rows_here, cols_here, head_groups, HEAD_DIM)
    whole_shape = (rows_here, sheet_cols, head_groups, HEAD_DIM)
    results = line_attention(
        query[:, :, :half_width].reshape(local_shape),
        keys_row.reshape(whole_shape),
        values_row.reshape(whole_shape),
        cotangent[:, :, :half_width].reshape(local_shape),
        allowed,
        "bq",
    )
    key_terms = results[2].reshape(rows_here, sheet_cols, half_width)
    value_terms = results[3].reshape(rows_here, sheet_cols, half_width)
    key_grads, value_grads = (
        lax.psum_scatter(key_terms, "cols", scatter_dimension=1, tiled=True),
        lax.psum_scatter(value_terms, "cols", scatter_dimension=1, tiled=True),
    )
    out_row = results[0].reshape(rows_here, cols_here, half_width).astype(jnp.bfloat16)
    dq_row = results[1].reshape(rows_here, cols_here, half_width).astype(jnp.bfloat16)
    dk_row = key_grads.astype(jnp.bfloat16)
    dv_row = value_grads.astype(jnp.bfloat16)
    columns_each = cols_here // row_devices
    moved = (
        lax.all_to_all(query[:, :, half_width:], "rows", split_axis=1, concat_axis=0, tiled=True),
        lax.all_to_all(key[:, :, half_width:], "rows", split_axis=1, concat_axis=0, tiled=True),
        lax.all_to_all(value[:, :, half_width:], "rows", split_axis=1, concat_axis=0, tiled=True),
        lax.all_to_all(
            cotangent[:, :, half_width:], "rows", split_axis=1, concat_axis=0, tiled=True
        ),
    )
    column_shape = (sheet_rows, columns_each, head_groups, HEAD_DIM)
    my_tables = lax.dynamic_slice_in_dim(
        col_mask, lax.axis_index("rows") * columns_each, columns_each, 0
    )
    col_len = sheet_rows // COL_BLOCKS
    positions = jnp.arange(sheet_rows)
    col_allowed = block_allow(my_tables, positions, positions, col_len, COL_BLOCKS)
    col_results = line_attention(
        moved[0].reshape(column_shape),
        moved[1].reshape(column_shape),
        moved[2].reshape(column_shape),
        moved[3].reshape(column_shape),
        col_allowed,
        "qb",
    )
    column_flat = (sheet_rows, columns_each, half_width)
    col_pieces = [piece.reshape(column_flat).astype(jnp.bfloat16) for piece in col_results]
    out_col, dq_col, dk_col, dv_col = (
        lax.all_to_all(col_pieces[0], "rows", split_axis=0, concat_axis=1, tiled=True),
        lax.all_to_all(col_pieces[1], "rows", split_axis=0, concat_axis=1, tiled=True),
        lax.all_to_all(col_pieces[2], "rows", split_axis=0, concat_axis=1, tiled=True),
        lax.all_to_all(col_pieces[3], "rows", split_axis=0, concat_axis=1, tiled=True),
    )
    lepe = depthwise(padded_value, taps, rows_here, cols_here, False)
    back_conv = depthwise(padded_grad, taps, rows_here, cols_here, True)
    attended16 = jnp.concatenate([out_row, out_col], axis=2)
    out = (attended16.astype(jnp.float32) + lepe).astype(jnp.bfloat16)
    dquery = jnp.concatenate([dq_row, dq_col], axis=2)
    dkey = jnp.concatenate([dk_row, dk_col], axis=2)
    dvalue_attn = jnp.concatenate([dv_row, dv_col], axis=2)
    dvalue = (dvalue_attn.astype(jnp.float32) + back_conv).astype(jnp.bfloat16)
    return (out, dquery, dkey, dvalue)


SUB = 8
VMEM_LIMIT = 28 << 20
MESH = pl.DeviceIdType.MESH


def attend(q, k, v, g, allow):
    scale = 1.0 / math.sqrt(HEAD_DIM)
    nt = (((1,), (1,)), ((), ()))
    nn = (((1,), (0,)), ((), ()))
    tn = (((0,), (0,)), ((), ()))
    dot = functools.partial(lax.dot_general, preferred_element_type=jnp.float32)
    s = jnp.where(allow, dot(q, k, nt) * scale, -jnp.inf)
    e = jnp.exp(s - jnp.max(s, axis=-1, keepdims=True))
    w = e * (1.0 / jnp.sum(e, axis=-1, keepdims=True))
    w16 = w.astype(jnp.bfloat16)
    att = dot(w16, v, nn)
    dw = dot(g, v, nt)
    delta = jnp.sum(g.astype(jnp.float32) * att, axis=-1, keepdims=True)
    ds = (w * (dw - delta) * scale).astype(jnp.bfloat16)
    return att, dot(ds, k, nn), dot(ds, q, tn), dot(w16, g, tn)


def dots():
    dot = functools.partial(lax.dot_general, preferred_element_type=jnp.float32)
    return (
        functools.partial(dot, dimension_numbers=(((1,), (1,)), ((), ()))),
        functools.partial(dot, dimension_numbers=(((1,), (0,)), ((), ()))),
        functools.partial(dot, dimension_numbers=(((0,), (0,)), ((), ()))),
    )


def softmax(q, k, allow):
    nt, _, _ = dots()
    s = jnp.where(allow, nt(q, k) * (1.0 / math.sqrt(HEAD_DIM)), -jnp.inf)
    e = jnp.exp(s - jnp.max(s, axis=-1, keepdims=True))
    return e * (1.0 / jnp.sum(e, axis=-1, keepdims=True))


def layer_kernel(dims, q_hbm, k_hbm, v_hbm, g_hbm, taps_hbm, row_hbm, col_hbm, ret, *rest):
    R, C, rows, groups, width = dims
    colbuf, colout, rowbuf, rowout, ext, conv, hop, land, weights, attended, spill, spilled = rest[:12]
    sent, came, here_in, ends_in, lines_in, late_in, taps, row_mask, col_mask = rest[12:]
    half = width // 2
    share = half // C
    heads = half // HEAD_DIM
    me = lax.axis_index("rows")
    mc = lax.axis_index("cols")
    inputs = (q_hbm, k_hbm, v_hbm, g_hbm)
    f32 = jnp.float32
    first, second = pl.ds(0, half), pl.ds(half, half)

    def lanes(start, size):
        return pl.ds(pl.multiple_of(start, 128), size)

    def send(src, dst, send_sem, recv_sem, target):
        return pltpu.make_async_remote_copy(
            src_ref=src, dst_ref=dst, send_sem=send_sem, recv_sem=recv_sem,
            device_id=target, device_id_type=MESH)

    col_sent, back_sent, row_sent, row_back_sent, near_sent, cross_sent, far_sent, pass_sent, pass_far_sent, border_sent, right_sent, left_sent, spill_sent = (
        sent.at[i] for i in range(13))
    col_came = [came.at[t] for t in range(4)]
    back_came = [came.at[4], came.at[5], came.at[5], came.at[6]]
    row_came, hop_came, hop_far_came, near_came, cross_came, right_came, left_came, spill_came = (came.at[7 + i] for i in range(8))

    def drain(semaphore, ref):
        pltpu.make_async_copy(ref, ref, semaphore).wait()

    def home(t):
        return land.at[t // 3] if t in (0, 3) else ret.at[t]

    def col_in(t, p, slot):
        return send(inputs[t].at[:, p, :, second], colbuf.at[t, slot],
                    col_sent, col_came[t], {"rows": p})

    def col_back(t, p, slot):
        if t == 1:
            pair = pl.ds(1, 2)
            src, dst = colout.at[pair, p], ret.at[pair, :, slot, :, second]
        else:
            src, dst = colout.at[t, p], land.at[t // 3, :, slot, :, second]
        return send(src, dst, back_sent, back_came[t], {"rows": p})

    def row_in(t, p, slot):
        return send(inputs[t].at[:, :, :, lanes(p * share, share)], rowbuf.at[t, :, slot],
                    row_sent, row_came, {"cols": p})

    def row_back(t, p, slot):
        return send(rowout.at[t, :, p], home(t).at[:, :, :, lanes(slot * share, share)],
                    row_back_sent, back_came[t], {"cols": p})

    odd = lax.rem(me, 2)
    sign = 2 * odd - 1
    crosses = jnp.logical_and(me + sign >= 0, me + sign < R)
    relays = jnp.logical_and(me - 2 * sign >= 0, me - 2 * sign < R)
    inner = pl.ds(1, groups)
    even_slot, odd_slot = (1 - odd) * (rows + 1), odd * (rows + 1)
    mid = R // 2
    side = me // mid
    gate = mid - 1 + side
    at_gate = me == gate
    beside_gate = me - sign == gate
    shares = (6 * half // 8, 5 * half // 8)
    room = half - min(shares)
    base = side * mid
    away = jnp.logical_not(at_gate)
    has_right, has_left = mc < C - 1, mc > 0

    def by_side(act):
        for s in range(2):
            pl.when(side == s)(functools.partial(act, shares[s]))

    def cross(t, direct):
        return send(inputs[2 + t].at[odd * (rows - 1), :, :, pl.ds(0, direct)],
                    ext.at[t, even_slot, inner, :, pl.ds(0, direct)], cross_sent, cross_came, {"rows": me + sign})

    def detour(t, direct):
        return send(inputs[2 + t].at[odd * (rows - 1), :, :, pl.ds(direct, half - direct)],
                    hop.at[t, :, :, pl.ds(0, half - direct)], cross_sent, hop_came, {"rows": me - sign})

    def detour_far(t, span):
        return send(inputs[2 + t].at[odd * (rows - 1), span, :, second],
                    hop.at[t, span, :, pl.ds(room, half)], far_sent, hop_far_came, {"rows": me - sign})

    def forward(direct):
        return send(hop.at[:, :, :, pl.ds(0, half - direct)], ext.at[:, odd_slot, inner, :, pl.ds(direct, half - direct)],
                    pass_sent, cross_came, {"rows": me - 2 * sign})

    def forward_far(span):
        return send(hop.at[:, span, :, pl.ds(room, half)], ext.at[:, odd_slot, inner].at[:, span, :, second],
                    pass_far_sent, cross_came, {"rows": me - 2 * sign})

    def near(t):
        return send(inputs[2 + t].at[(1 - odd) * (rows - 1)], ext.at[t, odd_slot, inner],
                    near_sent, near_came, {"rows": me - sign})

    def rightward(t):
        return send(inputs[2 + t].at[:, groups - 1], ext.at[t, pl.ds(1, rows), 0],
                    right_sent, right_came, {"cols": mc + 1})

    def leftward(t):
        return send(inputs[2 + t].at[:, 0], ext.at[t, pl.ds(1, rows), groups + 1],
                    left_sent, left_came, {"cols": mc - 1})

    def corner_right(r):
        return send(ext.at[:, r, groups], ext.at[:, r, 0], right_sent, right_came, {"cols": mc + 1})

    def corner_left(r):
        return send(ext.at[:, r, 1], ext.at[:, r, groups + 1], left_sent, left_came, {"cols": mc - 1})

    border_from = colbuf.at[pl.ds(2, 2), mid - side, side * (rows - 1)]
    border_to = ext.at[:, (1 - side) * (rows + 1), 1 + me, :, second]

    def border():
        return send(border_from, border_to, border_sent, cross_came, {"rows": gate})

    def by_gate(gone, act):
        @pl.when(gone)
        def _():
            act(pl.ds(base, 1))
            act(pl.ds(base + mid - 1, 1))

        pl.when(jnp.logical_not(gone))(lambda: act(pl.ds(0, groups)))

    def drain_far(gone, semaphore):
        pl.when(gone)(lambda: drain(semaphore, hop.at[:, pl.ds(0, 2), :, pl.ds(room, half)]))
        pl.when(jnp.logical_not(gone))(lambda: drain(semaphore, hop.at[:, :, :, pl.ds(room, half)]))

    def spill_copy(p):
        return send(spill.at[:, p - base], spilled, spill_sent, spill_came, {"rows": p})

    def others_on(here, count, act, spread=False):
        def step(n, carry):
            d = n + 1
            if spread:
                d = count // 2 + jnp.where(lax.rem(n, 2) == 0, d // 2, -(d // 2))
            act(lax.rem(here + d, count))
            return carry

        lax.fori_loop(0, count - 1, step, 0)

    each_row = functools.partial(others_on, me, R)
    each_col = functools.partial(others_on, mc, C)

    quarter = R // 4
    in_mid = jnp.logical_and(me >= quarter, me < R - quarter)
    far_mid = mid - side * quarter
    near_mid = quarter + side * quarter
    far_end, near_end = (1 - side) * (R - quarter), side * (R - quarter)
    early = jnp.logical_and(in_mid, me == near_mid)
    barrier = pltpu.get_barrier_semaphore()

    def group(bases, act):
        def step(n, carry):
            base = bases[-1]
            for i in range(len(bases) - 1, 0, -1):
                base = jnp.where(n < i * quarter, bases[i - 1], base)
            p = base + lax.rem(n, quarter)
            pl.when(p != me)(lambda: act(p))
            return carry

        lax.fori_loop(0, len(bases) * quarter, step, 0)

    def tell(semaphore, target):
        pl.semaphore_signal(semaphore, inc=1, device_id=target, device_id_type=MESH)

    @pl.when(in_mid)
    def _():
        @pl.when(early)
        def _():
            group((far_mid, near_mid, far_end, near_end), lambda p: tell(barrier, {"rows": p}))
            pl.semaphore_wait(barrier, 1)

        @pl.when(jnp.logical_not(early))
        def _():
            for start in (far_mid, near_mid):
                for j in range(1, quarter):
                    @pl.when(start + j != me)
                    def _(p=start + j):
                        tell(barrier, {"rows": p})
            group((far_end, near_end), lambda p: tell(barrier, {"rows": p}))
            pl.semaphore_wait(barrier, mid - 1)
            tell(late_in, {"rows": far_mid})
            tell(late_in, {"rows": near_mid})

    @pl.when(jnp.logical_not(in_mid))
    def _():
        group((far_end, near_end), lambda p: tell(barrier, {"rows": p}))
        each_col(lambda p: tell(barrier, {"cols": p}))
        pl.semaphore_wait(barrier, R - 1 + C - 1)
        each_col(lambda p: tell(lines_in, {"cols": p}))

    def send_cols(kinds, bases):
        for t in kinds:
            group(bases, lambda p: col_in(t, p, me).start())

    @pl.when(early)
    def _():
        for t in (0, 1):
            col_in(t, far_mid, me).start()
        pl.semaphore_wait(late_in, mid - 2)
        for start in (far_mid, near_mid):
            for j in range(1, quarter):
                for t in (0, 1):
                    col_in(t, start + j, me).start()

    @pl.when(jnp.logical_not(early))
    def _():
        send_cols((0, 1), (far_mid, near_mid))

    @pl.when(jnp.logical_not(in_mid))
    def _():
        pl.semaphore_wait(lines_in, C - 1)
        group((far_mid, near_mid), lambda p: tell(ends_in, {"rows": p}))

    @pl.when(in_mid)
    def _():
        pl.semaphore_wait(ends_in, 2 * quarter)

    send_cols((0, 1), (far_end, near_end))
    send_cols((2, 3), (far_mid, far_end, near_mid, near_end))

    def send_halo():
        @pl.when(crosses)
        def _():
            for t in range(2):
                pl.when(at_gate)(lambda: by_side(lambda direct: detour(t, direct).start()))
                by_gate(at_gate, lambda span: detour_far(t, span).start())
                pl.when(at_gate)(lambda: by_side(lambda direct: cross(t, direct).start()))
                pl.when(away)(lambda: cross(t, half).start())

        for t in range(2):
            near(t).start()

    def send_sides():
        @pl.when(has_right)
        def _():
            for t in range(2):
                rightward(t).start()

        @pl.when(has_left)
        def _():
            for t in range(2):
                leftward(t).start()

    def pass_halo():
        @pl.when(relays)
        def _():
            def hand_on(direct):
                drain(hop_came, hop.at[:, :, :, pl.ds(0, half - direct)])
                forward(direct).start()

            pl.when(beside_gate)(lambda: by_side(hand_on))

            drain_far(beside_gate, hop_far_came)
            by_gate(beside_gate, lambda span: forward_far(span).start())

    def send_rows(t):
        each_col(lambda p: row_in(t, p, mc).start(), spread=True)

    for t in range(4):
        send_rows(t)
    send_halo()
    send_sides()

    tables = [
        pltpu.make_async_copy(src, dst, here_in.at[i])
        for i, (src, dst) in enumerate(((taps_hbm, taps), (row_hbm, row_mask), (col_hbm, col_mask)))
    ]
    for c in tables:
        c.start()
    for t in range(4):
        pltpu.make_async_copy(inputs[t].at[:, :, :, lanes(mc * share, share)], rowbuf.at[t, :, mc], row_came).start()
        pltpu.make_async_copy(inputs[t].at[:, me, :, second], colbuf.at[t, me], col_came[t]).start()
    for t in range(2):
        pltpu.make_async_copy(inputs[2 + t], ext.at[t, pl.ds(1, rows), inner], here_in.at[3]).start()
    for edge, area in (
        (me == 0, (slice(None), 0, inner)),
        (me == R - 1, (slice(None), rows + 1, inner)),
        (mc == 0, (slice(None), slice(None), 0)),
        (mc == C - 1, (slice(None), slice(None), groups + 1)),
    ):
        @pl.when(edge)
        def _(area=area):
            for t in range(2):
                view = ext.at[(t,) + area[1:]]
                view[...] = jnp.zeros(view.shape, view.dtype)

    @pl.when(at_gate)
    def _():
        for t in range(2):
            view = ext.at[t, (1 - side) * (rows + 1), pl.ds(1 + mid - base + 1, mid - 2), :, second]
            view[...] = jnp.zeros(view.shape, view.dtype)
    for c in tables:
        c.wait()
    drain(here_in.at[3], ext.at[:, pl.ds(1, rows), inner])

    def spill_step(n, carry):
        cols = lanes(half + n * 128, 128)
        taps_here = taps[:, cols].astype(f32)
        for t in range(2):
            source = ext[t, rows - side * (rows - 1), pl.ds(1 + base + 1, mid - 2), :, cols].astype(f32)
            edge = jnp.zeros((2 * SUB, 128), f32)
            line = jnp.concatenate([edge, source.reshape((mid - 2) * SUB, 128), edge], axis=0)
            total = jnp.zeros((mid * SUB, 128), f32)
            for b in range(3):
                above, below = (b, 6 + b) if t == 0 else (8 - b, 2 - b)
                tap = jnp.where(side == 1, taps_here[below : below + 1], taps_here[above : above + 1])
                total = total + tap * line[SUB + b - 1 : SUB + b - 1 + mid * SUB]
            spill[t, :, :, lanes(n * 128, 128)] = total.reshape(mid, SUB, 128)
        return carry

    @pl.when(at_gate)
    def _():
        lax.fori_loop(0, half // 128, spill_step, 0)
        pltpu.make_async_copy(spill.at[:, me - base], spilled, spill_came).start()
        for j in range(mid):
            @pl.when(base + j != me)
            def _(p=base + j):
                spill_copy(p).start()

    length = R * rows * SUB
    col_size = length // COL_BLOCKS
    key_pos = lax.broadcasted_iota(jnp.int32, (SUB, length), 1)
    lane_col = lax.broadcasted_iota(jnp.int32, (SUB, length), 0)
    block = jnp.where(lax.rem(key_pos, SUB) == lane_col, key_pos // col_size, -1)
    col_tables = []
    for b in range(COL_BLOCKS):
        table = jnp.zeros((SUB, length), jnp.int32)
        for c in range(SUB):
            for j in range(COL_BLOCKS):
                here = jnp.logical_and(lane_col == c, block == j)
                table = jnp.where(here, col_mask[b, j, me * SUB + c], table)
        col_tables.append(table)

    pass_halo()

    drain(row_came, rowbuf)
    tokens = C * groups * SUB

    def row_step(n, carry):
        i, h = n // (share // HEAD_DIM), lax.rem(n, share // HEAD_DIM)
        cols = lanes(h * HEAD_DIM, HEAD_DIM)
        x = [rowbuf[t, i, :, :, :, cols].astype(f32).reshape(tokens, HEAD_DIM).astype(jnp.bfloat16) for t in range(4)]
        size = tokens // SHEET_ROW_BLOCKS
        place = lax.broadcasted_iota(jnp.int32, (SUB, tokens), 1) // size
        bands = []
        for b in range(SHEET_ROW_BLOCKS):
            table = jnp.zeros((SUB, tokens), jnp.int32)
            for j in range(SHEET_ROW_BLOCKS):
                table = jnp.where(place == j, row_mask[b, j, i], table)
            bands.append(jnp.broadcast_to(table[None], (size // SUB, SUB, tokens)).reshape(size, tokens))
        allow = jnp.concatenate(bands, axis=0) > 0
        for t, y in enumerate(attend(*x, allow)):
            rowout[t, i, :, :, :, cols] = y.reshape(C, groups, SUB, HEAD_DIM).astype(jnp.bfloat16)
        return carry

    lax.fori_loop(0, rows * (share // HEAD_DIM), row_step, 0)
    for t in (0, 3, 1, 2):
        each_col(lambda p: row_back(t, p, mc).start(), spread=True)
        pltpu.make_async_copy(rowout.at[t, :, mc], home(t).at[:, :, :, lanes(mc * share, share)], back_came[t]).start()

    nt, nn, tn = dots()

    def arrived(t):
        drain(col_came[t], colbuf.at[t])

    def give_back(t):
        @pl.when(side == 1)
        def _():
            each_row(lambda p: col_back(t, p, me).start(), spread=True)

        @pl.when(side == 0)
        def _():
            def step(n, carry):
                i = n // 2
                p = jnp.where(lax.rem(n, 2) == 0, mid + lax.rem(i + 2, mid), lax.rem(me + i + 1, mid))
                col_back(t, p, me).start()
                return carry

            lax.fori_loop(0, R - 1, step, 0)

        for u in (1, 2) if t == 1 else (t,):
            pltpu.make_async_copy(colout.at[u, me], home(u).at[:, me, :, second], back_came[u]).start()

    def column(t, h):
        return colbuf[t, :, :, :, lanes(h * HEAD_DIM, HEAD_DIM)].astype(f32).reshape(length, HEAD_DIM).astype(jnp.bfloat16)

    def give(t, h, y):
        colout[t, :, :, :, lanes(h * HEAD_DIM, HEAD_DIM)] = y.reshape(R, rows, SUB, HEAD_DIM).astype(jnp.bfloat16)

    def weigh(h, carry):
        allow = jnp.concatenate(
            [jnp.broadcast_to(t[None], (col_size // SUB, SUB, length)).reshape(col_size, length) for t in col_tables], axis=0) > 0
        weights[h] = softmax(column(0, h), column(1, h), allow)
        return carry

    def forward_step(h, carry):
        att = nn(weights[h].astype(jnp.bfloat16), column(2, h))
        attended[h] = att
        give(0, h, att)
        return carry

    def value_step(h, carry):
        give(3, h, tn(weights[h].astype(jnp.bfloat16), column(3, h)))
        return carry

    def score_step(h, carry):
        g = column(3, h)
        delta = jnp.sum(g.astype(f32) * attended[h], axis=-1, keepdims=True)
        ds = (weights[h] * (nt(g, column(2, h)) - delta) * (1.0 / math.sqrt(HEAD_DIM))).astype(jnp.bfloat16)
        give(1, h, nn(ds, column(1, h)))
        give(2, h, tn(ds, column(0, h)))
        return carry

    arrived(0)
    arrived(1)
    lax.fori_loop(0, heads, weigh, 0)
    arrived(2)
    lax.fori_loop(0, heads, forward_step, 0)

    def add_spill(t, u):
        place = colout.at[t, mid - side, side * (rows - 1)]
        place[...] = (place[...].astype(f32) + spilled[u]).astype(jnp.bfloat16)

    drain(spill_came, spilled)
    add_spill(0, 0)
    give_back(0)
    arrived(3)

    @pl.when(away)
    def _():
        border().start()

    @pl.when(at_gate)
    def _():
        pltpu.make_async_copy(border_from, border_to, cross_came).start()

    lax.fori_loop(0, heads, value_step, 0)
    add_spill(3, 1)
    give_back(3)

    drain(near_came, ext.at[:, even_slot, inner])

    @pl.when(crosses)
    def _():
        pl.when(at_gate)(lambda: drain(cross_came, ext.at[:, odd_slot, pl.ds(0, (groups + mid + 2) // 2)]))
        pl.when(away)(lambda: drain(cross_came, ext.at[:, odd_slot, inner]))

    for r in (0, rows + 1):
        @pl.when(has_right)
        def _(r=r):
            corner_right(r).start()

        @pl.when(has_left)
        def _(r=r):
            corner_left(r).start()

    lax.fori_loop(0, heads, score_step, 0)
    give_back(1)

    @pl.when(has_left)
    def _():
        drain(right_came, ext.at[:, :, 0])

    @pl.when(has_right)
    def _():
        drain(left_came, ext.at[:, :, groups + 1])

    long = groups * SUB

    def conv_step(n, carry):
        cols = lanes(n * 128, 128)
        taps_here = taps[:, cols].astype(f32)
        for t in range(2):
            sums = [None] * rows
            for r in range(rows + 2):
                line = ext[t, r, :, :, cols].astype(f32).reshape(long + 2 * SUB, 128)
                for b in range(3):
                    seen = line[SUB + b - 1 : SUB + b - 1 + long]
                    for a in range(3):
                        o = r - a
                        if 0 <= o < rows:
                            tap = 3 * a + b if t == 0 else 8 - 3 * a - b
                            term = taps_here[tap : tap + 1] * seen
                            sums[o] = term if sums[o] is None else sums[o] + term
            for o in range(rows):
                conv[t, o, :, :, cols] = sums[o].reshape(groups, SUB, 128)
        return carry

    lax.fori_loop(0, width // 128, conv_step, 0)

    drain(col_sent, colbuf.at[:, pl.ds(0, R - 1)])
    for semaphore in (row_sent, row_back_sent):
        drain(semaphore, rowbuf.at[:, :, pl.ds(0, C - 1)])
    drain(near_sent, ext.at[:, 0, inner])

    @pl.when(crosses)
    def _():
        drain(cross_sent, ext.at[:, 0, inner, :, first])
        drain_far(at_gate, far_sent)

    @pl.when(relays)
    def _():
        pl.when(beside_gate)(lambda: by_side(lambda direct: drain(pass_sent, hop.at[:, :, :, pl.ds(0, half - direct)])))
        drain_far(beside_gate, pass_far_sent)

    @pl.when(away)
    def _():
        drain(border_sent, border_from)

    @pl.when(at_gate)
    def _():
        drain(spill_sent, spill.at[:, pl.ds(0, mid - 1)])

    @pl.when(has_right)
    def _():
        drain(right_sent, ext.at[:, :, 0])

    @pl.when(has_left)
    def _():
        drain(left_sent, ext.at[:, :, 0])

    stored = []
    for t in range(2):
        drain(back_came[3 * t], land.at[t])

        def add_step(n, carry):
            cols = lanes(n * 128, 128)
            land[t, :, :, :, cols] = (land[t, :, :, :, cols].astype(f32) + conv[t, :, :, :, cols]).astype(jnp.bfloat16)
            return carry

        lax.fori_loop(0, width // 128, add_step, 0)
        stored.append(pltpu.make_async_copy(land.at[t], ret.at[3 * t], here_in.at[4 + t]))
        stored[t].start()
    drain(back_sent, colbuf.at[:, pl.ds(0, R - 1)])
    drain(back_came[1], ret.at[pl.ds(1, 2)])
    for c in stored:
        c.wait()


def finish_kernel(ret, *rest):
    for t in range(4):
        pltpu.make_async_copy(ret.at[t], rest[t], rest[4]).start()
    pltpu.make_async_copy(ret, ret, rest[4]).wait()


def fused_body(query, key, value, cotangent, conv_weight, row_mask, col_mask):
    rows, cols_here, width = query.shape
    R, C = lax.axis_size("rows"), lax.axis_size("cols")
    groups = cols_here // SUB
    half = width // 2
    share = half // C
    views = [x.reshape(rows, groups, SUB, width) for x in (query, key, value, cotangent)]
    bf16 = jnp.bfloat16
    any_spec = pl.BlockSpec(memory_space=pl.ANY)
    dma = pltpu.SemaphoreType.DMA
    heads = half // HEAD_DIM
    length = R * rows * SUB
    row_table, col_table = jnp.transpose(row_mask, (1, 2, 0)), jnp.transpose(col_mask, (1, 2, 0))
    ret = pl.pallas_call(
        functools.partial(layer_kernel, (R, C, rows, groups, width)),
        out_shape=jax.ShapeDtypeStruct((4, rows, groups, SUB, width), bf16),
        in_specs=[any_spec] * 7,
        out_specs=any_spec,
        scratch_shapes=[
            pltpu.VMEM((4, R, rows, SUB, half), bf16),
            pltpu.VMEM((4, R, rows, SUB, half), bf16),
            pltpu.VMEM((4, rows, C, groups, SUB, share), bf16),
            pltpu.VMEM((4, rows, C, groups, SUB, share), bf16),
            pltpu.VMEM((2, rows + 2, groups + 2, SUB, width), bf16),
            pltpu.VMEM((2, rows, groups, SUB, width), jnp.float32),
            pltpu.VMEM((2, groups, SUB, half + half - 5 * half // 8), bf16),
            pltpu.VMEM((2, rows, groups, SUB, width), bf16),
            pltpu.VMEM((heads, length, length), jnp.float32),
            pltpu.VMEM((heads, length, HEAD_DIM), jnp.float32),
            pltpu.VMEM((2, R // 2, SUB, half), jnp.float32),
            pltpu.VMEM((2, SUB, half), jnp.float32),
            dma((13,)), dma((15,)), dma((6,)), pltpu.SemaphoreType.REGULAR, pltpu.SemaphoreType.REGULAR, pltpu.SemaphoreType.REGULAR,
            pltpu.VMEM(conv_weight.shape, bf16), pltpu.SMEM(row_table.shape, jnp.int32), pltpu.SMEM(col_table.shape, jnp.int32),
        ],
        compiler_params=pltpu.CompilerParams(collective_id=0, has_side_effects=True, vmem_limit_bytes=VMEM_LIMIT),
    )(*[pltpu.with_memory_space_constraint(x, pltpu.HBM) for x in (*views, conv_weight, row_table, col_table)])
    outs = pl.pallas_call(
        finish_kernel,
        out_shape=[jax.ShapeDtypeStruct((rows, groups, SUB, width), bf16)] * 4,
        in_specs=[any_spec],
        out_specs=[any_spec] * 4,
        scratch_shapes=[dma(())],
        compiler_params=pltpu.CompilerParams(vmem_limit_bytes=1 << 20),
    )(ret)
    return tuple(x.reshape(query.shape) for x in outs)


def any_body(query, key, value, cotangent, conv_weight, row_mask, col_mask):
    rows, cols_here, width = query.shape
    R, C = lax.axis_size("rows"), lax.axis_size("cols")
    fits = R % 8 == 0 and cols_here == R * SUB and (width // 2) % (C * HEAD_DIM) == 0 and (width // 2) % (8 * HEAD_DIM) == 0
    chosen = fused_body if fits else body
    return chosen(query, key, value, cotangent, conv_weight, row_mask, col_mask)


def solution(mesh):
    return jax.shard_map(
        any_body,
        mesh=mesh,
        in_specs=(
            P("rows", "cols", None),
            P("rows", "cols", None),
            P("rows", "cols", None),
            P("rows", "cols", None),
            P(),
            P("rows", None, None),
            P("cols", None, None),
        ),
        out_specs=(
            P("rows", "cols", None),
            P("rows", "cols", None),
            P("rows", "cols", None),
            P("rows", "cols", None),
        ),
        check_vma=False,
    )
```

```python
import functools
import math

import jax
import jax.numpy as jnp
from jax import lax
from jax.experimental import pallas as pl
from jax.experimental.pallas import tpu as pltpu
from jax.sharding import PartitionSpec as P

HEAD_DIM = 128
SHEET_ROW_BLOCKS = 2
COL_BLOCKS = 3


def padded(array, sides, width):
    for axis, dim in sides:
        devices, length = (lax.axis_size(axis), array.shape[dim])
        up = [(i, (i + 1) % devices) for i in range(devices - 1)]
        down = [(j, i) for i, j in up]
        last = lax.slice_in_dim(array, length - width, length, axis=dim)
        leading = lax.slice_in_dim(array, 0, width, axis=dim)
        before = lax.ppermute(last, axis, up)
        after = lax.ppermute(leading, axis, down)
        array = jnp.concatenate([before, array, after], axis=dim)
    return array


def block_allow(block_mask_table, query_pos, key_pos, block_len, block_count):
    labels = jnp.arange(block_count)
    query_onehot_rows = (query_pos[:, None] // block_len == labels[None, :]).astype(jnp.float32)
    key_onehot_rows = (key_pos[:, None] // block_len == labels[None, :]).astype(jnp.float32)
    merged_links = jnp.einsum(
        "xv,zvs,hs->zxh", query_onehot_rows, block_mask_table.astype(jnp.float32), key_onehot_rows
    )
    return merged_links > 0.5


def line_attention(query_part, key_part, value_part, grad_part, allowed, layout):
    if layout == "bq":
        query_form = "bqhd"
        key_layout_shape = "bkhd"
    else:
        query_form = "qbhd"
        key_layout_shape = "kbhd"
    score_scale = 1.0 / math.sqrt(query_part.shape[-1])
    pair_form = query_form + "," + key_layout_shape + "->bhqk"
    scores = (
        jnp.einsum(pair_form, query_part, key_part, preferred_element_type=jnp.float32)
        * score_scale
    )
    scores = jnp.where(allowed[:, None], scores, -jnp.inf)
    highest = jnp.max(scores, axis=-1, keepdims=True)
    weights = jnp.exp(scores - highest)
    weights = weights / jnp.sum(weights, axis=-1, keepdims=True)
    rounded = weights.astype(jnp.bfloat16)
    attended = jnp.einsum(
        "bhqk," + key_layout_shape + "->" + query_form,
        rounded,
        value_part,
        preferred_element_type=jnp.float32,
    )
    dweights = jnp.einsum(pair_form, grad_part, value_part, preferred_element_type=jnp.float32)
    delta = jnp.sum(grad_part.astype(jnp.float32) * attended, axis=-1)
    if layout == "bq":
        delta = jnp.transpose(delta, (0, 2, 1))
    else:
        delta = jnp.transpose(delta, (1, 2, 0))
    dscores = (weights * (dweights - delta[..., None]) * score_scale).astype(jnp.bfloat16)
    dquery = jnp.einsum(
        "bhqk," + key_layout_shape + "->" + query_form,
        dscores,
        key_part,
        preferred_element_type=jnp.float32,
    )
    dkey = jnp.einsum(
        "bhqk," + query_form + "->" + key_layout_shape,
        dscores,
        query_part,
        preferred_element_type=jnp.float32,
    )
    dvalue = jnp.einsum(
        "bhqk," + query_form + "->" + key_layout_shape,
        rounded,
        grad_part,
        preferred_element_type=jnp.float32,
    )
    return (attended, dquery, dkey, dvalue)


def depthwise(padded_field, taps, rows_count, cols_count, reverse_taps):
    summed = jnp.zeros((rows_count, cols_count, taps.shape[1]), jnp.float32)
    for row_offset_start in range(3):
        for offset_col in range(3):
            if reverse_taps:
                start_row = 2 - row_offset_start
                start_col = 2 - offset_col
            else:
                start_row = row_offset_start
                start_col = offset_col
            window = padded_field[
                start_row : start_row + rows_count, start_col : start_col + cols_count
            ]
            summed = summed + taps[row_offset_start * 3 + offset_col] * window.astype(jnp.float32)
    return summed


def body(query, key, value, cotangent, conv_weight, row_mask, col_mask):
    rows_here, cols_here, width = query.shape
    half_width = width // 2
    head_groups = half_width // HEAD_DIM
    row_devices = lax.axis_size("rows")
    col_devices = lax.axis_size("cols")
    sheet_rows = rows_here * row_devices
    sheet_cols = cols_here * col_devices
    taps = conv_weight.astype(jnp.float32)
    padded_value = padded(value, (("rows", 0), ("cols", 1)), 1)
    padded_grad = padded(cotangent, (("rows", 0), ("cols", 1)), 1)
    row_len = sheet_cols // SHEET_ROW_BLOCKS
    keys_row, values_row = (
        lax.all_gather(key[:, :, :half_width], "cols", axis=1, tiled=True),
        lax.all_gather(value[:, :, :half_width], "cols", axis=1, tiled=True),
    )
    col_start = lax.axis_index("cols") * cols_here
    allowed = block_allow(
        row_mask,
        col_start + jnp.arange(cols_here),
        jnp.arange(sheet_cols),
        row_len,
        SHEET_ROW_BLOCKS,
    )
    local_shape = (rows_here, cols_here, head_groups, HEAD_DIM)
    whole_shape = (rows_here, sheet_cols, head_groups, HEAD_DIM)
    results = line_attention(
        query[:, :, :half_width].reshape(local_shape),
        keys_row.reshape(whole_shape),
        values_row.reshape(whole_shape),
        cotangent[:, :, :half_width].reshape(local_shape),
        allowed,
        "bq",
    )
    key_terms = results[2].reshape(rows_here, sheet_cols, half_width)
    value_terms = results[3].reshape(rows_here, sheet_cols, half_width)
    key_grads, value_grads = (
        lax.psum_scatter(key_terms, "cols", scatter_dimension=1, tiled=True),
        lax.psum_scatter(value_terms, "cols", scatter_dimension=1, tiled=True),
    )
    out_row = results[0].reshape(rows_here, cols_here, half_width).astype(jnp.bfloat16)
    dq_row = results[1].reshape(rows_here, cols_here, half_width).astype(jnp.bfloat16)
    dk_row = key_grads.astype(jnp.bfloat16)
    dv_row = value_grads.astype(jnp.bfloat16)
    columns_each = cols_here // row_devices
    moved = (
        lax.all_to_all(query[:, :, half_width:], "rows", split_axis=1, concat_axis=0, tiled=True),
        lax.all_to_all(key[:, :, half_width:], "rows", split_axis=1, concat_axis=0, tiled=True),
        lax.all_to_all(value[:, :, half_width:], "rows", split_axis=1, concat_axis=0, tiled=True),
        lax.all_to_all(
            cotangent[:, :, half_width:], "rows", split_axis=1, concat_axis=0, tiled=True
        ),
    )
    column_shape = (sheet_rows, columns_each, head_groups, HEAD_DIM)
    my_tables = lax.dynamic_slice_in_dim(
        col_mask, lax.axis_index("rows") * columns_each, columns_each, 0
    )
    col_len = sheet_rows // COL_BLOCKS
    positions = jnp.arange(sheet_rows)
    col_allowed = block_allow(my_tables, positions, positions, col_len, COL_BLOCKS)
    col_results = line_attention(
        moved[0].reshape(column_shape),
        moved[1].reshape(column_shape),
        moved[2].reshape(column_shape),
        moved[3].reshape(column_shape),
        col_allowed,
        "qb",
    )
    column_flat = (sheet_rows, columns_each, half_width)
    col_pieces = [piece.reshape(column_flat).astype(jnp.bfloat16) for piece in col_results]
    out_col, dq_col, dk_col, dv_col = (
        lax.all_to_all(col_pieces[0], "rows", split_axis=0, concat_axis=1, tiled=True),
        lax.all_to_all(col_pieces[1], "rows", split_axis=0, concat_axis=1, tiled=True),
        lax.all_to_all(col_pieces[2], "rows", split_axis=0, concat_axis=1, tiled=True),
        lax.all_to_all(col_pieces[3], "rows", split_axis=0, concat_axis=1, tiled=True),
    )
    lepe = depthwise(padded_value, taps, rows_here, cols_here, False)
    back_conv = depthwise(padded_grad, taps, rows_here, cols_here, True)
    attended16 = jnp.concatenate([out_row, out_col], axis=2)
    out = (attended16.astype(jnp.float32) + lepe).astype(jnp.bfloat16)
    dquery = jnp.concatenate([dq_row, dq_col], axis=2)
    dkey = jnp.concatenate([dk_row, dk_col], axis=2)
    dvalue_attn = jnp.concatenate([dv_row, dv_col], axis=2)
    dvalue = (dvalue_attn.astype(jnp.float32) + back_conv).astype(jnp.bfloat16)
    return (out, dquery, dkey, dvalue)


SUB = 8
VMEM_LIMIT = 28 << 20
MESH = pl.DeviceIdType.MESH


def attend(q, k, v, g, allow):
    scale = 1.0 / math.sqrt(HEAD_DIM)
    nt = (((1,), (1,)), ((), ()))
    nn = (((1,), (0,)), ((), ()))
    tn = (((0,), (0,)), ((), ()))
    dot = functools.partial(lax.dot_general, preferred_element_type=jnp.float32)
    s = jnp.where(allow, dot(q, k, nt) * scale, -jnp.inf)
    e = jnp.exp(s - jnp.max(s, axis=-1, keepdims=True))
    w = e * (1.0 / jnp.sum(e, axis=-1, keepdims=True))
    w16 = w.astype(jnp.bfloat16)
    att = dot(w16, v, nn)
    dw = dot(g, v, nt)
    delta = jnp.sum(g.astype(jnp.float32) * att, axis=-1, keepdims=True)
    ds = (w * (dw - delta) * scale).astype(jnp.bfloat16)
    return att, dot(ds, k, nn), dot(ds, q, tn), dot(w16, g, tn)


def dots():
    dot = functools.partial(lax.dot_general, preferred_element_type=jnp.float32)
    return (
        functools.partial(dot, dimension_numbers=(((1,), (1,)), ((), ()))),
        functools.partial(dot, dimension_numbers=(((1,), (0,)), ((), ()))),
        functools.partial(dot, dimension_numbers=(((0,), (0,)), ((), ()))),
    )


def softmax(q, k, allow):
    nt, _, _ = dots()
    s = jnp.where(allow, nt(q, k) * (1.0 / math.sqrt(HEAD_DIM)), -jnp.inf)
    e = jnp.exp(s - jnp.max(s, axis=-1, keepdims=True))
    return e * (1.0 / jnp.sum(e, axis=-1, keepdims=True))


def layer_kernel(dims, q_hbm, k_hbm, v_hbm, g_hbm, taps_hbm, row_hbm, col_hbm, ret, *rest):
    R, C, rows, groups, width = dims
    colbuf, colout, rowbuf, rowout, ext, conv, hop, land, weights, attended, spill, spilled = rest[:12]
    sent, came, here_in, ends_in, lines_in, late_in, taps, row_mask, col_mask = rest[12:]
    half = width // 2
    share = half // C
    heads = half // HEAD_DIM
    me = lax.axis_index("rows")
    mc = lax.axis_index("cols")
    inputs = (q_hbm, k_hbm, v_hbm, g_hbm)
    f32 = jnp.float32
    first, second = pl.ds(0, half), pl.ds(half, half)

    def lanes(start, size):
        return pl.ds(pl.multiple_of(start, 128), size)

    def send(src, dst, send_sem, recv_sem, target):
        return pltpu.make_async_remote_copy(
            src_ref=src, dst_ref=dst, send_sem=send_sem, recv_sem=recv_sem,
            device_id=target, device_id_type=MESH)

    col_sent, row_sent, near_sent, cross_sent, far_sent, pass_sent, pass_far_sent, border_sent, right_sent, left_sent, spill_sent = (
        sent.at[i] for i in range(11))
    col_came = [came.at[t] for t in range(4)]
    back_came = [came.at[4], came.at[5], came.at[5], came.at[6]]
    row_came, hop_came, hop_far_came, near_came, cross_came, right_came, left_came, spill_came = (came.at[7 + i] for i in range(8))

    def drain(semaphore, ref):
        pltpu.make_async_copy(ref, ref, semaphore).wait()

    def home(t):
        return land.at[t // 3] if t in (0, 3) else ret.at[t]

    def col_in(t, p, slot):
        return send(inputs[t].at[:, p, :, second], colbuf.at[t, slot],
                    col_sent, col_came[t], {"rows": p})

    def col_back(t, p, slot):
        if t == 1:
            pair = pl.ds(1, 2)
            src, dst = colout.at[pair, p], ret.at[pair, :, slot, :, second]
        else:
            src, dst = colout.at[t, p], land.at[t // 3, :, slot, :, second]
        return send(src, dst, col_sent, back_came[t], {"rows": p})

    def row_in(t, p, slot):
        return send(inputs[t].at[:, :, :, lanes(p * share, share)], rowbuf.at[t, :, slot],
                    row_sent, row_came, {"cols": p})

    def row_back(t, p, slot):
        return send(rowout.at[t, :, p], home(t).at[:, :, :, lanes(slot * share, share)],
                    row_sent, back_came[t], {"cols": p})

    odd = lax.rem(me, 2)
    sign = 2 * odd - 1
    crosses = jnp.logical_and(me + sign >= 0, me + sign < R)
    relays = jnp.logical_and(me - 2 * sign >= 0, me - 2 * sign < R)
    inner = pl.ds(1, groups)
    even_slot, odd_slot = (1 - odd) * (rows + 1), odd * (rows + 1)
    mid = R // 2
    side = me // mid
    gate = mid - 1 + side
    at_gate = me == gate
    beside_gate = me - sign == gate
    shares = (6 * half // 8, 5 * half // 8)
    room = half - min(shares)
    base = side * mid
    away = jnp.logical_not(at_gate)
    has_right, has_left = mc < C - 1, mc > 0

    def by_side(act):
        for s in range(2):
            pl.when(side == s)(functools.partial(act, shares[s]))

    def cross(t, direct):
        return send(inputs[2 + t].at[odd * (rows - 1), :, :, pl.ds(0, direct)],
                    ext.at[t, even_slot, inner, :, pl.ds(0, direct)], cross_sent, cross_came, {"rows": me + sign})

    def detour(t, direct):
        return send(inputs[2 + t].at[odd * (rows - 1), :, :, pl.ds(direct, half - direct)],
                    hop.at[t, :, :, pl.ds(0, half - direct)], cross_sent, hop_came, {"rows": me - sign})

    def detour_far(t, span):
        return send(inputs[2 + t].at[odd * (rows - 1), span, :, second],
                    hop.at[t, span, :, pl.ds(room, half)], far_sent, hop_far_came, {"rows": me - sign})

    def forward(direct):
        return send(hop.at[:, :, :, pl.ds(0, half - direct)], ext.at[:, odd_slot, inner, :, pl.ds(direct, half - direct)],
                    pass_sent, cross_came, {"rows": me - 2 * sign})

    def forward_far(span):
        return send(hop.at[:, span, :, pl.ds(room, half)], ext.at[:, odd_slot, inner].at[:, span, :, second],
                    pass_far_sent, cross_came, {"rows": me - 2 * sign})

    def near(t):
        return send(inputs[2 + t].at[(1 - odd) * (rows - 1)], ext.at[t, odd_slot, inner],
                    near_sent, near_came, {"rows": me - sign})

    def rightward(t):
        return send(inputs[2 + t].at[:, groups - 1], ext.at[t, pl.ds(1, rows), 0],
                    right_sent, right_came, {"cols": mc + 1})

    def leftward(t):
        return send(inputs[2 + t].at[:, 0], ext.at[t, pl.ds(1, rows), groups + 1],
                    left_sent, left_came, {"cols": mc - 1})

    def corner_right(r):
        return send(ext.at[:, r, groups], ext.at[:, r, 0], right_sent, right_came, {"cols": mc + 1})

    def corner_left(r):
        return send(ext.at[:, r, 1], ext.at[:, r, groups + 1], left_sent, left_came, {"cols": mc - 1})

    border_from = colbuf.at[pl.ds(2, 2), mid - side, side * (rows - 1)]
    border_to = ext.at[:, (1 - side) * (rows + 1), 1 + me, :, second]

    def border():
        return send(border_from, border_to, border_sent, cross_came, {"rows": gate})

    def by_gate(gone, act):
        @pl.when(gone)
        def _():
            act(pl.ds(base, 1))
            act(pl.ds(base + mid - 1, 1))

        pl.when(jnp.logical_not(gone))(lambda: act(pl.ds(0, groups)))

    def drain_far(gone, semaphore):
        pl.when(gone)(lambda: drain(semaphore, hop.at[:, pl.ds(0, 2), :, pl.ds(room, half)]))
        pl.when(jnp.logical_not(gone))(lambda: drain(semaphore, hop.at[:, :, :, pl.ds(room, half)]))

    def spill_copy(p):
        return send(spill.at[:, p - base], spilled, spill_sent, spill_came, {"rows": p})

    def others_on(here, count, act, spread=False):
        def step(n, carry):
            d = n + 1
            if spread:
                d = count // 2 + jnp.where(lax.rem(n, 2) == 0, d // 2, -(d // 2))
            act(lax.rem(here + d, count))
            return carry

        lax.fori_loop(0, count - 1, step, 0)

    each_row = functools.partial(others_on, me, R)
    each_col = functools.partial(others_on, mc, C)

    quarter = R // 4
    in_mid = jnp.logical_and(me >= quarter, me < R - quarter)
    far_mid = mid - side * quarter
    near_mid = quarter + side * quarter
    far_end, near_end = (1 - side) * (R - quarter), side * (R - quarter)
    early = jnp.logical_and(in_mid, me == near_mid)
    barrier = pltpu.get_barrier_semaphore()

    def group(bases, act):
        def step(n, carry):
            base = bases[-1]
            for i in range(len(bases) - 1, 0, -1):
                base = jnp.where(n < i * quarter, bases[i - 1], base)
            p = base + lax.rem(n, quarter)
            pl.when(p != me)(lambda: act(p))
            return carry

        lax.fori_loop(0, len(bases) * quarter, step, 0)

    def tell(semaphore, target):
        pl.semaphore_signal(semaphore, inc=1, device_id=target, device_id_type=MESH)

    @pl.when(in_mid)
    def _():
        @pl.when(early)
        def _():
            group((far_mid, near_mid, far_end, near_end), lambda p: tell(barrier, {"rows": p}))
            pl.semaphore_wait(barrier, 1)

        @pl.when(jnp.logical_not(early))
        def _():
            for start in (far_mid, near_mid):
                for j in range(1, quarter):
                    @pl.when(start + j != me)
                    def _(p=start + j):
                        tell(barrier, {"rows": p})
            group((far_end, near_end), lambda p: tell(barrier, {"rows": p}))
            pl.semaphore_wait(barrier, mid - 1)
            tell(late_in, {"rows": far_mid})
            tell(late_in, {"rows": near_mid})

    @pl.when(jnp.logical_not(in_mid))
    def _():
        group((far_end, near_end), lambda p: tell(barrier, {"rows": p}))
        each_col(lambda p: tell(barrier, {"cols": p}))
        pl.semaphore_wait(barrier, R - 1 + C - 1)
        each_col(lambda p: tell(lines_in, {"cols": p}))

    def send_cols(kinds, bases):
        for t in kinds:
            group(bases, lambda p: col_in(t, p, me).start())

    @pl.when(early)
    def _():
        for t in (0, 1):
            col_in(t, far_mid, me).start()
        pl.semaphore_wait(late_in, mid - 2)
        for start in (far_mid, near_mid):
            for j in range(1, quarter):
                for t in (0, 1):
                    col_in(t, start + j, me).start()

    @pl.when(jnp.logical_not(early))
    def _():
        send_cols((0, 1), (far_mid, near_mid))

    @pl.when(jnp.logical_not(in_mid))
    def _():
        pl.semaphore_wait(lines_in, C - 1)
        group((far_mid, near_mid), lambda p: tell(ends_in, {"rows": p}))

    @pl.when(in_mid)
    def _():
        pl.semaphore_wait(ends_in, 2 * quarter)

    send_cols((0, 1), (far_end, near_end))
    send_cols((2, 3), (far_mid, far_end, near_mid, near_end))

    def send_halo():
        @pl.when(crosses)
        def _():
            for t in range(2):
                pl.when(at_gate)(lambda: by_side(lambda direct: detour(t, direct).start()))
                by_gate(at_gate, lambda span: detour_far(t, span).start())
                pl.when(at_gate)(lambda: by_side(lambda direct: cross(t, direct).start()))
                pl.when(away)(lambda: cross(t, half).start())

        for t in range(2):
            near(t).start()

    def send_sides():
        @pl.when(has_right)
        def _():
            for t in range(2):
                rightward(t).start()

        @pl.when(has_left)
        def _():
            for t in range(2):
                leftward(t).start()

    def pass_halo():
        @pl.when(relays)
        def _():
            def hand_on(direct):
                drain(hop_came, hop.at[:, :, :, pl.ds(0, half - direct)])
                forward(direct).start()

            pl.when(beside_gate)(lambda: by_side(hand_on))

            drain_far(beside_gate, hop_far_came)
            by_gate(beside_gate, lambda span: forward_far(span).start())

    def send_rows(t):
        each_col(lambda p: row_in(t, p, mc).start(), spread=True)

    for t in range(4):
        send_rows(t)
    send_halo()
    send_sides()

    tables = [
        pltpu.make_async_copy(src, dst, here_in.at[i])
        for i, (src, dst) in enumerate(((taps_hbm, taps), (row_hbm, row_mask), (col_hbm, col_mask)))
    ]
    for c in tables:
        c.start()
    for t in range(4):
        pltpu.make_async_copy(inputs[t].at[:, :, :, lanes(mc * share, share)], rowbuf.at[t, :, mc], row_came).start()
        pltpu.make_async_copy(inputs[t].at[:, me, :, second], colbuf.at[t, me], col_came[t]).start()
    for t in range(2):
        pltpu.make_async_copy(inputs[2 + t], ext.at[t, pl.ds(1, rows), inner], here_in.at[3]).start()
    for edge, area in (
        (me == 0, (slice(None), 0, inner)),
        (me == R - 1, (slice(None), rows + 1, inner)),
        (mc == 0, (slice(None), slice(None), 0)),
        (mc == C - 1, (slice(None), slice(None), groups + 1)),
    ):
        @pl.when(edge)
        def _(area=area):
            for t in range(2):
                view = ext.at[(t,) + area[1:]]
                view[...] = jnp.zeros(view.shape, view.dtype)

    @pl.when(at_gate)
    def _():
        for t in range(2):
            view = ext.at[t, (1 - side) * (rows + 1), pl.ds(1 + mid - base + 1, mid - 2), :, second]
            view[...] = jnp.zeros(view.shape, view.dtype)
    for c in tables:
        c.wait()
    drain(here_in.at[3], ext.at[:, pl.ds(1, rows), inner])

    def spill_step(n, carry):
        cols = lanes(half + n * 128, 128)
        taps_here = taps[:, cols].astype(f32)
        for t in range(2):
            source = ext[t, rows - side * (rows - 1), pl.ds(1 + base + 1, mid - 2), :, cols].astype(f32)
            edge = jnp.zeros((2 * SUB, 128), f32)
            line = jnp.concatenate([edge, source.reshape((mid - 2) * SUB, 128), edge], axis=0)
            total = jnp.zeros((mid * SUB, 128), f32)
            for b in range(3):
                above, below = (b, 6 + b) if t == 0 else (8 - b, 2 - b)
                tap = jnp.where(side == 1, taps_here[below : below + 1], taps_here[above : above + 1])
                total = total + tap * line[SUB + b - 1 : SUB + b - 1 + mid * SUB]
            spill[t, :, :, lanes(n * 128, 128)] = total.reshape(mid, SUB, 128)
        return carry

    @pl.when(at_gate)
    def _():
        lax.fori_loop(0, half // 128, spill_step, 0)
        pltpu.make_async_copy(spill.at[:, me - base], spilled, spill_came).start()
        for j in range(mid):
            @pl.when(base + j != me)
            def _(p=base + j):
                spill_copy(p).start()

    length = R * rows * SUB
    col_size = length // COL_BLOCKS
    key_pos = lax.broadcasted_iota(jnp.int32, (SUB, length), 1)
    lane_col = lax.broadcasted_iota(jnp.int32, (SUB, length), 0)
    block = jnp.where(lax.rem(key_pos, SUB) == lane_col, key_pos // col_size, -1)
    col_tables = []
    for b in range(COL_BLOCKS):
        table = jnp.zeros((SUB, length), jnp.int32)
        for c in range(SUB):
            for j in range(COL_BLOCKS):
                here = jnp.logical_and(lane_col == c, block == j)
                table = jnp.where(here, col_mask[b, j, me * SUB + c], table)
        col_tables.append(table)

    pass_halo()

    drain(row_came, rowbuf)
    tokens = C * groups * SUB

    def row_step(n, carry):
        i, h = n // (share // HEAD_DIM), lax.rem(n, share // HEAD_DIM)
        cols = lanes(h * HEAD_DIM, HEAD_DIM)
        x = [rowbuf[t, i, :, :, :, cols].astype(f32).reshape(tokens, HEAD_DIM).astype(jnp.bfloat16) for t in range(4)]
        size = tokens // SHEET_ROW_BLOCKS
        place = lax.broadcasted_iota(jnp.int32, (SUB, tokens), 1) // size
        bands = []
        for b in range(SHEET_ROW_BLOCKS):
            table = jnp.zeros((SUB, tokens), jnp.int32)
            for j in range(SHEET_ROW_BLOCKS):
                table = jnp.where(place == j, row_mask[b, j, i], table)
            bands.append(jnp.broadcast_to(table[None], (size // SUB, SUB, tokens)).reshape(size, tokens))
        allow = jnp.concatenate(bands, axis=0) > 0
        for t, y in enumerate(attend(*x, allow)):
            rowout[t, i, :, :, :, cols] = y.reshape(C, groups, SUB, HEAD_DIM).astype(jnp.bfloat16)
        return carry

    lax.fori_loop(0, rows * (share // HEAD_DIM), row_step, 0)
    for t in (0, 3, 1, 2):
        each_col(lambda p: row_back(t, p, mc).start(), spread=True)
        pltpu.make_async_copy(rowout.at[t, :, mc], home(t).at[:, :, :, lanes(mc * share, share)], back_came[t]).start()

    nt, nn, tn = dots()

    def arrived(t):
        drain(col_came[t], colbuf.at[t])

    def give_back(t):
        @pl.when(side == 1)
        def _():
            each_row(lambda p: col_back(t, p, me).start(), spread=True)

        @pl.when(side == 0)
        def _():
            def step(n, carry):
                i = n // 2
                p = jnp.where(lax.rem(n, 2) == 0, mid + lax.rem(i + 2, mid), lax.rem(me + i + 1, mid))
                col_back(t, p, me).start()
                return carry

            lax.fori_loop(0, R - 1, step, 0)

        for u in (1, 2) if t == 1 else (t,):
            pltpu.make_async_copy(colout.at[u, me], home(u).at[:, me, :, second], back_came[u]).start()

    def column(t, h):
        return colbuf[t, :, :, :, lanes(h * HEAD_DIM, HEAD_DIM)].astype(f32).reshape(length, HEAD_DIM).astype(jnp.bfloat16)

    def give(t, h, y):
        colout[t, :, :, :, lanes(h * HEAD_DIM, HEAD_DIM)] = y.reshape(R, rows, SUB, HEAD_DIM).astype(jnp.bfloat16)

    def weigh(h, carry):
        allow = jnp.concatenate(
            [jnp.broadcast_to(t[None], (col_size // SUB, SUB, length)).reshape(col_size, length) for t in col_tables], axis=0) > 0
        weights[h] = softmax(column(0, h), column(1, h), allow)
        return carry

    def forward_step(h, carry):
        att = nn(weights[h].astype(jnp.bfloat16), column(2, h))
        attended[h] = att
        give(0, h, att)
        return carry

    def value_step(h, carry):
        give(3, h, tn(weights[h].astype(jnp.bfloat16), column(3, h)))
        return carry

    def score_step(h, carry):
        g = column(3, h)
        delta = jnp.sum(g.astype(f32) * attended[h], axis=-1, keepdims=True)
        ds = (weights[h] * (nt(g, column(2, h)) - delta) * (1.0 / math.sqrt(HEAD_DIM))).astype(jnp.bfloat16)
        give(1, h, nn(ds, column(1, h)))
        give(2, h, tn(ds, column(0, h)))
        return carry

    arrived(0)
    arrived(1)
    lax.fori_loop(0, heads, weigh, 0)
    arrived(2)
    lax.fori_loop(0, heads, forward_step, 0)

    def add_spill(t, u):
        place = colout.at[t, mid - side, side * (rows - 1)]
        place[...] = (place[...].astype(f32) + spilled[u]).astype(jnp.bfloat16)

    drain(spill_came, spilled)
    add_spill(0, 0)
    give_back(0)
    arrived(3)

    @pl.when(away)
    def _():
        border().start()

    @pl.when(at_gate)
    def _():
        pltpu.make_async_copy(border_from, border_to, cross_came).start()

    lax.fori_loop(0, heads, value_step, 0)
    add_spill(3, 1)
    give_back(3)

    drain(near_came, ext.at[:, even_slot, inner])

    @pl.when(crosses)
    def _():
        pl.when(at_gate)(lambda: drain(cross_came, ext.at[:, odd_slot, pl.ds(0, (groups + mid + 2) // 2)]))
        pl.when(away)(lambda: drain(cross_came, ext.at[:, odd_slot, inner]))

    for r in (0, rows + 1):
        @pl.when(has_right)
        def _(r=r):
            corner_right(r).start()

        @pl.when(has_left)
        def _(r=r):
            corner_left(r).start()

    lax.fori_loop(0, heads, score_step, 0)
    give_back(1)

    @pl.when(has_left)
    def _():
        drain(right_came, ext.at[:, :, 0])

    @pl.when(has_right)
    def _():
        drain(left_came, ext.at[:, :, groups + 1])

    long = groups * SUB

    def conv_step(n, carry):
        cols = lanes(n * 128, 128)
        taps_here = taps[:, cols].astype(f32)
        for t in range(2):
            sums = [None] * rows
            for r in range(rows + 2):
                line = ext[t, r, :, :, cols].astype(f32).reshape(long + 2 * SUB, 128)
                for b in range(3):
                    seen = line[SUB + b - 1 : SUB + b - 1 + long]
                    for a in range(3):
                        o = r - a
                        if 0 <= o < rows:
                            tap = 3 * a + b if t == 0 else 8 - 3 * a - b
                            term = taps_here[tap : tap + 1] * seen
                            sums[o] = term if sums[o] is None else sums[o] + term
            for o in range(rows):
                conv[t, o, :, :, cols] = sums[o].reshape(groups, SUB, 128)
        return carry

    lax.fori_loop(0, width // 128, conv_step, 0)

    drain(row_sent, conv.at[:, :, pl.ds(0, groups * (C - 1) // C)])
    drain(near_sent, ext.at[:, 0, inner])

    @pl.when(crosses)
    def _():
        drain(cross_sent, ext.at[:, 0, inner, :, first])
        drain_far(at_gate, far_sent)

    @pl.when(relays)
    def _():
        pl.when(beside_gate)(lambda: by_side(lambda direct: drain(pass_sent, hop.at[:, :, :, pl.ds(0, half - direct)])))
        drain_far(beside_gate, pass_far_sent)

    @pl.when(away)
    def _():
        drain(border_sent, border_from)

    @pl.when(at_gate)
    def _():
        drain(spill_sent, spill.at[:, pl.ds(0, mid - 1)])

    @pl.when(has_right)
    def _():
        drain(right_sent, ext.at[:, :, 0])

    @pl.when(has_left)
    def _():
        drain(left_sent, ext.at[:, :, 0])

    stored = []
    for t in range(2):
        drain(back_came[3 * t], land.at[t])

        def add_step(n, carry):
            cols = lanes(n * 128, 128)
            land[t, :, :, :, cols] = (land[t, :, :, :, cols].astype(f32) + conv[t, :, :, :, cols]).astype(jnp.bfloat16)
            return carry

        lax.fori_loop(0, width // 128, add_step, 0)
        stored.append(pltpu.make_async_copy(land.at[t], ret.at[3 * t], here_in.at[4]))
        stored[t].start()
    drain(col_sent, conv.at[:, :, pl.ds(0, R - 1)])
    drain(back_came[1], ret.at[pl.ds(1, 2)])
    drain(here_in.at[4], land)


def finish_kernel(ret, *rest):
    for t in range(4):
        pltpu.make_async_copy(ret.at[t], rest[t], rest[4]).start()
    pltpu.make_async_copy(ret, ret, rest[4]).wait()


def fused_body(query, key, value, cotangent, conv_weight, row_mask, col_mask):
    rows, cols_here, width = query.shape
    R, C = lax.axis_size("rows"), lax.axis_size("cols")
    groups = cols_here // SUB
    half = width // 2
    share = half // C
    views = [x.reshape(rows, groups, SUB, width) for x in (query, key, value, cotangent)]
    bf16 = jnp.bfloat16
    any_spec = pl.BlockSpec(memory_space=pl.ANY)
    dma = pltpu.SemaphoreType.DMA
    heads = half // HEAD_DIM
    length = R * rows * SUB
    row_table, col_table = jnp.transpose(row_mask, (1, 2, 0)), jnp.transpose(col_mask, (1, 2, 0))
    ret = pl.pallas_call(
        functools.partial(layer_kernel, (R, C, rows, groups, width)),
        out_shape=jax.ShapeDtypeStruct((4, rows, groups, SUB, width), bf16),
        in_specs=[any_spec] * 7,
        out_specs=any_spec,
        scratch_shapes=[
            pltpu.VMEM((4, R, rows, SUB, half), bf16),
            pltpu.VMEM((4, R, rows, SUB, half), bf16),
            pltpu.VMEM((4, rows, C, groups, SUB, share), bf16),
            pltpu.VMEM((4, rows, C, groups, SUB, share), bf16),
            pltpu.VMEM((2, rows + 2, groups + 2, SUB, width), bf16),
            pltpu.VMEM((2, rows, groups, SUB, width), jnp.float32),
            pltpu.VMEM((2, groups, SUB, half + half - 5 * half // 8), bf16),
            pltpu.VMEM((2, rows, groups, SUB, width), bf16),
            pltpu.VMEM((heads, length, length), jnp.float32),
            pltpu.VMEM((heads, length, HEAD_DIM), jnp.float32),
            pltpu.VMEM((2, R // 2, SUB, half), jnp.float32),
            pltpu.VMEM((2, SUB, half), jnp.float32),
            dma((11,)), dma((15,)), dma((5,)), pltpu.SemaphoreType.REGULAR, pltpu.SemaphoreType.REGULAR, pltpu.SemaphoreType.REGULAR,
            pltpu.VMEM(conv_weight.shape, bf16), pltpu.SMEM(row_table.shape, jnp.int32), pltpu.SMEM(col_table.shape, jnp.int32),
        ],
        compiler_params=pltpu.CompilerParams(collective_id=0, has_side_effects=True, vmem_limit_bytes=VMEM_LIMIT),
    )(*[pltpu.with_memory_space_constraint(x, pltpu.HBM) for x in (*views, conv_weight, row_table, col_table)])
    outs = pl.pallas_call(
        finish_kernel,
        out_shape=[jax.ShapeDtypeStruct((rows, groups, SUB, width), bf16)] * 4,
        in_specs=[any_spec],
        out_specs=[any_spec] * 4,
        scratch_shapes=[dma(())],
        compiler_params=pltpu.CompilerParams(vmem_limit_bytes=1 << 20),
    )(ret)
    return tuple(x.reshape(query.shape) for x in outs)


def any_body(query, key, value, cotangent, conv_weight, row_mask, col_mask):
    rows, cols_here, width = query.shape
    R, C = lax.axis_size("rows"), lax.axis_size("cols")
    fits = R % 8 == 0 and cols_here == R * SUB and (width // 2) % (C * HEAD_DIM) == 0 and (width // 2) % (8 * HEAD_DIM) == 0
    chosen = fused_body if fits else body
    return chosen(query, key, value, cotangent, conv_weight, row_mask, col_mask)


def solution(mesh):
    return jax.shard_map(
        any_body,
        mesh=mesh,
        in_specs=(
            P("rows", "cols", None),
            P("rows", "cols", None),
            P("rows", "cols", None),
            P("rows", "cols", None),
            P(),
            P("rows", None, None),
            P("cols", None, None),
        ),
        out_specs=(
            P("rows", "cols", None),
            P("rows", "cols", None),
            P("rows", "cols", None),
            P("rows", "cols", None),
        ),
        check_vma=False,
    )
```
